32 devices in a mesh: ray: 8 (over y, x, core), cell: 4 (over z).
Axes of the slice: x: 2, y: 2, z: 4, core: 2. Of those that a mesh axis runs over, the one named last changes fastest.
Arguments:
- ray_tiles: float32 [3072, 64, 128], P(('ray', 'cell')), may hold values from -0.15625 to 0.15625
- tile_group: int32 [32, 96], P(('ray', 'cell')), may hold values from 0 to 7
- tile_slot: int32 [32, 96], P(('ray', 'cell')), may hold values from 0 to 15, as said below
- slot_block: int32 [32, 16], P(('ray', 'cell')), may hold values from -1 to 31, as said below
- u_basis: float32 [8, 16384], P(None, ('ray', 'cell'))
- v_prev: float32 [8, 16384], P(None, 'cell')
- b_prev: float32 [8, 8], replicated, may hold values from -4 to 4
Outputs:
- v_next: float32 [8, 16384], P(None, 'cell')
- u_next: float32 [8, 16384], P(None, ('ray', 'cell'))
- alpha_factor: float32 [8, 8], replicated
- beta_factor: float32 [8, 8], replicated
The draws below stay inside these ranges and needn't reach their ends.
Inputs may be any that keep to these rules, and one draw needn't show every extreme that they name: Slot p * 4 + s of device d carries a block of cell slab p; slot_block gives that block's index within the slab, distinct over s for one d and p, or -1 where the slot is unused; for each device and slab p, the used slots are p * 4 to p * 4 + n - 1 for some n from 1 to 4; there is one slab, the same for every device, whose 4 slots are all used on every device. `tile_slot`: each tile names a used slot of its device, and every used slot is named by some tile.
All inputs are finite; a program needn't handle non-finite values.
Results may differ from the reference program's by a relative error of at most 0.0003.
Values sent between devices are 32-bit elements; how exact they have to be, the bound alone decides.
A program may use at most 64 MiB of HBM per device.

```python
import jax
import jax.numpy as jnp
from jax import lax

COMP = 8
CAP = 4
BLK_DEV = 32
TILES = 96
GROUPS = 8
GROUP_RAYS = 64
NBLK = 128
CELLS = 16384
SLOTS = 16
RAYS = 16384
N_CELL = 4
DEVICES = 32


def draw_routing(key):
    keys = jax.random.split(jax.random.fold_in(key, 7), 4)
    hottest = jax.random.randint(keys[0], (), 0, N_CELL)
    counts = jax.random.randint(keys[1], (DEVICES, N_CELL), 1, CAP + 1)
    counts = jnp.where(jnp.arange(N_CELL)[None, :] == hottest, CAP, counts)
    perm_keys = jax.random.split(keys[2], DEVICES * N_CELL)
    chosen = jax.vmap(lambda k: jax.random.permutation(k, BLK_DEV)[:CAP])(perm_keys)
    chosen = chosen.reshape(DEVICES, N_CELL, CAP)
    active = jnp.arange(CAP)[None, None, :] < counts[:, :, None]
    slot_block = jnp.where(active, chosen, -1).reshape(DEVICES, SLOTS)
    active_flat = active.reshape(DEVICES, SLOTS)
    order = jnp.argsort(jnp.where(active_flat, 0, 1), axis=1, stable=True)
    live = jnp.sum(active_flat.astype(jnp.int32), axis=1, keepdims=True)
    spread = jax.random.randint(keys[3], (DEVICES, TILES), 0, 1 << 20)
    positions = jnp.arange(TILES)[None, :]
    picked = jnp.where(positions < live, positions, spread % live)
    tile_slot = jnp.take_along_axis(order, picked, axis=1)
    return (tile_slot.astype(jnp.int32), slot_block.astype(jnp.int32))


def draw_tile_slot(key, part):
    return draw_routing(key)[0]


def draw_slot_block(key, part):
    return draw_routing(key)[1]


def draw_u_basis(key, part):
    column = jnp.arange(RAYS) // (GROUPS * GROUP_RAYS)
    rising = 0.3 * 3.0 ** (column.astype(jnp.float32) / max(DEVICES - 1, 1))
    base = jax.random.normal(key, (COMP, RAYS), jnp.float32)
    return base * rising[None, :]


def draw_v_prev(key, part):
    column = jnp.arange(CELLS) // (BLK_DEV * 128)
    rising = 3.0 ** (column.astype(jnp.float32) / max(NBLK // BLK_DEV - 1, 1))
    base = jax.random.normal(key, (COMP, CELLS), jnp.float32)
    return base * rising[None, :]


def plant(array, key, low, top_value):
    index_at = [jax.random.randint(jax.random.fold_in(key, axis), (), 0, length) for axis, length in enumerate(array.shape)]
    main_axis = array.shape.index(max(array.shape))
    next_to = index_at[:main_axis] + [(index_at[main_axis] + 1) % array.shape[main_axis]] + index_at[main_axis + 1:]
    return array.at[tuple(index_at)].set(low).at[tuple(next_to)].set(top_value)


def steps_of(own_key, dims, cuts, low, largest):
    def one(axis_at, parts):
        draws = jax.random.uniform(jax.random.fold_in(jax.random.fold_in(own_key, 6), axis_at), (parts,), jnp.float32, low / len(cuts), largest / len(cuts))
        return jnp.repeat(jnp.exp(draws), dims[axis_at] // parts).reshape((-1,) + (1,) * (len(dims) - axis_at - 1))

    level = one(*cuts[0])
    for cut in cuts[1:]:
        level = level * one(*cut)
    return level


def bell_draw(stream_key, shape, scale, reach, cuts=(), kind=jnp.bfloat16):
    values = scale * jax.random.normal(stream_key, shape, jnp.float32)
    if cuts:
        values = values * steps_of(stream_key, shape, cuts, -0.22, 0.18)
    return jnp.clip(values, -reach, reach).astype(kind)


def setup_inputs(seed: int = 0) -> dict:
    key_list = jax.random.split(jax.random.key(seed), 8)
    return {
        "ray_tiles": bell_draw(key_list[0], (DEVICES * TILES, GROUP_RAYS, 128), (TILES * 128 // GROUPS) ** -0.5, 0.15625, ((0, 32),), jnp.float32),
        "tile_group": plant(jax.random.randint(key_list[1], (DEVICES, TILES), 0, GROUPS), jax.random.fold_in(key_list[1], 1), 0, GROUPS - 1).astype(jnp.int32),
        "tile_slot": draw_tile_slot(jax.random.fold_in(key_list[7], 71), 0),
        "slot_block": draw_slot_block(jax.random.fold_in(key_list[7], 71), 0),
        "u_basis": draw_u_basis(jax.random.fold_in(key_list[7], 71), 0),
        "v_prev": draw_v_prev(jax.random.fold_in(key_list[7], 71), 0),
        "b_prev": bell_draw(key_list[6], (COMP, COMP), 0.3, 4.0, (), jnp.float32),
    }


def triangular_left(factor, rhs):
    return lax.linalg.triangular_solve(factor, rhs, left_side=True, lower=True)

def reference(ray_tiles, tile_group, tile_slot, slot_block, u_basis, v_prev, b_prev):
    highest = lax.Precision.HIGHEST
    local_block = jnp.take_along_axis(slot_block, tile_slot, axis=1)
    global_block = (tile_slot // CAP * BLK_DEV + local_block).astype(jnp.int32)
    tiles_dev = ray_tiles.reshape(DEVICES, TILES, GROUP_RAYS, 128)
    u_dev = u_basis.reshape(COMP, DEVICES, GROUPS, GROUP_RAYS).transpose(1, 0, 2, 3)

    def forward(accum, item):
        tiles_one, groups_one, blocks_one, u_one = item
        u_tiles = jnp.take(u_one, groups_one, axis=1)
        contrib = jnp.einsum('ktr,trc->tkc', u_tiles, tiles_one, precision=highest)
        return (accum + jax.ops.segment_sum(contrib, blocks_one, num_segments=NBLK), None)
    summed, unused = lax.scan(forward, jnp.zeros((NBLK, COMP, 128), jnp.float32), (tiles_dev, tile_group, global_block, u_dev))
    x_cells = summed.transpose(1, 0, 2).reshape(COMP, CELLS)
    w_cells = x_cells - jnp.dot(b_prev, v_prev, precision=highest)
    alpha_factor = jnp.linalg.cholesky(jnp.dot(w_cells, w_cells.T, precision=highest) / CELLS)
    v_next = triangular_left(alpha_factor, w_cells)
    v_blocks = v_next.reshape(COMP, NBLK, 128).transpose(1, 0, 2)

    def backward(carry, item):
        tiles_one, groups_one, blocks_one = item
        basis_tiles = jnp.take(v_blocks, blocks_one, axis=0)
        ray_terms = jnp.einsum('tkc,trc->tkr', basis_tiles, tiles_one, precision=highest)
        membership = (groups_one[:, None] == jnp.arange(GROUPS, dtype=jnp.int32)[None, :]).astype(jnp.float32)
        image = jnp.einsum('tg,tkr->kgr', membership, ray_terms, precision=highest)
        return (carry, image)
    unused_carry, images = lax.scan(backward, jnp.zeros((), jnp.float32), (tiles_dev, tile_group, global_block))
    ray_image = images.transpose(1, 0, 2, 3).reshape(COMP, RAYS)
    ray_residual = ray_image - jnp.dot(alpha_factor.T, u_basis, precision=highest)
    beta_factor = jnp.linalg.cholesky(jnp.dot(ray_residual, ray_residual.T, precision=highest) / RAYS)
    u_next = triangular_left(beta_factor, ray_residual)
    return (v_next, u_next, alpha_factor, beta_factor)
```

```python
import functools

import jax
import jax.numpy as jnp
from jax import lax
from jax.experimental import pallas as pl
from jax.experimental.pallas import tpu as pltpu
from jax.sharding import PartitionSpec as P

CAP = 4
GROUPS = 8
CHUNKS = 8
UNROLL = 8
DIRECT = 32
BATCH = 4
MESH = pl.DeviceIdType.MESH
F32 = jnp.float32
BF16 = jnp.bfloat16


def split_rows(value):
    high = value.astype(BF16).astype(F32)
    return jnp.concatenate([high, value - high], axis=0).astype(BF16)


def local_kernel(group_ref, slot_ref, block_ref, tiles_hbm, u_ref, packet_ref, high_hbm, low_hbm, tiles, dense, high_ref, low_ref, sems, out_sems):
    tile_count, tile_rays, width = tiles.shape
    slots = block_ref.shape[1]
    per_chunk = tile_count // CHUNKS

    def chunk(i):
        rows = pl.ds(i * per_chunk, per_chunk)
        return pltpu.make_async_copy(tiles_hbm.at[rows], tiles.at[rows], sems.at[i])

    for i in range(CHUNKS):
        chunk(i).start()

    row = lax.broadcasted_iota(jnp.int32, (8, width), 0)
    for p in range(slots // CAP):
        index = jnp.full((8, width), -1, jnp.int32)
        for s in range(CAP):
            index = jnp.where(row == s, block_ref[0, p * CAP + s], index)
        packet_ref[p, CAP] = index.astype(F32)

    @pl.loop(0, slots)
    def _(s):
        dense[:, pl.ds(pl.multiple_of(s * width, width), width)] = jnp.zeros((dense.shape[0], width), F32)

    for i in range(CHUNKS):
        chunk(i).wait()

        @pl.loop(0, per_chunk // BATCH)
        def _(at):
            first = i * per_chunk + at * BATCH
            where = [(group_ref[0, first + n], slot_ref[0, first + n]) for n in range(BATCH)]
            values = [tiles[first + n] for n in range(BATCH)]
            for (group, slot), value in zip(where, values):
                rows = pl.ds(pl.multiple_of(group * tile_rays, tile_rays), tile_rays)
                columns = pl.ds(pl.multiple_of(slot * width, width), width)
                dense[rows, columns] += value

    u_pair = split_rows(u_ref[...])
    comps = u_ref.shape[0]
    span = 2 * width

    def stores(n):
        return [
            pltpu.make_async_copy(source.at[n], target.at[n], out_sems.at[at, n])
            for at, (source, target) in enumerate(((high_ref, high_hbm), (low_ref, low_hbm)))
        ]

    def product(n):
        columns = pl.ds(pl.multiple_of(n * span, span), span)
        block = dense[:, columns]
        high = block.astype(BF16)
        low = (block - high.astype(F32)).astype(BF16)
        high_ref[n] = high
        low_ref[n] = low
        for store in stores(n):
            store.start()
        both = jnp.dot(u_pair, high, preferred_element_type=F32)
        rest = jnp.dot(u_pair, low, preferred_element_type=F32)
        total = both[:comps] + (both[comps:] + rest[:comps])
        for half in range(2):
            s = 2 * n + half
            packet_ref[s // CAP, s % CAP] = total[:, half * width : (half + 1) * width]

    def finish(n):
        for store in stores(n):
            store.wait()

    each_peer(slots // 2, product, 0)
    each_peer(slots // 2, finish, 0)


def each_peer(n, body, first=1):
    if n <= UNROLL:
        for k in range(first, n):
            body(k)
    else:
        pl.loop(first, n)(body)


def row_of(tile, k):
    return jnp.broadcast_to(tile[k : k + 1, :], tile.shape)


def column_of(tile, k):
    return jnp.broadcast_to(tile[:, k : k + 1], (tile.shape[0], 128))


def gram(blocks):
    lane = lax.broadcasted_iota(jnp.int32, (8, 128), 1)
    tile = jnp.zeros((8, 128), F32)
    for j in range(8):
        products = blocks[0] * row_of(blocks[0], j)
        for block in blocks[1:]:
            products = products + block * row_of(block, j)
        tile = jnp.where(lane == j, jnp.sum(products, axis=1, keepdims=True), tile)
    return tile


def factor(tile):
    row = lax.broadcasted_iota(jnp.int32, (8, 128), 0)
    lane = lax.broadcasted_iota(jnp.int32, (8, 128), 1)
    lower = jnp.zeros((8, 128), F32)
    upper = jnp.zeros((8, 128), F32)
    inverse = jnp.where(row == lane, 1.0, 0.0).astype(F32)
    for j in range(8):
        across = row_of(tile, j)
        down = column_of(tile, j)
        scale = 1.0 / jnp.sqrt(row_of(down, j))
        across = across * scale
        down = jnp.where(row >= j, down * scale, 0.0)
        lower = jnp.where(lane == j, down, lower)
        upper = jnp.where((row == j) & (lane >= j), across, upper)
        tile = tile - down * across
        pivot = row_of(inverse, j) * scale
        inverse = jnp.where(row == j, pivot, inverse - jnp.where(row > j, down, 0.0) * pivot)
    return lower, upper, inverse


def columns_of(tile):
    return [column_of(tile, k) for k in range(8)]


def apply(columns, block):
    total = columns[0] * row_of(block, 0)
    for k in range(1, 8):
        total = total + columns[k] * row_of(block, k)
    return total


def step_kernel(
    n_ray, n_cell, cells_all, rays_all,
    packet_hbm, high_hbm, low_hbm, u_hbm, v_prev_hbm, b_hbm,
    v_hbm, small_ref,
    packet_ref, u_ref, v_prev_ref, b_ref, v_ref, slots_in, part, pieces_in, slab_in, back_out, back_in, ray_gram, cell_gram, all_gram, high, low, w_slots,
    load_sem, send1, recv1, send2, recv2, send3, recv3, send4, recv4, send5, recv5, send6, recv6, send7, recv7,
):
    ray = lax.axis_index("ray")
    cell = lax.axis_index("cell")
    piece = pieces_in.shape[1]
    blocks = n_ray * piece

    early = [
        pltpu.make_async_copy(source, target, load_sem.at[2 + i])
        for i, (source, target) in enumerate(
            ((packet_hbm, packet_ref), (u_hbm, u_ref), (v_prev_hbm, v_prev_ref), (b_hbm, b_ref))
        )
    ]
    for load in early:
        load.start()
    loads = [
        pltpu.make_async_copy(high_hbm, high, load_sem.at[0]),
        pltpu.make_async_copy(low_hbm, low, load_sem.at[1]),
    ]
    for load in loads:
        load.start()

    barrier = pltpu.get_barrier_semaphore()

    each_peer(n_ray, lambda k: pl.semaphore_signal(barrier, inc=1, device_id={"ray": lax.rem(ray + k, n_ray)}, device_id_type=MESH))

    each_peer(n_cell, lambda k: pl.semaphore_signal(barrier, inc=1, device_id={"cell": lax.rem(cell + k, n_cell)}, device_id_type=MESH))

    pl.semaphore_wait(barrier, n_ray + n_cell - 2)

    def over(axis, me, n, source, target, send, recv):
        def copy(k):
            peer = lax.rem(me + k, n)
            return pltpu.make_async_remote_copy(
                src_ref=source(peer),
                dst_ref=target(me),
                send_sem=send.at[k - 1],
                recv_sem=recv.at[k - 1],
                device_id={axis: peer},
                device_id_type=MESH,
            )

        def wait_recv(k):
            origin = lax.rem(me + n - k, n)
            pltpu.make_async_remote_copy(
                src_ref=source(lax.rem(me + k, n)),
                dst_ref=target(origin),
                send_sem=send.at[k - 1],
                recv_sem=recv.at[k - 1],
                device_id={axis: lax.rem(me + k, n)},
                device_id_type=MESH,
            ).wait_recv()

        def receive():
            each_peer(n, wait_recv)

        def finish():
            each_peer(n, lambda k: copy(k).wait_send())

        return copy, receive, finish

    to_slab, from_slots, end1 = over(
        "cell", cell, n_cell, lambda peer: packet_ref.at[peer], lambda me: slots_in.at[me], send1, recv1
    )
    early[0].wait()
    each_peer(n_cell, lambda k: to_slab(k).start())
    for load in early[1:]:
        load.wait()
    slots_in[cell] = packet_ref[cell]
    from_slots()

    def index_tiles(p):
        tile = slots_in[p, CAP]
        return [row_of(tile, s) for s in range(CAP)]

    indices = [index_tiles(p) for p in range(n_cell)]

    def dense_block(b):
        number = jnp.full((8, 128), b, jnp.int32).astype(F32)
        total = jnp.zeros((8, 128), F32)
        for p in range(n_cell):
            for s in range(CAP):
                total = total + jnp.where(indices[p][s] == number, slots_in[p, s], 0.0)
        return total

    to_piece, from_pieces, end2 = over(
        "ray", ray, n_ray, lambda peer: part.at[peer], lambda me: pieces_in.at[me], send2, recv2
    )

    def send_piece(k):
        peer = lax.rem(ray + k, n_ray)
        for i in range(piece):
            part[peer, i] = dense_block(peer * piece + i)
        to_piece(k).start()

    each_peer(n_ray, send_piece)

    for i in range(piece):
        pieces_in[ray, i] = dense_block(ray * piece + i)

    b_columns = columns_of(b_ref[...])
    known = []
    for i in range(piece):
        at = pl.multiple_of((ray * piece + i) * 128, 128)
        known.append(apply(b_columns, v_prev_ref[:, pl.ds(at, 128)]))
    from_pieces()
    own = []
    for i in range(piece):
        total = pieces_in[0, i]
        for r in range(1, n_ray):
            total = total + pieces_in[r, i]
        own.append(total - known[i])
        slab_in[ray, i] = own[i]
    slab_in[ray, piece] = gram(own)

    to_ray, from_ray, end3 = over(
        "ray", ray, n_ray, lambda peer: slab_in.at[ray], lambda me: slab_in.at[me], send3, recv3
    )
    each_peer(n_ray, lambda k: to_ray(k).start())
    from_ray()

    slab_gram = slab_in[0, piece]
    for r in range(1, n_ray):
        slab_gram = slab_gram + slab_in[r, piece]

    def answer(p):
        wanted = index_tiles(p)
        found = [jnp.zeros((8, 128), F32) for s in range(CAP)]
        for b in range(blocks):
            block = slab_in[b // piece, b % piece]
            for s in range(CAP):
                found[s] = jnp.where(wanted[s] == float(b), block, found[s])
        return found

    to_cell, from_cell, end4 = over(
        "cell", cell, n_cell, lambda peer: back_out.at[peer], lambda me: back_in.at[me], send4, recv4
    )

    def send_answer(k):
        peer = lax.rem(cell + k, n_cell)
        found = answer(peer)
        for s in range(CAP):
            back_out[peer, s] = found[s]
        back_out[peer, CAP] = slab_gram
        to_cell(k).start()

    each_peer(n_cell, send_answer)

    found = answer(cell)
    for s in range(CAP):
        back_in[cell, s] = found[s]
    back_in[cell, CAP] = slab_gram
    for load in loads:
        load.wait()
    from_cell()

    whole_gram = back_in[0, CAP]
    for p in range(1, n_cell):
        whole_gram = whole_gram + back_in[p, CAP]
    for p in range(n_cell):
        for s in range(CAP):
            at = p * CAP + s
            w_slots[at // 2, :, (at % 2) * 128 : (at % 2 + 1) * 128] = back_in[p, s]
    across = (((1,), (1,)), ((), ()))

    def image_of(n):
        w_pair = split_rows(w_slots[n])
        both = lax.dot_general(w_pair, high[n], across, preferred_element_type=F32)
        rest = lax.dot_general(w_pair, low[n], across, preferred_element_type=F32)
        return both[:8] + (both[8:] + rest[:8])

    steps = high.shape[0]
    if steps <= UNROLL:
        image = image_of(0)
        for n in range(1, steps):
            image = image + image_of(n)
    else:
        image = lax.fori_loop(1, steps, lambda n, total: total + image_of(n), image_of(0))

    alpha, alpha_t, alpha_inverse = factor(whole_gram * (1.0 / cells_all))
    inverse_columns = columns_of(alpha_inverse)
    alpha_t_columns = columns_of(alpha_t)
    ray_blocks = u_ref.shape[1] // 128
    residual = []
    for i in range(ray_blocks):
        lanes = slice(i * 128, (i + 1) * 128)
        residual.append(apply(inverse_columns, image[:, lanes]) - apply(alpha_t_columns, u_ref[:, lanes]))
    everyone = n_ray * n_cell
    flat = ray * n_cell + cell
    own_gram = gram(residual)

    def gram_copy(k, back):
        peer = lax.rem(flat + k, everyone)
        slot = lax.rem(flat + everyone - k, everyone) if back else flat
        return pltpu.make_async_remote_copy(
            src_ref=all_gram.at[flat],
            dst_ref=all_gram.at[slot],
            send_sem=send7.at[k - 1],
            recv_sem=recv7.at[k - 1],
            device_id={"ray": lax.div(peer, n_cell), "cell": lax.rem(peer, n_cell)},
            device_id_type=MESH,
        )

    if everyone <= DIRECT:
        all_gram[flat] = own_gram
        for k in range(1, everyone):
            gram_copy(k, False).start()
    else:
        ray_gram[ray] = own_gram
        to_gram, from_gram, end5 = over(
            "ray", ray, n_ray, lambda peer: ray_gram.at[ray], lambda me: ray_gram.at[me], send5, recv5
        )
        each_peer(n_ray, lambda k: to_gram(k).start())

    small_ref[0] = alpha
    for i in range(ray_blocks):
        small_ref[2 + i] = residual[i]
    for b in range(blocks):
        v_ref[:, b * 128 : (b + 1) * 128] = apply(inverse_columns, slab_in[b // piece, b % piece])
    store = pltpu.make_async_copy(v_ref, v_hbm, load_sem.at[6])
    store.start()

    if everyone <= DIRECT:
        for k in range(1, everyone):
            gram_copy(k, True).wait_recv()
        total = all_gram[0]
        for d in range(1, everyone):
            total = total + all_gram[d]
    else:
        from_gram()
        total = ray_gram[0]
        for r in range(1, n_ray):
            total = total + ray_gram[r]
        cell_gram[cell] = total
        to_total, from_total, end6 = over(
            "cell", cell, n_cell, lambda peer: cell_gram.at[cell], lambda me: cell_gram.at[me], send6, recv6
        )
        each_peer(n_cell, lambda k: to_total(k).start())
        from_total()
        total = cell_gram[0]
        for p in range(1, n_cell):
            total = total + cell_gram[p]
    small_ref[1] = total * (1.0 / rays_all)
    store.wait()
    for end in (end1, end2, end3, end4):
        end()
    if everyone <= DIRECT:
        for k in range(1, everyone):
            gram_copy(k, False).wait_send()
    else:
        end5()
        end6()


def last_kernel(v_in, small, v_out, u_out, alpha_out, beta_out):
    v_out[...] = v_in[...]
    alpha_out[...] = small[0][:, :8]
    beta, _, beta_inverse = factor(small[1])
    beta_out[...] = beta[:, :8]
    beta_columns = columns_of(beta_inverse)
    for i in range(small.shape[0] - 2):
        u_out[:, i * 128 : (i + 1) * 128] = apply(beta_columns, small[2 + i])


def flips_of(index, count):
    flips, bit = {}, 1
    while bit < count:
        flips[bit] = bit * (1 - 2 * lax.rem(lax.div(index, bit), 2))
        bit *= 2
    return flips


def flipped(index, flips, mask):
    for bit, step in flips.items():
        if mask & bit:
            index = index + step
    return index


def far_first(n_ray, n_cell):
    masks = [(2 * a, c) for a in range(n_ray // 2) for c in range(n_cell) if a or c]
    return sorted(masks, key=lambda m: -(2 * bin(m[0]).count("1") + m[1]))


def halves_of(value):
    high = value.astype(BF16)
    return high, (value - high.astype(F32)).astype(BF16)


def fused_kernel(
    n_ray, n_cell, cells_all, rays_all,
    group_hbm, slot_hbm, block_hbm, tiles_hbm, u_hbm, v_prev_hbm, b_hbm,
    v_hbm, small_ref,
    group_ref, slot_ref, block_ref, wanted_ref, wanted_in, tiles, u_ref, v_prev_ref, b_ref,
    u_twice, spread, split, turned, sums, packet, recv, part, part_in, known, w_ref,
    back_out, back_in, gram_out, gram_in, w_slots, pair_gram, all_gram, v_ref,
    tile_sem, load_sem, send1, recv1, send2, recv2, send3, recv3, send4, recv4, send5, recv5, send6, recv6, send7, recv7,
):
    ray = lax.axis_index("ray")
    cell = lax.axis_index("cell")
    tile_count, tile_rays, width = tiles.shape
    slots = block_ref.shape[1]
    comps = u_ref.shape[0]
    sources = n_ray // 2 * n_cell
    blocks = w_ref.shape[0]
    steps, span = split.shape[0], split.shape[1]
    chunks = tile_sem.shape[0]
    per_chunk = tile_count // chunks
    per_step = steps // chunks
    quad = span // tile_rays

    small_loads = [
        pltpu.make_async_copy(source, target, load_sem.at[i])
        for i, (source, target) in enumerate(
            (
                (u_hbm, u_ref), (slot_hbm, slot_ref), (group_hbm, group_ref), (block_hbm, block_ref),
                (v_prev_hbm, v_prev_ref), (b_hbm, b_ref),
            )
        )
    ]

    def chunk(i):
        rows = pl.ds(i * per_chunk, per_chunk)
        return pltpu.make_async_copy(tiles_hbm.at[rows], tiles.at[rows], tile_sem.at[i])

    for load in small_loads[:4]:
        load.start()
    for i in range(chunks):
        chunk(i).start()
    for load in small_loads[4:]:
        load.start()

    ray_flips = flips_of(ray, n_ray)
    cell_flips = flips_of(cell, n_cell)
    masks = far_first(n_ray, n_cell)
    peers = [(flipped(ray, ray_flips, a), flipped(cell, cell_flips, c)) for a, c in masks]
    twin = ray + ray_flips[1]
    cell_masks = list(range(n_cell - 1, 0, -1))
    cell_peers = [flipped(cell, cell_flips, c) for c in cell_masks]

    def number_of(ray_at, cell_at):
        return lax.div(ray_at, 2) * n_cell + cell_at

    me = number_of(ray, cell)

    barrier = pltpu.get_barrier_semaphore()
    for r, c in peers:
        pl.semaphore_signal(barrier, inc=1, device_id={"ray": r, "cell": c}, device_id_type=MESH)
    pl.semaphore_signal(barrier, inc=1, device_id={"ray": twin, "cell": cell}, device_id_type=MESH)

    def remote(source, target, send, recv_at, r, c):
        return pltpu.make_async_remote_copy(
            src_ref=source, dst_ref=target, send_sem=send, recv_sem=recv_at,
            device_id={"ray": r, "cell": c}, device_id_type=MESH,
        )

    for load in small_loads[:4]:
        load.wait()

    low = lax.broadcasted_iota(jnp.int32, (8, width), 1) < tile_rays
    low_pair = lax.broadcasted_iota(jnp.int32, (2 * comps, width), 1) < tile_rays
    lane = lax.broadcasted_iota(jnp.int32, (8, width), 1)
    for q in range(u_ref.shape[1] // width):
        block = u_ref[:, q * width : (q + 1) * width]
        turn = pltpu.roll(block, tile_rays, 1)
        for half, both in enumerate((jnp.where(low, block, turn), jnp.where(low, turn, block))):
            high = both.astype(BF16).astype(F32)
            u_twice[2 * q + half, :comps] = high
            u_twice[2 * q + half, comps:] = both - high

    @pl.loop(0, chunks)
    def _(c):
        for q in range(per_chunk // 2):
            at = c * per_chunk + 2 * q
            value = jnp.where(low_pair, u_twice[group_ref[0, at]], u_twice[group_ref[0, at + 1]])
            where = jnp.where(low_pair, slot_ref[0, at], slot_ref[0, at + 1])
            for s in range(slots):
                spread[c, s * 2 * comps : (s + 1) * 2 * comps, q * width : (q + 1) * width] = jnp.where(
                    where == s, value, 0.0
                ).astype(BF16)

    for p in range(n_cell):
        index = jnp.zeros((8, width), jnp.int32)
        for s in range(CAP):
            index = jnp.where(lane == me * (CAP + 1) + s, block_ref[0, p * CAP + s] + 1, index)
        packet[p, CAP * comps :] = index.astype(F32)

    for i in range(chunks):
        chunk(i).wait()
        value = tiles[i * per_chunk : (i + 1) * per_chunk].reshape(per_chunk * tile_rays, width)
        high, rest = halves_of(value)
        both = jnp.concatenate([high, rest], axis=1)
        split[i * per_step : (i + 1) * per_step] = both.reshape(per_step, span, 2 * width)
        product = jnp.dot(spread[i], both, preferred_element_type=F32)
        if i == 0:
            sums[...] = product
        else:
            sums[...] += product

    for s in range(slots):
        rows = sums[s * 2 * comps : (s + 1) * 2 * comps]
        rows = rows[:, :width] + rows[:, width:]
        packet[s // CAP, s % CAP * comps : (s % CAP + 1) * comps] = rows[:comps] + rows[comps:]
    recv[me] = packet[cell]

    pl.semaphore_wait(barrier, len(peers) + 1)
    first = [
        remote(packet.at[c], recv.at[me], send1.at[i], recv1.at[i], r, c) for i, (r, c) in enumerate(peers)
    ]
    for copy in first:
        copy.start()
    asks = [
        remote(block_hbm, wanted_in.at[cell], send2.at[i], recv2.at[i], ray, c) for i, c in enumerate(cell_peers)
    ]
    for copy in asks:
        copy.start()

    for load in small_loads[4:]:
        load.wait()
    b_columns = columns_of(b_ref[...])
    for b in range(blocks):
        known[b] = apply(b_columns, v_prev_ref[:, b * width : (b + 1) * width])

    @pl.loop(0, steps)
    def _(n):
        turned[n] = split[n].T

    for i, c in enumerate(cell_peers):
        remote(block_hbm, wanted_in.at[c], send2.at[i], recv2.at[i], ray, c).wait_recv()
    ask_loads = [
        pltpu.make_async_copy(wanted_in.at[c], wanted_ref.at[c], load_sem.at[6 + i]) for i, c in enumerate(cell_peers)
    ]
    for load in ask_loads:
        load.start()
    for load in ask_loads:
        load.wait()

    for i, (r, c) in enumerate(peers):
        remote(packet.at[c], recv.at[number_of(r, c)], send1.at[i], recv1.at[i], r, c).wait_recv()

    height = (CAP + 1) * comps
    flat = recv.reshape(sources * height, width)
    asked = jnp.sum(flat[pl.ds(CAP * comps, sources, stride=height), :], axis=0, keepdims=True) - 1.0
    row = lax.broadcasted_iota(jnp.int32, (blocks, width), 0).astype(F32)
    pick = jnp.where(row == jnp.broadcast_to(asked, (blocks, width)), 1.0, 0.0)[:, : sources * (CAP + 1)].astype(BF16)
    part_rows = part.reshape(blocks * comps, width)
    for r in range(comps):
        high, rest = halves_of(flat[pl.ds(r, sources * (CAP + 1), stride=comps), :])
        both = jnp.dot(pick, jnp.concatenate([high, rest], axis=1), preferred_element_type=F32)
        part_rows[pl.ds(r, blocks, stride=comps), :] = both[:, :width] + both[:, width:]

    swap = remote(part, part_in, send3.at[0], recv3.at[0], twin, cell)
    swap.start()
    swap.wait_recv()
    for b in range(blocks):
        w_ref[b] = part[b] + part_in[b] - known[b]

    def answer(ref, at):
        return [w_ref[jnp.maximum(ref(cell * CAP + s), 0)] for s in range(CAP)]

    answers = [
        remote(back_out.at[i], back_in.at[cell], send4.at[i], recv4.at[i], ray, c) for i, c in enumerate(cell_peers)
    ]
    for i, c in enumerate(cell_peers):
        for s in range(CAP):
            back_out[i, s] = w_ref[jnp.maximum(wanted_ref[c, 0, cell * CAP + s], 0)]
        answers[i].start()
    for s in range(CAP):
        back_in[cell, s] = w_ref[jnp.maximum(block_ref[0, cell * CAP + s], 0)]

    slab_gram = gram([w_ref[b] for b in range(blocks)])
    gram_out[...] = slab_gram
    gram_in[cell] = slab_gram
    grams = [
        remote(gram_out, gram_in.at[cell], send5.at[i], recv5.at[i], ray, c) for i, c in enumerate(cell_peers)
    ]
    for copy in grams:
        copy.start()

    for i, c in enumerate(cell_peers):
        remote(back_out.at[i], back_in.at[c], send4.at[i], recv4.at[i], ray, c).wait_recv()
    for p in range(n_cell):
        for s in range(CAP):
            w_slots[p * CAP + s] = split_rows(back_in[p, s])

    groups = u_ref.shape[1] // tile_rays
    totals = [jnp.zeros((8, width), F32) for g in range(groups)]
    for n in range(steps):
        at = n * quad
        rows = jnp.concatenate([w_slots[slot_ref[0, at + j]] for j in range(quad)], axis=0)
        found = jnp.dot(jnp.concatenate([rows, rows], axis=1), turned[n], preferred_element_type=F32)
        for j in range(quad // 2):
            lanes = slice(j * width, (j + 1) * width)
            top = 2 * j * 2 * comps
            pair = jnp.where(
                low_pair, found[top : top + 2 * comps, lanes], found[top + 2 * comps : top + 4 * comps, lanes]
            )
            pair = pair[:comps] + pair[comps:]
            owner = jnp.where(low, group_ref[0, at + 2 * j], group_ref[0, at + 2 * j + 1])
            for g in range(groups):
                totals[g] = totals[g] + jnp.where(owner == g, pair, 0.0)

    for i, c in enumerate(cell_peers):
        remote(gram_out, gram_in.at[c], send5.at[i], recv5.at[i], ray, c).wait_recv()
    whole_gram = gram_in[0]
    for p in range(1, n_cell):
        whole_gram = whole_gram + gram_in[p]
    alpha, alpha_t, alpha_inverse = factor(whole_gram * (1.0 / cells_all))
    inverse_columns = columns_of(alpha_inverse)
    alpha_t_columns = columns_of(alpha_t)
    totals = [total + pltpu.roll(total, tile_rays, 1) for total in totals]
    ray_blocks = u_ref.shape[1] // width
    residual = []
    for i in range(ray_blocks):
        image = jnp.where(low, totals[2 * i], totals[2 * i + 1])
        lanes = slice(i * width, (i + 1) * width)
        residual.append(apply(inverse_columns, image) - apply(alpha_t_columns, u_ref[:, lanes]))
    pair_gram[0] = gram(residual)
    twins = remote(pair_gram.at[0], pair_gram.at[1], send6.at[0], recv6.at[0], twin, cell)
    twins.start()
    small_ref[0] = alpha
    for i in range(ray_blocks):
        small_ref[2 + i] = residual[i]
    twins.wait_recv()
    all_gram[me] = pair_gram[0] + pair_gram[1]
    last = [
        remote(all_gram.at[me], all_gram.at[me], send7.at[i], recv7.at[i], r, c) for i, (r, c) in enumerate(peers)
    ]
    for copy in last:
        copy.start()
    for b in range(blocks):
        v_ref[:, b * width : (b + 1) * width] = apply(inverse_columns, w_ref[b])
    store = pltpu.make_async_copy(v_ref, v_hbm, load_sem.at[6])
    store.start()
    for i, (r, c) in enumerate(peers):
        remote(all_gram.at[me], all_gram.at[number_of(r, c)], send7.at[i], recv7.at[i], r, c).wait_recv()
    total = all_gram[0]
    for d in range(1, sources):
        total = total + all_gram[d]
    small_ref[1] = total * (1.0 / rays_all)
    store.wait()
    for copy in first + asks + [swap] + answers + grams + [twins] + last:
        copy.wait_send()


def fused(n_ray, n_cell, ray_tiles, tile_group, tile_slot, slot_block, u_basis, v_prev, b_prev):
    tile_count, tile_rays, width = ray_tiles.shape
    comps, rays = u_basis.shape
    slots = slot_block.shape[1]
    blocks = v_prev.shape[1] // width
    sources = n_ray // 2 * n_cell
    steps = tile_count * tile_rays // (2 * width)
    vmem = pl.BlockSpec(memory_space=pltpu.VMEM)
    anywhere = pl.BlockSpec(memory_space=pl.ANY)
    tile = (comps, width)
    pair = slots * 2 * comps
    one = pltpu.SemaphoreType.DMA((1,))
    far = pltpu.SemaphoreType.DMA((sources - 1,))
    cells = pltpu.SemaphoreType.DMA((n_cell - 1,))
    return pl.pallas_call(
        functools.partial(fused_kernel, n_ray, n_cell, v_prev.shape[1] * n_cell, rays * n_ray * n_cell),
        out_shape=(
            jax.ShapeDtypeStruct(v_prev.shape, F32),
            jax.ShapeDtypeStruct((2 + rays // width,) + tile, F32),
        ),
        in_specs=[anywhere] * 7,
        out_specs=(anywhere, vmem),
        scratch_shapes=[
            pltpu.SMEM(tile_group.shape, jnp.int32),
            pltpu.SMEM(tile_slot.shape, jnp.int32),
            pltpu.SMEM(slot_block.shape, jnp.int32),
            pltpu.SMEM((n_cell,) + slot_block.shape, jnp.int32),
            pltpu.VMEM((n_cell,) + slot_block.shape, jnp.int32),
            pltpu.VMEM(ray_tiles.shape, F32),
            pltpu.VMEM(u_basis.shape, F32),
            pltpu.VMEM(v_prev.shape, F32),
            pltpu.VMEM(b_prev.shape, F32),
            pltpu.VMEM((rays // tile_rays, 2 * comps, width), F32),
            pltpu.VMEM((CHUNKS, pair, tile_count // CHUNKS * tile_rays), BF16),
            pltpu.VMEM((steps, 2 * width, 2 * width), BF16),
            pltpu.VMEM((steps, 2 * width, 2 * width), BF16),
            pltpu.VMEM((pair, 2 * width), F32),
            pltpu.VMEM((n_cell, (CAP + 1) * comps, width), F32),
            pltpu.VMEM((sources, (CAP + 1) * comps, width), F32),
            pltpu.VMEM((blocks,) + tile, F32),
            pltpu.VMEM((blocks,) + tile, F32),
            pltpu.VMEM((blocks,) + tile, F32),
            pltpu.VMEM((blocks,) + tile, F32),
            pltpu.VMEM((n_cell - 1, CAP) + tile, F32),
            pltpu.VMEM((n_cell, CAP) + tile, F32),
            pltpu.VMEM(tile, F32),
            pltpu.VMEM((n_cell,) + tile, F32),
            pltpu.VMEM((slots, 2 * comps, width), BF16),
            pltpu.VMEM((2,) + tile, F32),
            pltpu.VMEM((sources,) + tile, F32),
            pltpu.VMEM(v_prev.shape, F32),
            pltpu.SemaphoreType.DMA((CHUNKS,)),
            pltpu.SemaphoreType.DMA((6 + n_cell,)),
            far, far, cells, cells, one, one, cells, cells, cells, cells, one, one, far, far,
        ],
        compiler_params=pltpu.CompilerParams(
            collective_id=0, has_side_effects=True, vmem_limit_bytes=56 << 20
        ),
    )(tile_group, tile_slot, slot_block, ray_tiles, u_basis, v_prev, b_prev)


def per_device(n_ray, n_cell, ray_tiles, tile_group, tile_slot, slot_block, u_basis, v_prev, b_prev):
    tile_count, tile_rays, width = ray_tiles.shape
    comps, rays = u_basis.shape
    slots = slot_block.shape[1]
    blocks = v_prev.shape[1] // width
    piece = blocks // n_ray
    vmem = pl.BlockSpec(memory_space=pltpu.VMEM)
    smem = pl.BlockSpec(memory_space=pltpu.SMEM)
    anywhere = pl.BlockSpec(memory_space=pl.ANY)
    tile = (comps, width)
    packets = (n_cell, CAP + 1) + tile
    limit = 56 << 20
    if n_ray * n_cell <= DIRECT:
        v_next, small = fused(n_ray, n_cell, ray_tiles, tile_group, tile_slot, slot_block, u_basis, v_prev, b_prev)
    else:
        packet, high, low = pl.pallas_call(
            local_kernel,
            out_shape=(
                jax.ShapeDtypeStruct(packets, F32),
                jax.ShapeDtypeStruct((slots // 2, rays, 2 * width), BF16),
                jax.ShapeDtypeStruct((slots // 2, rays, 2 * width), BF16),
            ),
            in_specs=[smem, smem, smem, anywhere, vmem],
            out_specs=(vmem, anywhere, anywhere),
            scratch_shapes=[
                pltpu.VMEM(ray_tiles.shape, F32),
                pltpu.VMEM((rays, slots * width), F32),
                pltpu.VMEM((slots // 2, rays, 2 * width), BF16),
                pltpu.VMEM((slots // 2, rays, 2 * width), BF16),
                pltpu.SemaphoreType.DMA((CHUNKS,)),
                pltpu.SemaphoreType.DMA((2, slots // 2)),
            ],
            compiler_params=pltpu.CompilerParams(vmem_limit_bytes=limit),
        )(tile_group, tile_slot, slot_block, ray_tiles, u_basis)

        ray_sem = pltpu.SemaphoreType.DMA((n_ray - 1,))
        direct = min(n_ray * n_cell, DIRECT)
        all_sem = pltpu.SemaphoreType.DMA((direct - 1,))
        cell_sem = pltpu.SemaphoreType.DMA((n_cell - 1,))
        small_shape = (2 + rays // width,) + tile
        v_next, small = pl.pallas_call(
            functools.partial(step_kernel, n_ray, n_cell, v_prev.shape[1] * n_cell, rays * n_ray * n_cell),
            out_shape=(jax.ShapeDtypeStruct(v_prev.shape, F32), jax.ShapeDtypeStruct(small_shape, F32)),
            in_specs=[anywhere] * 6,
            out_specs=(anywhere, vmem),
            scratch_shapes=[
                pltpu.VMEM(packets, F32),
                pltpu.VMEM(u_basis.shape, F32),
                pltpu.VMEM(v_prev.shape, F32),
                pltpu.VMEM(b_prev.shape, F32),
                pltpu.VMEM(v_prev.shape, F32),
                pltpu.VMEM(packets, F32),
                pltpu.VMEM((n_ray, piece) + tile, F32),
                pltpu.VMEM((n_ray, piece) + tile, F32),
                pltpu.VMEM((n_ray, piece + 1) + tile, F32),
                pltpu.VMEM(packets, F32),
                pltpu.VMEM(packets, F32),
                pltpu.VMEM((n_ray,) + tile, F32),
                pltpu.VMEM((n_cell,) + tile, F32),
                pltpu.VMEM((direct,) + tile, F32),
                pltpu.VMEM((slots // 2, rays, 2 * width), BF16),
                pltpu.VMEM((slots // 2, rays, 2 * width), BF16),
                pltpu.VMEM((slots // 2, comps, 2 * width), F32),
                pltpu.SemaphoreType.DMA((7,)),
                cell_sem, cell_sem, ray_sem, ray_sem, ray_sem, ray_sem,
                cell_sem, cell_sem, ray_sem, ray_sem, cell_sem, cell_sem, all_sem, all_sem,
            ],
            compiler_params=pltpu.CompilerParams(
                collective_id=0, has_side_effects=True, vmem_limit_bytes=limit
            ),
        )(packet, high, low, u_basis, v_prev, b_prev)
    return pl.pallas_call(
        last_kernel,
        out_shape=(
            jax.ShapeDtypeStruct(v_prev.shape, F32),
            jax.ShapeDtypeStruct(u_basis.shape, F32),
            jax.ShapeDtypeStruct((comps, comps), F32),
            jax.ShapeDtypeStruct((comps, comps), F32),
        ),
        in_specs=[vmem, vmem],
        out_specs=(vmem, vmem, vmem, vmem),
    )(v_next, small)


def solution(mesh):
    in_specs = (
        P(("ray", "cell"), None, None),
        P(("ray", "cell"), None),
        P(("ray", "cell"), None),
        P(("ray", "cell"), None),
        P(None, ("ray", "cell")),
        P(None, "cell"),
        P(),
    )
    out_specs = (P(None, "cell"), P(None, ("ray", "cell")), P(), P())
    return jax.shard_map(
        functools.partial(per_device, mesh.shape["ray"], mesh.shape["cell"]),
        mesh=mesh,
        in_specs=in_specs,
        out_specs=out_specs,
        check_vma=False,
    )
```

```python
import functools

import jax
import jax.numpy as jnp
from jax import lax
from jax.experimental import pallas as pl
from jax.experimental.pallas import tpu as pltpu
from jax.sharding import PartitionSpec as P

CAP = 4
GROUPS = 8
CHUNKS = 8
UNROLL = 8
DIRECT = 32
BATCH = 4
MESH = pl.DeviceIdType.MESH
F32 = jnp.float32
BF16 = jnp.bfloat16


def split_rows(value):
    high = value.astype(BF16).astype(F32)
    return jnp.concatenate([high, value - high], axis=0).astype(BF16)


def local_kernel(group_ref, slot_ref, block_ref, tiles_hbm, u_ref, packet_ref, high_hbm, low_hbm, tiles, dense, high_ref, low_ref, sems, out_sems):
    tile_count, tile_rays, width = tiles.shape
    slots = block_ref.shape[1]
    per_chunk = tile_count // CHUNKS

    def chunk(i):
        rows = pl.ds(i * per_chunk, per_chunk)
        return pltpu.make_async_copy(tiles_hbm.at[rows], tiles.at[rows], sems.at[i])

    for i in range(CHUNKS):
        chunk(i).start()

    row = lax.broadcasted_iota(jnp.int32, (8, width), 0)
    for p in range(slots // CAP):
        index = jnp.full((8, width), -1, jnp.int32)
        for s in range(CAP):
            index = jnp.where(row == s, block_ref[0, p * CAP + s], index)
        packet_ref[p, CAP] = index.astype(F32)

    @pl.loop(0, slots)
    def _(s):
        dense[:, pl.ds(pl.multiple_of(s * width, width), width)] = jnp.zeros((dense.shape[0], width), F32)

    for i in range(CHUNKS):
        chunk(i).wait()

        @pl.loop(0, per_chunk // BATCH)
        def _(at):
            first = i * per_chunk + at * BATCH
            where = [(group_ref[0, first + n], slot_ref[0, first + n]) for n in range(BATCH)]
            values = [tiles[first + n] for n in range(BATCH)]
            for (group, slot), value in zip(where, values):
                rows = pl.ds(pl.multiple_of(group * tile_rays, tile_rays), tile_rays)
                columns = pl.ds(pl.multiple_of(slot * width, width), width)
                dense[rows, columns] += value

    u_pair = split_rows(u_ref[...])
    comps = u_ref.shape[0]
    span = 2 * width

    def stores(n):
        return [
            pltpu.make_async_copy(source.at[n], target.at[n], out_sems.at[at, n])
            for at, (source, target) in enumerate(((high_ref, high_hbm), (low_ref, low_hbm)))
        ]

    def product(n):
        columns = pl.ds(pl.multiple_of(n * span, span), span)
        block = dense[:, columns]
        high = block.astype(BF16)
        low = (block - high.astype(F32)).astype(BF16)
        high_ref[n] = high
        low_ref[n] = low
        for store in stores(n):
            store.start()
        both = jnp.dot(u_pair, high, preferred_element_type=F32)
        rest = jnp.dot(u_pair, low, preferred_element_type=F32)
        total = both[:comps] + (both[comps:] + rest[:comps])
        for half in range(2):
            s = 2 * n + half
            packet_ref[s // CAP, s % CAP] = total[:, half * width : (half + 1) * width]

    def finish(n):
        for store in stores(n):
            store.wait()

    each_peer(slots // 2, product, 0)
    each_peer(slots // 2, finish, 0)


def each_peer(n, body, first=1):
    if n <= UNROLL:
        for k in range(first, n):
            body(k)
    else:
        pl.loop(first, n)(body)


def row_of(tile, k):
    return jnp.broadcast_to(tile[k : k + 1, :], tile.shape)


def column_of(tile, k):
    return jnp.broadcast_to(tile[:, k : k + 1], (tile.shape[0], 128))


def gram(blocks):
    lane = lax.broadcasted_iota(jnp.int32, (8, 128), 1)
    tile = jnp.zeros((8, 128), F32)
    for j in range(8):
        products = blocks[0] * row_of(blocks[0], j)
        for block in blocks[1:]:
            products = products + block * row_of(block, j)
        tile = jnp.where(lane == j, jnp.sum(products, axis=1, keepdims=True), tile)
    return tile


def factor(tile):
    row = lax.broadcasted_iota(jnp.int32, (8, 128), 0)
    lane = lax.broadcasted_iota(jnp.int32, (8, 128), 1)
    lower = jnp.zeros((8, 128), F32)
    upper = jnp.zeros((8, 128), F32)
    inverse = jnp.where(row == lane, 1.0, 0.0).astype(F32)
    for j in range(8):
        across = row_of(tile, j)
        down = column_of(tile, j)
        scale = 1.0 / jnp.sqrt(row_of(down, j))
        across = across * scale
        down = jnp.where(row >= j, down * scale, 0.0)
        lower = jnp.where(lane == j, down, lower)
        upper = jnp.where((row == j) & (lane >= j), across, upper)
        tile = tile - down * across
        pivot = row_of(inverse, j) * scale
        inverse = jnp.where(row == j, pivot, inverse - jnp.where(row > j, down, 0.0) * pivot)
    return lower, upper, inverse


def columns_of(tile):
    return [column_of(tile, k) for k in range(8)]


def apply(columns, block):
    total = columns[0] * row_of(block, 0)
    for k in range(1, 8):
        total = total + columns[k] * row_of(block, k)
    return total


def step_kernel(
    n_ray, n_cell, cells_all, rays_all,
    packet_hbm, high_hbm, low_hbm, u_hbm, v_prev_hbm, b_hbm,
    v_hbm, small_ref,
    packet_ref, u_ref, v_prev_ref, b_ref, v_ref, slots_in, part, pieces_in, slab_in, back_out, back_in, ray_gram, cell_gram, all_gram, high, low, w_slots,
    load_sem, send1, recv1, send2, recv2, send3, recv3, send4, recv4, send5, recv5, send6, recv6, send7, recv7,
):
    ray = lax.axis_index("ray")
    cell = lax.axis_index("cell")
    piece = pieces_in.shape[1]
    blocks = n_ray * piece

    early = [
        pltpu.make_async_copy(source, target, load_sem.at[2 + i])
        for i, (source, target) in enumerate(
            ((packet_hbm, packet_ref), (u_hbm, u_ref), (v_prev_hbm, v_prev_ref), (b_hbm, b_ref))
        )
    ]
    for load in early:
        load.start()
    loads = [
        pltpu.make_async_copy(high_hbm, high, load_sem.at[0]),
        pltpu.make_async_copy(low_hbm, low, load_sem.at[1]),
    ]
    for load in loads:
        load.start()

    barrier = pltpu.get_barrier_semaphore()

    each_peer(n_ray, lambda k: pl.semaphore_signal(barrier, inc=1, device_id={"ray": lax.rem(ray + k, n_ray)}, device_id_type=MESH))

    each_peer(n_cell, lambda k: pl.semaphore_signal(barrier, inc=1, device_id={"cell": lax.rem(cell + k, n_cell)}, device_id_type=MESH))

    pl.semaphore_wait(barrier, n_ray + n_cell - 2)

    def over(axis, me, n, source, target, send, recv):
        def copy(k):
            peer = lax.rem(me + k, n)
            return pltpu.make_async_remote_copy(
                src_ref=source(peer),
                dst_ref=target(me),
                send_sem=send.at[k - 1],
                recv_sem=recv.at[k - 1],
                device_id={axis: peer},
                device_id_type=MESH,
            )

        def wait_recv(k):
            origin = lax.rem(me + n - k, n)
            pltpu.make_async_remote_copy(
                src_ref=source(lax.rem(me + k, n)),
                dst_ref=target(origin),
                send_sem=send.at[k - 1],
                recv_sem=recv.at[k - 1],
                device_id={axis: lax.rem(me + k, n)},
                device_id_type=MESH,
            ).wait_recv()

        def receive():
            each_peer(n, wait_recv)

        def finish():
            each_peer(n, lambda k: copy(k).wait_send())

        return copy, receive, finish

    to_slab, from_slots, end1 = over(
        "cell", cell, n_cell, lambda peer: packet_ref.at[peer], lambda me: slots_in.at[me], send1, recv1
    )
    early[0].wait()
    each_peer(n_cell, lambda k: to_slab(k).start())
    for load in early[1:]:
        load.wait()
    slots_in[cell] = packet_ref[cell]
    from_slots()

    def index_tiles(p):
        tile = slots_in[p, CAP]
        return [row_of(tile, s) for s in range(CAP)]

    indices = [index_tiles(p) for p in range(n_cell)]

    def dense_block(b):
        number = jnp.full((8, 128), b, jnp.int32).astype(F32)
        total = jnp.zeros((8, 128), F32)
        for p in range(n_cell):
            for s in range(CAP):
                total = total + jnp.where(indices[p][s] == number, slots_in[p, s], 0.0)
        return total

    to_piece, from_pieces, end2 = over(
        "ray", ray, n_ray, lambda peer: part.at[peer], lambda me: pieces_in.at[me], send2, recv2
    )

    def send_piece(k):
        peer = lax.rem(ray + k, n_ray)
        for i in range(piece):
            part[peer, i] = dense_block(peer * piece + i)
        to_piece(k).start()

    each_peer(n_ray, send_piece)

    for i in range(piece):
        pieces_in[ray, i] = dense_block(ray * piece + i)

    b_columns = columns_of(b_ref[...])
    known = []
    for i in range(piece):
        at = pl.multiple_of((ray * piece + i) * 128, 128)
        known.append(apply(b_columns, v_prev_ref[:, pl.ds(at, 128)]))
    from_pieces()
    own = []
    for i in range(piece):
        total = pieces_in[0, i]
        for r in range(1, n_ray):
            total = total + pieces_in[r, i]
        own.append(total - known[i])
        slab_in[ray, i] = own[i]
    slab_in[ray, piece] = gram(own)

    to_ray, from_ray, end3 = over(
        "ray", ray, n_ray, lambda peer: slab_in.at[ray], lambda me: slab_in.at[me], send3, recv3
    )
    each_peer(n_ray, lambda k: to_ray(k).start())
    from_ray()

    slab_gram = slab_in[0, piece]
    for r in range(1, n_ray):
        slab_gram = slab_gram + slab_in[r, piece]

    def answer(p):
        wanted = index_tiles(p)
        found = [jnp.zeros((8, 128), F32) for s in range(CAP)]
        for b in range(blocks):
            block = slab_in[b // piece, b % piece]
            for s in range(CAP):
                found[s] = jnp.where(wanted[s] == float(b), block, found[s])
        return found

    to_cell, from_cell, end4 = over(
        "cell", cell, n_cell, lambda peer: back_out.at[peer], lambda me: back_in.at[me], send4, recv4
    )

    def send_answer(k):
        peer = lax.rem(cell + k, n_cell)
        found = answer(peer)
        for s in range(CAP):
            back_out[peer, s] = found[s]
        back_out[peer, CAP] = slab_gram
        to_cell(k).start()

    each_peer(n_cell, send_answer)

    found = answer(cell)
    for s in range(CAP):
        back_in[cell, s] = found[s]
    back_in[cell, CAP] = slab_gram
    for load in loads:
        load.wait()
    from_cell()

    whole_gram = back_in[0, CAP]
    for p in range(1, n_cell):
        whole_gram = whole_gram + back_in[p, CAP]
    for p in range(n_cell):
        for s in range(CAP):
            at = p * CAP + s
            w_slots[at // 2, :, (at % 2) * 128 : (at % 2 + 1) * 128] = back_in[p, s]
    across = (((1,), (1,)), ((), ()))

    def image_of(n):
        w_pair = split_rows(w_slots[n])
        both = lax.dot_general(w_pair, high[n], across, preferred_element_type=F32)
        rest = lax.dot_general(w_pair, low[n], across, preferred_element_type=F32)
        return both[:8] + (both[8:] + rest[:8])

    steps = high.shape[0]
    if steps <= UNROLL:
        image = image_of(0)
        for n in range(1, steps):
            image = image + image_of(n)
    else:
        image = lax.fori_loop(1, steps, lambda n, total: total + image_of(n), image_of(0))

    alpha, alpha_t, alpha_inverse = factor(whole_gram * (1.0 / cells_all))
    inverse_columns = columns_of(alpha_inverse)
    alpha_t_columns = columns_of(alpha_t)
    ray_blocks = u_ref.shape[1] // 128
    residual = []
    for i in range(ray_blocks):
        lanes = slice(i * 128, (i + 1) * 128)
        residual.append(apply(inverse_columns, image[:, lanes]) - apply(alpha_t_columns, u_ref[:, lanes]))
    everyone = n_ray * n_cell
    flat = ray * n_cell + cell
    own_gram = gram(residual)

    def gram_copy(k, back):
        peer = lax.rem(flat + k, everyone)
        slot = lax.rem(flat + everyone - k, everyone) if back else flat
        return pltpu.make_async_remote_copy(
            src_ref=all_gram.at[flat],
            dst_ref=all_gram.at[slot],
            send_sem=send7.at[k - 1],
            recv_sem=recv7.at[k - 1],
            device_id={"ray": lax.div(peer, n_cell), "cell": lax.rem(peer, n_cell)},
            device_id_type=MESH,
        )

    if everyone <= DIRECT:
        all_gram[flat] = own_gram
        for k in range(1, everyone):
            gram_copy(k, False).start()
    else:
        ray_gram[ray] = own_gram
        to_gram, from_gram, end5 = over(
            "ray", ray, n_ray, lambda peer: ray_gram.at[ray], lambda me: ray_gram.at[me], send5, recv5
        )
        each_peer(n_ray, lambda k: to_gram(k).start())

    small_ref[0] = alpha
    for i in range(ray_blocks):
        small_ref[2 + i] = residual[i]
    for b in range(blocks):
        v_ref[:, b * 128 : (b + 1) * 128] = apply(inverse_columns, slab_in[b // piece, b % piece])
    store = pltpu.make_async_copy(v_ref, v_hbm, load_sem.at[6])
    store.start()

    if everyone <= DIRECT:
        for k in range(1, everyone):
            gram_copy(k, True).wait_recv()
        total = all_gram[0]
        for d in range(1, everyone):
            total = total + all_gram[d]
    else:
        from_gram()
        total = ray_gram[0]
        for r in range(1, n_ray):
            total = total + ray_gram[r]
        cell_gram[cell] = total
        to_total, from_total, end6 = over(
            "cell", cell, n_cell, lambda peer: cell_gram.at[cell], lambda me: cell_gram.at[me], send6, recv6
        )
        each_peer(n_cell, lambda k: to_total(k).start())
        from_total()
        total = cell_gram[0]
        for p in range(1, n_cell):
            total = total + cell_gram[p]
    small_ref[1] = total * (1.0 / rays_all)
    store.wait()
    for end in (end1, end2, end3, end4):
        end()
    if everyone <= DIRECT:
        for k in range(1, everyone):
            gram_copy(k, False).wait_send()
    else:
        end5()
        end6()


def last_kernel(v_hbm, small_hbm, v_out, u_out, alpha_out, beta_out, small, u_ref, alpha_ref, beta_ref, sems):
    v_copy = pltpu.make_async_copy(v_hbm, v_out, sems.at[0])
    load = pltpu.make_async_copy(small_hbm, small, sems.at[1])
    load.start()
    v_copy.start()
    load.wait()
    alpha_ref[...] = small[0][:, :8]
    beta, _, beta_inverse = factor(small[1])
    beta_ref[...] = beta[:, :8]
    beta_columns = columns_of(beta_inverse)
    for i in range(small.shape[0] - 2):
        u_ref[:, i * 128 : (i + 1) * 128] = apply(beta_columns, small[2 + i])
    stores = [
        pltpu.make_async_copy(source, target, sems.at[2 + i])
        for i, (source, target) in enumerate(((u_ref, u_out), (alpha_ref, alpha_out), (beta_ref, beta_out)))
    ]
    for store in stores:
        store.start()
    v_copy.wait()
    for store in stores:
        store.wait()


def flips_of(index, count):
    flips, bit = {}, 1
    while bit < count:
        flips[bit] = bit * (1 - 2 * lax.rem(lax.div(index, bit), 2))
        bit *= 2
    return flips


def flipped(index, flips, mask):
    for bit, step in flips.items():
        if mask & bit:
            index = index + step
    return index


def far_first(n_ray, n_cell):
    masks = [(2 * a, c) for a in range(n_ray // 2) for c in range(n_cell) if a or c]
    return sorted(masks, key=lambda m: -(2 * bin(m[0]).count("1") + m[1]))


def halves_of(value):
    high = value.astype(BF16)
    return high, (value - high.astype(F32)).astype(BF16)


def fused_kernel(
    n_ray, n_cell, cells_all, rays_all,
    group_hbm, slot_hbm, block_hbm, tiles_hbm, u_hbm, v_prev_hbm, b_hbm,
    v_hbm, small_ref,
    group_ref, slot_ref, block_ref, asked_ref, asked_twin_ref, index_out, index_in, index_twin, tiles, u_ref, v_prev_ref, b_ref,
    u_twice, spread, split, turned, sums, packet, recv, part, part_in, known, w_ref,
    back_out, back_in, gram_out, gram_in, w_slots, pair_gram, all_gram, v_ref,
    tile_sem, load_sem, send1, recv1, send2, recv2, send3, recv3, send4, recv4, send5, recv5, send6, recv6, send7, recv7, send8, recv8,
):
    ray = lax.axis_index("ray")
    cell = lax.axis_index("cell")
    tile_count, tile_rays, width = tiles.shape
    slots = block_ref.shape[1]
    comps = u_ref.shape[0]
    sources = n_ray // 2 * n_cell
    blocks = w_ref.shape[0]
    steps, span = split.shape[0], split.shape[1]
    chunks = tile_sem.shape[0]
    per_chunk = tile_count // chunks
    per_step = steps // chunks
    quad = span // tile_rays

    small_loads = [
        pltpu.make_async_copy(source, target, load_sem.at[i])
        for i, (source, target) in enumerate(
            (
                (u_hbm, u_ref), (slot_hbm, slot_ref), (group_hbm, group_ref), (block_hbm, block_ref),
                (v_prev_hbm, v_prev_ref), (b_hbm, b_ref),
            )
        )
    ]

    def chunk(i):
        rows = pl.ds(i * per_chunk, per_chunk)
        return pltpu.make_async_copy(tiles_hbm.at[rows], tiles.at[rows], tile_sem.at[i])

    for load in small_loads[:4]:
        load.start()
    for i in range(chunks):
        chunk(i).start()
    for load in small_loads[4:]:
        load.start()

    ray_flips = flips_of(ray, n_ray)
    cell_flips = flips_of(cell, n_cell)
    masks = far_first(n_ray, n_cell)
    peers = [(flipped(ray, ray_flips, a), flipped(cell, cell_flips, c)) for a, c in masks]
    twin = ray + ray_flips[1]
    cell_masks = list(range(n_cell - 1, 0, -1))
    cell_peers = [flipped(cell, cell_flips, c) for c in cell_masks]
    twins = [(twin, c) for c in cell_peers] + [(twin, cell)]
    core = lax.rem(ray, 2)
    other = 1 - core

    def number_of(ray_at, cell_at):
        return lax.div(ray_at, 2) * n_cell + cell_at

    me = number_of(ray, cell)

    barrier = pltpu.get_barrier_semaphore()
    for r, c in peers + twins:
        pl.semaphore_signal(barrier, inc=1, device_id={"ray": r, "cell": c}, device_id_type=MESH)

    def remote(source, target, send, recv_at, r, c):
        return pltpu.make_async_remote_copy(
            src_ref=source, dst_ref=target, send_sem=send, recv_sem=recv_at,
            device_id={"ray": r, "cell": c}, device_id_type=MESH,
        )

    for load in small_loads[:4]:
        load.wait()

    low = lax.broadcasted_iota(jnp.int32, (8, width), 1) < tile_rays
    low_pair = lax.broadcasted_iota(jnp.int32, (2 * comps, width), 1) < tile_rays
    lane = lax.broadcasted_iota(jnp.int32, (8, width), 1)
    for q in range(u_ref.shape[1] // width):
        block = u_ref[:, q * width : (q + 1) * width]
        turn = pltpu.roll(block, tile_rays, 1)
        for half, both in enumerate((jnp.where(low, block, turn), jnp.where(low, turn, block))):
            high = both.astype(BF16).astype(F32)
            u_twice[2 * q + half, :comps] = high
            u_twice[2 * q + half, comps:] = both - high

    @pl.loop(0, chunks)
    def _(c):
        for q in range(per_chunk // 2):
            at = c * per_chunk + 2 * q
            value = jnp.where(low_pair, u_twice[group_ref[0, at]], u_twice[group_ref[0, at + 1]])
            where = jnp.where(low_pair, slot_ref[0, at], slot_ref[0, at + 1])
            for s in range(slots):
                spread[c, s * 2 * comps : (s + 1) * 2 * comps, q * width : (q + 1) * width] = jnp.where(
                    where == s, value, 0.0
                ).astype(BF16)

    for p in range(n_cell):
        index = jnp.zeros((1, width), jnp.int32)
        for s in range(CAP):
            index = jnp.where(lane[:1] == me * CAP + s, block_ref[0, p * CAP + s] + 1, index)
        index_out[p] = index
    index_in[me] = index_out[cell]

    pl.semaphore_wait(barrier, len(peers) + len(twins))
    indices = [
        remote(index_out.at[c], index_in.at[me], send2.at[i], recv2.at[i], r, c) for i, (r, c) in enumerate(peers)
    ] + [
        remote(index_out.at[c], index_twin.at[cell], send8.at[i], recv8.at[i], r, c) for i, (r, c) in enumerate(twins)
    ]
    for copy in indices:
        copy.start()

    for i in range(chunks):
        chunk(i).wait()
        value = tiles[i * per_chunk : (i + 1) * per_chunk].reshape(per_chunk * tile_rays, width)
        high, rest = halves_of(value)
        both = jnp.concatenate([high, rest], axis=1)
        split[i * per_step : (i + 1) * per_step] = both.reshape(per_step, span, 2 * width)
        product = jnp.dot(spread[i], both, preferred_element_type=F32)
        if i == 0:
            sums[...] = product
        else:
            sums[...] += product

    for s in range(slots):
        rows = sums[s * 2 * comps : (s + 1) * 2 * comps]
        rows = rows[:, :width] + rows[:, width:]
        packet[s // CAP, s % CAP * comps : (s % CAP + 1) * comps] = rows[:comps] + rows[comps:]
    recv[me] = packet[cell]

    first = [
        remote(packet.at[c], recv.at[me], send1.at[i], recv1.at[i], r, c) for i, (r, c) in enumerate(peers)
    ]
    for copy in first:
        copy.start()
    for load in small_loads[4:]:
        load.wait()
    b_columns = columns_of(b_ref[...])
    for b in range(blocks):
        known[b] = apply(b_columns, v_prev_ref[:, b * width : (b + 1) * width])

    @pl.loop(0, steps)
    def _(n):
        turned[n] = split[n].T

    for i, (r, c) in enumerate(peers):
        remote(index_out.at[c], index_in.at[number_of(r, c)], send2.at[i], recv2.at[i], r, c).wait_recv()
    for i, (r, c) in enumerate(twins):
        remote(index_out.at[c], index_twin.at[c], send8.at[i], recv8.at[i], r, c).wait_recv()
    ask_loads = [
        pltpu.make_async_copy(index_in, asked_ref, load_sem.at[6]),
        pltpu.make_async_copy(index_twin, asked_twin_ref, load_sem.at[7]),
    ]
    for load in ask_loads:
        load.start()
    asked = jnp.sum(index_in[:, 0, :], axis=0, keepdims=True) - 1
    row = lax.broadcasted_iota(jnp.int32, (blocks, width), 0)
    pick = jnp.where(row == jnp.broadcast_to(asked, (blocks, width)), 1.0, 0.0)[:, : sources * CAP].astype(BF16)
    for load in ask_loads:
        load.wait()

    for i, (r, c) in enumerate(peers):
        remote(packet.at[c], recv.at[number_of(r, c)], send1.at[i], recv1.at[i], r, c).wait_recv()

    flat = recv.reshape(sources * CAP * comps, width)
    part_rows = part.reshape(blocks * comps, width)
    for r in range(comps):
        high, rest = halves_of(flat[pl.ds(r, sources * CAP, stride=comps), :])
        both = jnp.dot(pick, jnp.concatenate([high, rest], axis=1), preferred_element_type=F32)
        part_rows[pl.ds(r, blocks, stride=comps), :] = both[:, :width] + both[:, width:]

    share = (1 - core).astype(F32)

    def answer(target, ref):
        for s in range(CAP):
            b = jnp.maximum(ref(s) - 1, 0)
            target[s] = part[b] - share * known[b]

    answers = []
    for i, (r, c) in enumerate([(ray, c) for c in cell_peers] + twins):
        if i < len(cell_peers):
            answer(back_out.at[i], lambda s: asked_ref[number_of(r, c), 0, number_of(r, c) * CAP + s])
        else:
            answer(back_out.at[i], lambda s: asked_twin_ref[c, 0, number_of(r, c) * CAP + s])
        answers.append(remote(back_out.at[i], back_in.at[core, cell], send4.at[i], recv4.at[i], r, c))
        answers[i].start()
    swap = remote(part, part_in, send3.at[0], recv3.at[0], twin, cell)
    swap.start()
    answer(back_in.at[core, cell], lambda s: block_ref[0, cell * CAP + s] + 1)
    swap.wait_recv()
    for b in range(blocks):
        w_ref[b] = part[b] + part_in[b] - known[b]

    slab_gram = gram([w_ref[b] for b in range(blocks)])
    gram_out[...] = slab_gram
    gram_in[cell] = slab_gram
    grams = [
        remote(gram_out, gram_in.at[cell], send5.at[i], recv5.at[i], ray, c) for i, c in enumerate(cell_peers)
    ]
    for copy in grams:
        copy.start()

    for i, (r, c) in enumerate([(ray, c) for c in cell_peers] + twins):
        k = core if i < len(cell_peers) else other
        remote(back_out.at[i], back_in.at[k, c], send4.at[i], recv4.at[i], r, c).wait_recv()
    for p in range(n_cell):
        for s in range(CAP):
            w_slots[p * CAP + s] = split_rows(back_in[0, p, s] + back_in[1, p, s])

    groups = u_ref.shape[1] // tile_rays
    totals = [jnp.zeros((8, width), F32) for g in range(groups)]
    for n in range(steps):
        at = n * quad
        rows = jnp.concatenate([w_slots[slot_ref[0, at + j]] for j in range(quad)], axis=0)
        found = jnp.dot(jnp.concatenate([rows, rows], axis=1), turned[n], preferred_element_type=F32)
        for j in range(quad // 2):
            lanes = slice(j * width, (j + 1) * width)
            top = 2 * j * 2 * comps
            pair = jnp.where(
                low_pair, found[top : top + 2 * comps, lanes], found[top + 2 * comps : top + 4 * comps, lanes]
            )
            pair = pair[:comps] + pair[comps:]
            owner = jnp.where(low, group_ref[0, at + 2 * j], group_ref[0, at + 2 * j + 1])
            for g in range(groups):
                totals[g] = totals[g] + jnp.where(owner == g, pair, 0.0)

    for i, c in enumerate(cell_peers):
        remote(gram_out, gram_in.at[c], send5.at[i], recv5.at[i], ray, c).wait_recv()
    whole_gram = gram_in[0]
    for p in range(1, n_cell):
        whole_gram = whole_gram + gram_in[p]
    alpha, alpha_t, alpha_inverse = factor(whole_gram * (1.0 / cells_all))
    inverse_columns = columns_of(alpha_inverse)
    alpha_t_columns = columns_of(alpha_t)
    totals = [total + pltpu.roll(total, tile_rays, 1) for total in totals]
    ray_blocks = u_ref.shape[1] // width
    residual = []
    for i in range(ray_blocks):
        image = jnp.where(low, totals[2 * i], totals[2 * i + 1])
        lanes = slice(i * width, (i + 1) * width)
        residual.append(apply(inverse_columns, image) - apply(alpha_t_columns, u_ref[:, lanes]))
    pair_gram[0] = gram(residual)
    pairs = remote(pair_gram.at[0], pair_gram.at[1], send6.at[0], recv6.at[0], twin, cell)
    pairs.start()
    small_ref[0] = alpha
    for i in range(ray_blocks):
        small_ref[2 + i] = residual[i]
    pairs.wait_recv()
    all_gram[me] = pair_gram[0] + pair_gram[1]
    last = [
        remote(all_gram.at[me], all_gram.at[me], send7.at[i], recv7.at[i], r, c) for i, (r, c) in enumerate(peers)
    ]
    for copy in last:
        copy.start()
    for b in range(blocks):
        v_ref[:, b * width : (b + 1) * width] = apply(inverse_columns, w_ref[b])
    store = pltpu.make_async_copy(v_ref, v_hbm, load_sem.at[8])
    store.start()
    for i, (r, c) in enumerate(peers):
        remote(all_gram.at[me], all_gram.at[number_of(r, c)], send7.at[i], recv7.at[i], r, c).wait_recv()
    total = all_gram[0]
    for d in range(1, sources):
        total = total + all_gram[d]
    small_ref[1] = total * (1.0 / rays_all)
    store.wait()
    for copy in first + indices + [swap] + answers + grams + [pairs] + last:
        copy.wait_send()


def fused(n_ray, n_cell, ray_tiles, tile_group, tile_slot, slot_block, u_basis, v_prev, b_prev):
    tile_count, tile_rays, width = ray_tiles.shape
    comps, rays = u_basis.shape
    slots = slot_block.shape[1]
    blocks = v_prev.shape[1] // width
    sources = n_ray // 2 * n_cell
    steps = tile_count * tile_rays // (2 * width)
    vmem = pl.BlockSpec(memory_space=pltpu.VMEM)
    anywhere = pl.BlockSpec(memory_space=pl.ANY)
    tile = (comps, width)
    pair = slots * 2 * comps
    one = pltpu.SemaphoreType.DMA((1,))
    far = pltpu.SemaphoreType.DMA((sources - 1,))
    cells = pltpu.SemaphoreType.DMA((n_cell - 1,))
    both = pltpu.SemaphoreType.DMA((2 * n_cell - 1,))
    every = pltpu.SemaphoreType.DMA((n_cell,))
    return pl.pallas_call(
        functools.partial(fused_kernel, n_ray, n_cell, v_prev.shape[1] * n_cell, rays * n_ray * n_cell),
        out_shape=(
            jax.ShapeDtypeStruct(v_prev.shape, F32),
            jax.ShapeDtypeStruct((2 + rays // width,) + tile, F32),
        ),
        in_specs=[anywhere] * 7,
        out_specs=(anywhere, vmem),
        scratch_shapes=[
            pltpu.SMEM(tile_group.shape, jnp.int32),
            pltpu.SMEM(tile_slot.shape, jnp.int32),
            pltpu.SMEM(slot_block.shape, jnp.int32),
            pltpu.SMEM((sources, 1, width), jnp.int32),
            pltpu.SMEM((n_cell, 1, width), jnp.int32),
            pltpu.VMEM((n_cell, 1, width), jnp.int32),
            pltpu.VMEM((sources, 1, width), jnp.int32),
            pltpu.VMEM((n_cell, 1, width), jnp.int32),
            pltpu.VMEM(ray_tiles.shape, F32),
            pltpu.VMEM(u_basis.shape, F32),
            pltpu.VMEM(v_prev.shape, F32),
            pltpu.VMEM(b_prev.shape, F32),
            pltpu.VMEM((rays // tile_rays, 2 * comps, width), F32),
            pltpu.VMEM((CHUNKS, pair, tile_count // CHUNKS * tile_rays), BF16),
            pltpu.VMEM((steps, 2 * width, 2 * width), BF16),
            pltpu.VMEM((steps, 2 * width, 2 * width), BF16),
            pltpu.VMEM((pair, 2 * width), F32),
            pltpu.VMEM((n_cell, CAP * comps, width), F32),
            pltpu.VMEM((sources, CAP * comps, width), F32),
            pltpu.VMEM((blocks,) + tile, F32),
            pltpu.VMEM((blocks,) + tile, F32),
            pltpu.VMEM((blocks,) + tile, F32),
            pltpu.VMEM((blocks,) + tile, F32),
            pltpu.VMEM((2 * n_cell - 1, CAP) + tile, F32),
            pltpu.VMEM((2, n_cell, CAP) + tile, F32),
            pltpu.VMEM(tile, F32),
            pltpu.VMEM((n_cell,) + tile, F32),
            pltpu.VMEM((slots, 2 * comps, width), BF16),
            pltpu.VMEM((2,) + tile, F32),
            pltpu.VMEM((sources,) + tile, F32),
            pltpu.VMEM(v_prev.shape, F32),
            pltpu.SemaphoreType.DMA((CHUNKS,)),
            pltpu.SemaphoreType.DMA((9,)),
            far, far, far, far, one, one, both, both, cells, cells, one, one, far, far, every, every,
        ],
        compiler_params=pltpu.CompilerParams(
            collective_id=0, has_side_effects=True, vmem_limit_bytes=56 << 20
        ),
    )(tile_group, tile_slot, slot_block, ray_tiles, u_basis, v_prev, b_prev)


def per_device(n_ray, n_cell, ray_tiles, tile_group, tile_slot, slot_block, u_basis, v_prev, b_prev):
    tile_count, tile_rays, width = ray_tiles.shape
    comps, rays = u_basis.shape
    slots = slot_block.shape[1]
    blocks = v_prev.shape[1] // width
    piece = blocks // n_ray
    vmem = pl.BlockSpec(memory_space=pltpu.VMEM)
    smem = pl.BlockSpec(memory_space=pltpu.SMEM)
    anywhere = pl.BlockSpec(memory_space=pl.ANY)
    tile = (comps, width)
    packets = (n_cell, CAP + 1) + tile
    limit = 56 << 20
    small_shape = (2 + rays // width,) + tile
    if n_ray * n_cell <= DIRECT:
        v_next, small = fused(n_ray, n_cell, ray_tiles, tile_group, tile_slot, slot_block, u_basis, v_prev, b_prev)
    else:
        packet, high, low = pl.pallas_call(
            local_kernel,
            out_shape=(
                jax.ShapeDtypeStruct(packets, F32),
                jax.ShapeDtypeStruct((slots // 2, rays, 2 * width), BF16),
                jax.ShapeDtypeStruct((slots // 2, rays, 2 * width), BF16),
            ),
            in_specs=[smem, smem, smem, anywhere, vmem],
            out_specs=(vmem, anywhere, anywhere),
            scratch_shapes=[
                pltpu.VMEM(ray_tiles.shape, F32),
                pltpu.VMEM((rays, slots * width), F32),
                pltpu.VMEM((slots // 2, rays, 2 * width), BF16),
                pltpu.VMEM((slots // 2, rays, 2 * width), BF16),
                pltpu.SemaphoreType.DMA((CHUNKS,)),
                pltpu.SemaphoreType.DMA((2, slots // 2)),
            ],
            compiler_params=pltpu.CompilerParams(vmem_limit_bytes=limit),
        )(tile_group, tile_slot, slot_block, ray_tiles, u_basis)

        ray_sem = pltpu.SemaphoreType.DMA((n_ray - 1,))
        direct = min(n_ray * n_cell, DIRECT)
        all_sem = pltpu.SemaphoreType.DMA((direct - 1,))
        cell_sem = pltpu.SemaphoreType.DMA((n_cell - 1,))
        v_next, small = pl.pallas_call(
            functools.partial(step_kernel, n_ray, n_cell, v_prev.shape[1] * n_cell, rays * n_ray * n_cell),
            out_shape=(jax.ShapeDtypeStruct(v_prev.shape, F32), jax.ShapeDtypeStruct(small_shape, F32)),
            in_specs=[anywhere] * 6,
            out_specs=(anywhere, vmem),
            scratch_shapes=[
                pltpu.VMEM(packets, F32),
                pltpu.VMEM(u_basis.shape, F32),
                pltpu.VMEM(v_prev.shape, F32),
                pltpu.VMEM(b_prev.shape, F32),
                pltpu.VMEM(v_prev.shape, F32),
                pltpu.VMEM(packets, F32),
                pltpu.VMEM((n_ray, piece) + tile, F32),
                pltpu.VMEM((n_ray, piece) + tile, F32),
                pltpu.VMEM((n_ray, piece + 1) + tile, F32),
                pltpu.VMEM(packets, F32),
                pltpu.VMEM(packets, F32),
                pltpu.VMEM((n_ray,) + tile, F32),
                pltpu.VMEM((n_cell,) + tile, F32),
                pltpu.VMEM((direct,) + tile, F32),
                pltpu.VMEM((slots // 2, rays, 2 * width), BF16),
                pltpu.VMEM((slots // 2, rays, 2 * width), BF16),
                pltpu.VMEM((slots // 2, comps, 2 * width), F32),
                pltpu.SemaphoreType.DMA((7,)),
                cell_sem, cell_sem, ray_sem, ray_sem, ray_sem, ray_sem,
                cell_sem, cell_sem, ray_sem, ray_sem, cell_sem, cell_sem, all_sem, all_sem,
            ],
            compiler_params=pltpu.CompilerParams(
                collective_id=0, has_side_effects=True, vmem_limit_bytes=limit
            ),
        )(packet, high, low, u_basis, v_prev, b_prev)
    return pl.pallas_call(
        last_kernel,
        out_shape=(
            jax.ShapeDtypeStruct(v_prev.shape, F32),
            jax.ShapeDtypeStruct(u_basis.shape, F32),
            jax.ShapeDtypeStruct((comps, comps), F32),
            jax.ShapeDtypeStruct((comps, comps), F32),
        ),
        in_specs=[anywhere, anywhere],
        out_specs=(anywhere, anywhere, anywhere, anywhere),
        scratch_shapes=[
            pltpu.VMEM(small_shape, F32),
            pltpu.VMEM(u_basis.shape, F32),
            pltpu.VMEM((comps, comps), F32),
            pltpu.VMEM((comps, comps), F32),
            pltpu.SemaphoreType.DMA((5,)),
        ],
    )(v_next, small)


def solution(mesh):
    in_specs = (
        P(("ray", "cell"), None, None),
        P(("ray", "cell"), None),
        P(("ray", "cell"), None),
        P(("ray", "cell"), None),
        P(None, ("ray", "cell")),
        P(None, "cell"),
        P(),
    )
    out_specs = (P(None, "cell"), P(None, ("ray", "cell")), P(), P())
    return jax.shard_map(
        functools.partial(per_device, mesh.shape["ray"], mesh.shape["cell"]),
        mesh=mesh,
        in_specs=in_specs,
        out_specs=out_specs,
        check_vma=False,
    )
```

```python
import functools

import jax
import jax.numpy as jnp
from jax import lax
from jax.experimental import pallas as pl
from jax.experimental.pallas import tpu as pltpu
from jax.sharding import PartitionSpec as P

CAP = 4
GROUPS = 8
CHUNKS = 8
UNROLL = 8
DIRECT = 32
BATCH = 4
MESH = pl.DeviceIdType.MESH
F32 = jnp.float32
BF16 = jnp.bfloat16


def split_rows(value):
    high = value.astype(BF16).astype(F32)
    return jnp.concatenate([high, value - high], axis=0).astype(BF16)


def local_kernel(group_ref, slot_ref, block_ref, tiles_hbm, u_ref, packet_ref, high_hbm, low_hbm, tiles, dense, high_ref, low_ref, sems, out_sems):
    tile_count, tile_rays, width = tiles.shape
    slots = block_ref.shape[1]
    per_chunk = tile_count // CHUNKS

    def chunk(i):
        rows = pl.ds(i * per_chunk, per_chunk)
        return pltpu.make_async_copy(tiles_hbm.at[rows], tiles.at[rows], sems.at[i])

    for i in range(CHUNKS):
        chunk(i).start()

    row = lax.broadcasted_iota(jnp.int32, (8, width), 0)
    for p in range(slots // CAP):
        index = jnp.full((8, width), -1, jnp.int32)
        for s in range(CAP):
            index = jnp.where(row == s, block_ref[0, p * CAP + s], index)
        packet_ref[p, CAP] = index.astype(F32)

    @pl.loop(0, slots)
    def _(s):
        dense[:, pl.ds(pl.multiple_of(s * width, width), width)] = jnp.zeros((dense.shape[0], width), F32)

    for i in range(CHUNKS):
        chunk(i).wait()

        @pl.loop(0, per_chunk // BATCH)
        def _(at):
            first = i * per_chunk + at * BATCH
            where = [(group_ref[0, first + n], slot_ref[0, first + n]) for n in range(BATCH)]
            values = [tiles[first + n] for n in range(BATCH)]
            for (group, slot), value in zip(where, values):
                rows = pl.ds(pl.multiple_of(group * tile_rays, tile_rays), tile_rays)
                columns = pl.ds(pl.multiple_of(slot * width, width), width)
                dense[rows, columns] += value

    u_pair = split_rows(u_ref[...])
    comps = u_ref.shape[0]
    span = 2 * width

    def stores(n):
        return [
            pltpu.make_async_copy(source.at[n], target.at[n], out_sems.at[at, n])
            for at, (source, target) in enumerate(((high_ref, high_hbm), (low_ref, low_hbm)))
        ]

    def product(n):
        columns = pl.ds(pl.multiple_of(n * span, span), span)
        block = dense[:, columns]
        high = block.astype(BF16)
        low = (block - high.astype(F32)).astype(BF16)
        high_ref[n] = high
        low_ref[n] = low
        for store in stores(n):
            store.start()
        both = jnp.dot(u_pair, high, preferred_element_type=F32)
        rest = jnp.dot(u_pair, low, preferred_element_type=F32)
        total = both[:comps] + (both[comps:] + rest[:comps])
        for half in range(2):
            s = 2 * n + half
            packet_ref[s // CAP, s % CAP] = total[:, half * width : (half + 1) * width]

    def finish(n):
        for store in stores(n):
            store.wait()

    each_peer(slots // 2, product, 0)
    each_peer(slots // 2, finish, 0)


def each_peer(n, body, first=1):
    if n <= UNROLL:
        for k in range(first, n):
            body(k)
    else:
        pl.loop(first, n)(body)


def row_of(tile, k):
    return jnp.broadcast_to(tile[k : k + 1, :], tile.shape)


def column_of(tile, k):
    return jnp.broadcast_to(tile[:, k : k + 1], (tile.shape[0], 128))


def gram(blocks):
    lane = lax.broadcasted_iota(jnp.int32, (8, 128), 1)
    tile = jnp.zeros((8, 128), F32)
    for j in range(8):
        products = blocks[0] * row_of(blocks[0], j)
        for block in blocks[1:]:
            products = products + block * row_of(block, j)
        tile = jnp.where(lane == j, jnp.sum(products, axis=1, keepdims=True), tile)
    return tile


def factor(tile):
    row = lax.broadcasted_iota(jnp.int32, (8, 128), 0)
    lane = lax.broadcasted_iota(jnp.int32, (8, 128), 1)
    lower = jnp.zeros((8, 128), F32)
    upper = jnp.zeros((8, 128), F32)
    inverse = jnp.where(row == lane, 1.0, 0.0).astype(F32)
    for j in range(8):
        across = row_of(tile, j)
        down = column_of(tile, j)
        scale = 1.0 / jnp.sqrt(row_of(down, j))
        across = across * scale
        down = jnp.where(row >= j, down * scale, 0.0)
        lower = jnp.where(lane == j, down, lower)
        upper = jnp.where((row == j) & (lane >= j), across, upper)
        tile = tile - down * across
        pivot = row_of(inverse, j) * scale
        inverse = jnp.where(row == j, pivot, inverse - jnp.where(row > j, down, 0.0) * pivot)
    return lower, upper, inverse


def columns_of(tile):
    return [column_of(tile, k) for k in range(8)]


def apply(columns, block):
    total = columns[0] * row_of(block, 0)
    for k in range(1, 8):
        total = total + columns[k] * row_of(block, k)
    return total


def step_kernel(
    n_ray, n_cell, cells_all, rays_all,
    packet_hbm, high_hbm, low_hbm, u_hbm, v_prev_hbm, b_hbm,
    v_hbm, small_ref,
    packet_ref, u_ref, v_prev_ref, b_ref, v_ref, slots_in, part, pieces_in, slab_in, back_out, back_in, ray_gram, cell_gram, all_gram, high, low, w_slots,
    load_sem, send1, recv1, send2, recv2, send3, recv3, send4, recv4, send5, recv5, send6, recv6, send7, recv7,
):
    ray = lax.axis_index("ray")
    cell = lax.axis_index("cell")
    piece = pieces_in.shape[1]
    blocks = n_ray * piece

    early = [
        pltpu.make_async_copy(source, target, load_sem.at[2 + i])
        for i, (source, target) in enumerate(
            ((packet_hbm, packet_ref), (u_hbm, u_ref), (v_prev_hbm, v_prev_ref), (b_hbm, b_ref))
        )
    ]
    for load in early:
        load.start()
    loads = [
        pltpu.make_async_copy(high_hbm, high, load_sem.at[0]),
        pltpu.make_async_copy(low_hbm, low, load_sem.at[1]),
    ]
    for load in loads:
        load.start()

    barrier = pltpu.get_barrier_semaphore()

    each_peer(n_ray, lambda k: pl.semaphore_signal(barrier, inc=1, device_id={"ray": lax.rem(ray + k, n_ray)}, device_id_type=MESH))

    each_peer(n_cell, lambda k: pl.semaphore_signal(barrier, inc=1, device_id={"cell": lax.rem(cell + k, n_cell)}, device_id_type=MESH))

    pl.semaphore_wait(barrier, n_ray + n_cell - 2)

    def over(axis, me, n, source, target, send, recv):
        def copy(k):
            peer = lax.rem(me + k, n)
            return pltpu.make_async_remote_copy(
                src_ref=source(peer),
                dst_ref=target(me),
                send_sem=send.at[k - 1],
                recv_sem=recv.at[k - 1],
                device_id={axis: peer},
                device_id_type=MESH,
            )

        def wait_recv(k):
            origin = lax.rem(me + n - k, n)
            pltpu.make_async_remote_copy(
                src_ref=source(lax.rem(me + k, n)),
                dst_ref=target(origin),
                send_sem=send.at[k - 1],
                recv_sem=recv.at[k - 1],
                device_id={axis: lax.rem(me + k, n)},
                device_id_type=MESH,
            ).wait_recv()

        def receive():
            each_peer(n, wait_recv)

        def finish():
            each_peer(n, lambda k: copy(k).wait_send())

        return copy, receive, finish

    to_slab, from_slots, end1 = over(
        "cell", cell, n_cell, lambda peer: packet_ref.at[peer], lambda me: slots_in.at[me], send1, recv1
    )
    early[0].wait()
    each_peer(n_cell, lambda k: to_slab(k).start())
    for load in early[1:]:
        load.wait()
    slots_in[cell] = packet_ref[cell]
    from_slots()

    def index_tiles(p):
        tile = slots_in[p, CAP]
        return [row_of(tile, s) for s in range(CAP)]

    indices = [index_tiles(p) for p in range(n_cell)]

    def dense_block(b):
        number = jnp.full((8, 128), b, jnp.int32).astype(F32)
        total = jnp.zeros((8, 128), F32)
        for p in range(n_cell):
            for s in range(CAP):
                total = total + jnp.where(indices[p][s] == number, slots_in[p, s], 0.0)
        return total

    to_piece, from_pieces, end2 = over(
        "ray", ray, n_ray, lambda peer: part.at[peer], lambda me: pieces_in.at[me], send2, recv2
    )

    def send_piece(k):
        peer = lax.rem(ray + k, n_ray)
        for i in range(piece):
            part[peer, i] = dense_block(peer * piece + i)
        to_piece(k).start()

    each_peer(n_ray, send_piece)

    for i in range(piece):
        pieces_in[ray, i] = dense_block(ray * piece + i)

    b_columns = columns_of(b_ref[...])
    known = []
    for i in range(piece):
        at = pl.multiple_of((ray * piece + i) * 128, 128)
        known.append(apply(b_columns, v_prev_ref[:, pl.ds(at, 128)]))
    from_pieces()
    own = []
    for i in range(piece):
        total = pieces_in[0, i]
        for r in range(1, n_ray):
            total = total + pieces_in[r, i]
        own.append(total - known[i])
        slab_in[ray, i] = own[i]
    slab_in[ray, piece] = gram(own)

    to_ray, from_ray, end3 = over(
        "ray", ray, n_ray, lambda peer: slab_in.at[ray], lambda me: slab_in.at[me], send3, recv3
    )
    each_peer(n_ray, lambda k: to_ray(k).start())
    from_ray()

    slab_gram = slab_in[0, piece]
    for r in range(1, n_ray):
        slab_gram = slab_gram + slab_in[r, piece]

    def answer(p):
        wanted = index_tiles(p)
        found = [jnp.zeros((8, 128), F32) for s in range(CAP)]
        for b in range(blocks):
            block = slab_in[b // piece, b % piece]
            for s in range(CAP):
                found[s] = jnp.where(wanted[s] == float(b), block, found[s])
        return found

    to_cell, from_cell, end4 = over(
        "cell", cell, n_cell, lambda peer: back_out.at[peer], lambda me: back_in.at[me], send4, recv4
    )

    def send_answer(k):
        peer = lax.rem(cell + k, n_cell)
        found = answer(peer)
        for s in range(CAP):
            back_out[peer, s] = found[s]
        back_out[peer, CAP] = slab_gram
        to_cell(k).start()

    each_peer(n_cell, send_answer)

    found = answer(cell)
    for s in range(CAP):
        back_in[cell, s] = found[s]
    back_in[cell, CAP] = slab_gram
    for load in loads:
        load.wait()
    from_cell()

    whole_gram = back_in[0, CAP]
    for p in range(1, n_cell):
        whole_gram = whole_gram + back_in[p, CAP]
    for p in range(n_cell):
        for s in range(CAP):
            at = p * CAP + s
            w_slots[at // 2, :, (at % 2) * 128 : (at % 2 + 1) * 128] = back_in[p, s]
    across = (((1,), (1,)), ((), ()))

    def image_of(n):
        w_pair = split_rows(w_slots[n])
        both = lax.dot_general(w_pair, high[n], across, preferred_element_type=F32)
        rest = lax.dot_general(w_pair, low[n], across, preferred_element_type=F32)
        return both[:8] + (both[8:] + rest[:8])

    steps = high.shape[0]
    if steps <= UNROLL:
        image = image_of(0)
        for n in range(1, steps):
            image = image + image_of(n)
    else:
        image = lax.fori_loop(1, steps, lambda n, total: total + image_of(n), image_of(0))

    alpha, alpha_t, alpha_inverse = factor(whole_gram * (1.0 / cells_all))
    inverse_columns = columns_of(alpha_inverse)
    alpha_t_columns = columns_of(alpha_t)
    ray_blocks = u_ref.shape[1] // 128
    residual = []
    for i in range(ray_blocks):
        lanes = slice(i * 128, (i + 1) * 128)
        residual.append(apply(inverse_columns, image[:, lanes]) - apply(alpha_t_columns, u_ref[:, lanes]))
    everyone = n_ray * n_cell
    flat = ray * n_cell + cell
    own_gram = gram(residual)

    def gram_copy(k, back):
        peer = lax.rem(flat + k, everyone)
        slot = lax.rem(flat + everyone - k, everyone) if back else flat
        return pltpu.make_async_remote_copy(
            src_ref=all_gram.at[flat],
            dst_ref=all_gram.at[slot],
            send_sem=send7.at[k - 1],
            recv_sem=recv7.at[k - 1],
            device_id={"ray": lax.div(peer, n_cell), "cell": lax.rem(peer, n_cell)},
            device_id_type=MESH,
        )

    if everyone <= DIRECT:
        all_gram[flat] = own_gram
        for k in range(1, everyone):
            gram_copy(k, False).start()
    else:
        ray_gram[ray] = own_gram
        to_gram, from_gram, end5 = over(
            "ray", ray, n_ray, lambda peer: ray_gram.at[ray], lambda me: ray_gram.at[me], send5, recv5
        )
        each_peer(n_ray, lambda k: to_gram(k).start())

    small_ref[0] = alpha
    for i in range(ray_blocks):
        small_ref[2 + i] = residual[i]
    for b in range(blocks):
        v_ref[:, b * 128 : (b + 1) * 128] = apply(inverse_columns, slab_in[b // piece, b % piece])
    store = pltpu.make_async_copy(v_ref, v_hbm, load_sem.at[6])
    store.start()

    if everyone <= DIRECT:
        for k in range(1, everyone):
            gram_copy(k, True).wait_recv()
        total = all_gram[0]
        for d in range(1, everyone):
            total = total + all_gram[d]
    else:
        from_gram()
        total = ray_gram[0]
        for r in range(1, n_ray):
            total = total + ray_gram[r]
        cell_gram[cell] = total
        to_total, from_total, end6 = over(
            "cell", cell, n_cell, lambda peer: cell_gram.at[cell], lambda me: cell_gram.at[me], send6, recv6
        )
        each_peer(n_cell, lambda k: to_total(k).start())
        from_total()
        total = cell_gram[0]
        for p in range(1, n_cell):
            total = total + cell_gram[p]
    small_ref[1] = total * (1.0 / rays_all)
    store.wait()
    for end in (end1, end2, end3, end4):
        end()
    if everyone <= DIRECT:
        for k in range(1, everyone):
            gram_copy(k, False).wait_send()
    else:
        end5()
        end6()


def cholesky(tile, count=8):
    row = lax.broadcasted_iota(jnp.int32, (8, 128), 0)
    rest = [column_of(tile, k) for k in range(count)]
    lower, scales = [], []
    for j in range(count):
        scale = lax.rsqrt(row_of(rest[j], j))
        column = jnp.where(row >= j, rest[j] * scale, 0.0)
        lower.append(column)
        scales.append(scale)
        for k in range(j + 1, count):
            rest[k] = rest[k] - column * row_of(column, k)
    return lower, scales


def across_of(columns):
    lane = lax.broadcasted_iota(jnp.int32, (8, 128), 1)
    tile = jnp.zeros((8, 128), F32)
    for k, column in enumerate(columns):
        tile = jnp.where(lane == k, column, tile)
    return tile


def transposed(columns):
    row = lax.broadcasted_iota(jnp.int32, (8, 128), 0)
    turned = []
    for k in range(len(columns)):
        column = jnp.zeros((8, 128), F32)
        for i in range(k + 1):
            column = jnp.where(row == i, row_of(columns[i], k), column)
        turned.append(column)
    return turned


def solve(lower, scales, block):
    row = lax.broadcasted_iota(jnp.int32, (8, 128), 0)
    found = block
    for j, (column, scale) in enumerate(zip(lower, scales)):
        value = row_of(block, j) * scale
        found = jnp.where(row == j, value, found)
        block = block - column * value
    return found


def last_kernel(v_hbm, small_hbm, v_out, u_out, alpha_out, beta_out, v_ref, small, u_ref, alpha_ref, beta_ref, sems):
    load = pltpu.make_async_copy(small_hbm, small, sems.at[0])
    v_load = pltpu.make_async_copy(v_hbm, v_ref, sems.at[1])
    load.start()
    v_load.start()
    stores = [
        pltpu.make_async_copy(source, target, sems.at[2 + i])
        for i, (source, target) in enumerate(
            ((v_ref, v_out), (alpha_ref, alpha_out), (beta_ref, beta_out), (u_ref, u_out))
        )
    ]
    load.wait()
    alpha_ref[...] = small[0][:, :8]
    stores[1].start()
    v_load.wait()
    stores[0].start()
    lower, scales = cholesky(small[1])
    beta_ref[...] = across_of(lower)[:, :8]
    for i in range(small.shape[0] - 2):
        u_ref[:, i * 128 : (i + 1) * 128] = solve(lower, scales, small[2 + i])
    stores[2].start()
    stores[3].start()
    for store in stores:
        store.wait()


def flips_of(index, count):
    flips, bit = {}, 1
    while bit < count:
        flips[bit] = bit * (1 - 2 * lax.rem(lax.div(index, bit), 2))
        bit *= 2
    return flips


def flipped(index, flips, mask):
    for bit, step in flips.items():
        if mask & bit:
            index = index + step
    return index


def far_first(n_ray, n_cell):
    masks = [(2 * a, c) for a in range(n_ray // 2) for c in range(n_cell) if a or c]
    return sorted(masks, key=lambda m: -(2 * bin(m[0]).count("1") + m[1]))


def halves_of(value):
    high = value.astype(BF16)
    return high, (value - high.astype(F32)).astype(BF16)


def fused_kernel(
    n_ray, n_cell, cells_all, rays_all,
    group_hbm, slot_hbm, block_hbm, tiles_hbm, u_hbm, v_prev_hbm, b_hbm,
    v_hbm, small_ref,
    group_ref, slot_ref, block_ref, asked_ref, index_out, index_in, tiles, u_ref, v_prev_ref, b_ref,
    u_twice, spread, split, turned, sums, packet, recv, part, part_in, known, w_ref,
    back_out, back_in, gram_out, gram_in, w_slots, pair_gram, all_gram, v_ref,
    tile_sem, load_sem, send1, recv1, send2, recv2, send3, recv3, send4, recv4, send5, recv5, send6, recv6, send7, recv7,
):
    ray = lax.axis_index("ray")
    cell = lax.axis_index("cell")
    tile_count, tile_rays, width = tiles.shape
    slots = block_ref.shape[1]
    comps = u_ref.shape[0]
    sources = n_ray // 2 * n_cell
    blocks = w_ref.shape[0]
    steps, span = split.shape[0], split.shape[1]
    chunks = tile_sem.shape[0]
    per_chunk = tile_count // chunks
    per_step = steps // chunks
    quad = span // tile_rays

    small_loads = [
        pltpu.make_async_copy(source, target, load_sem.at[i])
        for i, (source, target) in enumerate(
            (
                (block_hbm, block_ref), (u_hbm, u_ref), (slot_hbm, slot_ref), (group_hbm, group_ref),
                (v_prev_hbm, v_prev_ref), (b_hbm, b_ref),
            )
        )
    ]

    def chunk(i):
        rows = pl.ds(i * per_chunk, per_chunk)
        return pltpu.make_async_copy(tiles_hbm.at[rows], tiles.at[rows], tile_sem.at[i])

    for load in small_loads[:4]:
        load.start()
    for i in range(chunks):
        chunk(i).start()
    for load in small_loads[4:]:
        load.start()

    ray_flips = flips_of(ray, n_ray)
    cell_flips = flips_of(cell, n_cell)
    masks = far_first(n_ray, n_cell)
    peers = [(flipped(ray, ray_flips, a), flipped(cell, cell_flips, c)) for a, c in masks]
    twin = ray + ray_flips[1]
    cell_masks = list(range(n_cell - 1, 0, -1))
    cell_peers = [flipped(cell, cell_flips, c) for c in cell_masks]

    def number_of(ray_at, cell_at):
        return lax.div(ray_at, 2) * n_cell + cell_at

    me = number_of(ray, cell)

    barrier = pltpu.get_barrier_semaphore()
    for r, c in peers + [(twin, cell)]:
        pl.semaphore_signal(barrier, inc=1, device_id={"ray": r, "cell": c}, device_id_type=MESH)

    def remote(source, target, send, recv_at, r, c):
        return pltpu.make_async_remote_copy(
            src_ref=source, dst_ref=target, send_sem=send, recv_sem=recv_at,
            device_id={"ray": r, "cell": c}, device_id_type=MESH,
        )

    small_loads[0].wait()
    lane = lax.broadcasted_iota(jnp.int32, (8, width), 1)
    for p in range(n_cell):
        index = jnp.zeros((1, width), jnp.int32)
        for s in range(CAP):
            index = jnp.where(lane[:1] == me * CAP + s, block_ref[0, p * CAP + s] + 1, index)
        index_out[p] = index
    index_in[me] = index_out[cell]

    pl.semaphore_wait(barrier, len(peers) + 1)
    indices = [
        remote(index_out.at[c], index_in.at[me], send2.at[i], recv2.at[i], r, c) for i, (r, c) in enumerate(peers)
    ]
    for copy in indices:
        copy.start()

    for load in small_loads[1:4]:
        load.wait()
    low = lane < tile_rays
    low_pair = lax.broadcasted_iota(jnp.int32, (2 * comps, width), 1) < tile_rays
    for q in range(u_ref.shape[1] // width):
        block = u_ref[:, q * width : (q + 1) * width]
        turn = pltpu.roll(block, tile_rays, 1)
        for half, both in enumerate((jnp.where(low, block, turn), jnp.where(low, turn, block))):
            high = both.astype(BF16).astype(F32)
            u_twice[2 * q + half, :comps] = high
            u_twice[2 * q + half, comps:] = both - high

    @pl.loop(0, chunks)
    def _(c):
        for q in range(per_chunk // 2):
            at = c * per_chunk + 2 * q
            value = jnp.where(low_pair, u_twice[group_ref[0, at]], u_twice[group_ref[0, at + 1]])
            where = jnp.where(low_pair, slot_ref[0, at], slot_ref[0, at + 1])
            for s in range(slots):
                spread[c, s * 2 * comps : (s + 1) * 2 * comps, q * width : (q + 1) * width] = jnp.where(
                    where == s, value, 0.0
                ).astype(BF16)

    for i in range(chunks):
        chunk(i).wait()
        value = tiles[i * per_chunk : (i + 1) * per_chunk].reshape(per_chunk * tile_rays, width)
        high, rest = halves_of(value)
        both = jnp.concatenate([high, rest], axis=1)
        split[i * per_step : (i + 1) * per_step] = both.reshape(per_step, span, 2 * width)
        product = jnp.dot(spread[i], both, preferred_element_type=F32)
        if i == 0:
            sums[...] = product
        else:
            sums[...] += product

    for s in range(slots):
        rows = sums[s * 2 * comps : (s + 1) * 2 * comps]
        rows = rows[:, :width] + rows[:, width:]
        packet[s // CAP, s % CAP * comps : (s % CAP + 1) * comps] = rows[:comps] + rows[comps:]
    recv[me] = packet[cell]

    first = [
        remote(packet.at[c], recv.at[me], send1.at[i], recv1.at[i], r, c) for i, (r, c) in enumerate(peers)
    ]
    for copy in first:
        copy.start()
    for load in small_loads[4:]:
        load.wait()
    b_columns = columns_of(b_ref[...])
    for b in range(blocks):
        known[b] = apply(b_columns, v_prev_ref[:, b * width : (b + 1) * width])

    @pl.loop(0, steps)
    def _(n):
        turned[n] = split[n].T

    for i, (r, c) in enumerate(peers):
        remote(index_out.at[c], index_in.at[number_of(r, c)], send2.at[i], recv2.at[i], r, c).wait_recv()
    ask_load = pltpu.make_async_copy(index_in, asked_ref, load_sem.at[6])
    ask_load.start()
    asked = jnp.sum(index_in[:, 0, :], axis=0, keepdims=True) - 1
    row = lax.broadcasted_iota(jnp.int32, (blocks, width), 0)
    pick = jnp.where(row == jnp.broadcast_to(asked, (blocks, width)), 1.0, 0.0)[:, : sources * CAP].astype(BF16)
    ask_load.wait()

    for i, (r, c) in enumerate(peers):
        remote(packet.at[c], recv.at[number_of(r, c)], send1.at[i], recv1.at[i], r, c).wait_recv()

    flat = recv.reshape(sources * CAP * comps, width)
    part_rows = part.reshape(blocks * comps, width)
    for r in range(comps):
        high, rest = halves_of(flat[pl.ds(r, sources * CAP, stride=comps), :])
        both = jnp.dot(pick, jnp.concatenate([high, rest], axis=1), preferred_element_type=F32)
        part_rows[pl.ds(r, blocks, stride=comps), :] = both[:, :width] + both[:, width:]

    swap = remote(part, part_in, send3.at[0], recv3.at[0], twin, cell)
    swap.start()
    swap.wait_recv()
    for b in range(blocks):
        w_ref[b] = part[b] + part_in[b] - known[b]

    answers = []
    for i, c in enumerate(cell_peers):
        for s in range(CAP):
            at = asked_ref[number_of(ray, c), 0, number_of(ray, c) * CAP + s]
            back_out[i, s] = w_ref[jnp.maximum(at - 1, 0)]
        answers.append(remote(back_out.at[i], back_in.at[cell], send4.at[i], recv4.at[i], ray, c))
        answers[i].start()
    for s in range(CAP):
        back_in[cell, s] = w_ref[jnp.maximum(block_ref[0, cell * CAP + s], 0)]

    slab_gram = gram([w_ref[b] for b in range(blocks)])
    gram_out[...] = slab_gram
    gram_in[cell] = slab_gram
    grams = [
        remote(gram_out, gram_in.at[cell], send5.at[i], recv5.at[i], ray, c) for i, c in enumerate(cell_peers)
    ]
    for copy in grams:
        copy.start()

    for i, c in enumerate(cell_peers):
        remote(back_out.at[i], back_in.at[c], send4.at[i], recv4.at[i], ray, c).wait_recv()
    for p in range(n_cell):
        for s in range(CAP):
            w_slots[p * CAP + s] = split_rows(back_in[p, s])

    groups = u_ref.shape[1] // tile_rays
    totals = [jnp.zeros((8, width), F32) for g in range(groups)]
    for n in range(steps):
        at = n * quad
        rows = jnp.concatenate([w_slots[slot_ref[0, at + j]] for j in range(quad)], axis=0)
        found = jnp.dot(jnp.concatenate([rows, rows], axis=1), turned[n], preferred_element_type=F32)
        for j in range(quad // 2):
            lanes = slice(j * width, (j + 1) * width)
            top = 2 * j * 2 * comps
            pair = jnp.where(
                low_pair, found[top : top + 2 * comps, lanes], found[top + 2 * comps : top + 4 * comps, lanes]
            )
            pair = pair[:comps] + pair[comps:]
            owner = jnp.where(low, group_ref[0, at + 2 * j], group_ref[0, at + 2 * j + 1])
            for g in range(groups):
                totals[g] = totals[g] + jnp.where(owner == g, pair, 0.0)

    for i, c in enumerate(cell_peers):
        remote(gram_out, gram_in.at[c], send5.at[i], recv5.at[i], ray, c).wait_recv()
    whole_gram = gram_in[0]
    for p in range(1, n_cell):
        whole_gram = whole_gram + gram_in[p]
    lower, scales = cholesky(whole_gram * (1.0 / cells_all))
    alpha_t_columns = transposed(lower)
    totals = [total + pltpu.roll(total, tile_rays, 1) for total in totals]
    ray_blocks = u_ref.shape[1] // width
    residual = []
    for i in range(ray_blocks):
        image = jnp.where(low, totals[2 * i], totals[2 * i + 1])
        lanes = slice(i * width, (i + 1) * width)
        residual.append(solve(lower, scales, image) - apply(alpha_t_columns, u_ref[:, lanes]))
    pair_gram[0] = gram(residual)
    pairs = remote(pair_gram.at[0], pair_gram.at[1], send6.at[0], recv6.at[0], twin, cell)
    pairs.start()
    small_ref[0] = across_of(lower)
    for i in range(ray_blocks):
        small_ref[2 + i] = residual[i]
    pairs.wait_recv()
    all_gram[me] = pair_gram[0] + pair_gram[1]
    last = [
        remote(all_gram.at[me], all_gram.at[me], send7.at[i], recv7.at[i], r, c) for i, (r, c) in enumerate(peers)
    ]
    for copy in last:
        copy.start()
    for b in range(blocks):
        v_ref[:, b * width : (b + 1) * width] = solve(lower, scales, w_ref[b])
    store = pltpu.make_async_copy(v_ref, v_hbm, load_sem.at[8])
    store.start()
    for i, (r, c) in enumerate(peers):
        remote(all_gram.at[me], all_gram.at[number_of(r, c)], send7.at[i], recv7.at[i], r, c).wait_recv()
    total = all_gram[0]
    for d in range(1, sources):
        total = total + all_gram[d]
    small_ref[1] = total * (1.0 / rays_all)
    store.wait()
    for copy in first + indices + [swap] + answers + grams + [pairs] + last:
        copy.wait_send()


def fused(n_ray, n_cell, ray_tiles, tile_group, tile_slot, slot_block, u_basis, v_prev, b_prev):
    tile_count, tile_rays, width = ray_tiles.shape
    comps, rays = u_basis.shape
    slots = slot_block.shape[1]
    blocks = v_prev.shape[1] // width
    sources = n_ray // 2 * n_cell
    steps = tile_count * tile_rays // (2 * width)
    vmem = pl.BlockSpec(memory_space=pltpu.VMEM)
    anywhere = pl.BlockSpec(memory_space=pl.ANY)
    tile = (comps, width)
    pair = slots * 2 * comps
    one = pltpu.SemaphoreType.DMA((1,))
    far = pltpu.SemaphoreType.DMA((sources - 1,))
    cells = pltpu.SemaphoreType.DMA((n_cell - 1,))
    return pl.pallas_call(
        functools.partial(fused_kernel, n_ray, n_cell, v_prev.shape[1] * n_cell, rays * n_ray * n_cell),
        out_shape=(
            jax.ShapeDtypeStruct(v_prev.shape, F32),
            jax.ShapeDtypeStruct((2 + rays // width,) + tile, F32),
        ),
        in_specs=[anywhere] * 7,
        out_specs=(anywhere, vmem),
        scratch_shapes=[
            pltpu.SMEM(tile_group.shape, jnp.int32),
            pltpu.SMEM(tile_slot.shape, jnp.int32),
            pltpu.SMEM(slot_block.shape, jnp.int32),
            pltpu.SMEM((sources, 1, width), jnp.int32),
            pltpu.VMEM((n_cell, 1, width), jnp.int32),
            pltpu.VMEM((sources, 1, width), jnp.int32),
            pltpu.VMEM(ray_tiles.shape, F32),
            pltpu.VMEM(u_basis.shape, F32),
            pltpu.VMEM(v_prev.shape, F32),
            pltpu.VMEM(b_prev.shape, F32),
            pltpu.VMEM((rays // tile_rays, 2 * comps, width), F32),
            pltpu.VMEM((CHUNKS, pair, tile_count // CHUNKS * tile_rays), BF16),
            pltpu.VMEM((steps, 2 * width, 2 * width), BF16),
            pltpu.VMEM((steps, 2 * width, 2 * width), BF16),
            pltpu.VMEM((pair, 2 * width), F32),
            pltpu.VMEM((n_cell, CAP * comps, width), F32),
            pltpu.VMEM((sources, CAP * comps, width), F32),
            pltpu.VMEM((blocks,) + tile, F32),
            pltpu.VMEM((blocks,) + tile, F32),
            pltpu.VMEM((blocks,) + tile, F32),
            pltpu.VMEM((blocks,) + tile, F32),
            pltpu.VMEM((n_cell - 1, CAP) + tile, F32),
            pltpu.VMEM((n_cell, CAP) + tile, F32),
            pltpu.VMEM(tile, F32),
            pltpu.VMEM((n_cell,) + tile, F32),
            pltpu.VMEM((slots, 2 * comps, width), BF16),
            pltpu.VMEM((2,) + tile, F32),
            pltpu.VMEM((sources,) + tile, F32),
            pltpu.VMEM(v_prev.shape, F32),
            pltpu.SemaphoreType.DMA((CHUNKS,)),
            pltpu.SemaphoreType.DMA((9,)),
            far, far, far, far, one, one, cells, cells, cells, cells, one, one, far, far,
        ],
        compiler_params=pltpu.CompilerParams(
            collective_id=0, has_side_effects=True, vmem_limit_bytes=56 << 20
        ),
    )(tile_group, tile_slot, slot_block, ray_tiles, u_basis, v_prev, b_prev)


def per_device(n_ray, n_cell, ray_tiles, tile_group, tile_slot, slot_block, u_basis, v_prev, b_prev):
    tile_count, tile_rays, width = ray_tiles.shape
    comps, rays = u_basis.shape
    slots = slot_block.shape[1]
    blocks = v_prev.shape[1] // width
    piece = blocks // n_ray
    vmem = pl.BlockSpec(memory_space=pltpu.VMEM)
    smem = pl.BlockSpec(memory_space=pltpu.SMEM)
    anywhere = pl.BlockSpec(memory_space=pl.ANY)
    tile = (comps, width)
    packets = (n_cell, CAP + 1) + tile
    limit = 56 << 20
    small_shape = (2 + rays // width,) + tile
    if n_ray * n_cell <= DIRECT:
        v_next, small = fused(n_ray, n_cell, ray_tiles, tile_group, tile_slot, slot_block, u_basis, v_prev, b_prev)
    else:
        packet, high, low = pl.pallas_call(
            local_kernel,
            out_shape=(
                jax.ShapeDtypeStruct(packets, F32),
                jax.ShapeDtypeStruct((slots // 2, rays, 2 * width), BF16),
                jax.ShapeDtypeStruct((slots // 2, rays, 2 * width), BF16),
            ),
            in_specs=[smem, smem, smem, anywhere, vmem],
            out_specs=(vmem, anywhere, anywhere),
            scratch_shapes=[
                pltpu.VMEM(ray_tiles.shape, F32),
                pltpu.VMEM((rays, slots * width), F32),
                pltpu.VMEM((slots // 2, rays, 2 * width), BF16),
                pltpu.VMEM((slots // 2, rays, 2 * width), BF16),
                pltpu.SemaphoreType.DMA((CHUNKS,)),
                pltpu.SemaphoreType.DMA((2, slots // 2)),
            ],
            compiler_params=pltpu.CompilerParams(vmem_limit_bytes=limit),
        )(tile_group, tile_slot, slot_block, ray_tiles, u_basis)

        ray_sem = pltpu.SemaphoreType.DMA((n_ray - 1,))
        direct = min(n_ray * n_cell, DIRECT)
        all_sem = pltpu.SemaphoreType.DMA((direct - 1,))
        cell_sem = pltpu.SemaphoreType.DMA((n_cell - 1,))
        v_next, small = pl.pallas_call(
            functools.partial(step_kernel, n_ray, n_cell, v_prev.shape[1] * n_cell, rays * n_ray * n_cell),
            out_shape=(jax.ShapeDtypeStruct(v_prev.shape, F32), jax.ShapeDtypeStruct(small_shape, F32)),
            in_specs=[anywhere] * 6,
            out_specs=(anywhere, vmem),
            scratch_shapes=[
                pltpu.VMEM(packets, F32),
                pltpu.VMEM(u_basis.shape, F32),
                pltpu.VMEM(v_prev.shape, F32),
                pltpu.VMEM(b_prev.shape, F32),
                pltpu.VMEM(v_prev.shape, F32),
                pltpu.VMEM(packets, F32),
                pltpu.VMEM((n_ray, piece) + tile, F32),
                pltpu.VMEM((n_ray, piece) + tile, F32),
                pltpu.VMEM((n_ray, piece + 1) + tile, F32),
                pltpu.VMEM(packets, F32),
                pltpu.VMEM(packets, F32),
                pltpu.VMEM((n_ray,) + tile, F32),
                pltpu.VMEM((n_cell,) + tile, F32),
                pltpu.VMEM((direct,) + tile, F32),
                pltpu.VMEM((slots // 2, rays, 2 * width), BF16),
                pltpu.VMEM((slots // 2, rays, 2 * width), BF16),
                pltpu.VMEM((slots // 2, comps, 2 * width), F32),
                pltpu.SemaphoreType.DMA((7,)),
                cell_sem, cell_sem, ray_sem, ray_sem, ray_sem, ray_sem,
                cell_sem, cell_sem, ray_sem, ray_sem, cell_sem, cell_sem, all_sem, all_sem,
            ],
            compiler_params=pltpu.CompilerParams(
                collective_id=0, has_side_effects=True, vmem_limit_bytes=limit
            ),
        )(packet, high, low, u_basis, v_prev, b_prev)
    return pl.pallas_call(
        last_kernel,
        out_shape=(
            jax.ShapeDtypeStruct(v_prev.shape, F32),
            jax.ShapeDtypeStruct(u_basis.shape, F32),
            jax.ShapeDtypeStruct((comps, comps), F32),
            jax.ShapeDtypeStruct((comps, comps), F32),
        ),
        in_specs=[anywhere, anywhere],
        out_specs=(anywhere, anywhere, anywhere, anywhere),
        scratch_shapes=[
            pltpu.VMEM(v_prev.shape, F32),
            pltpu.VMEM(small_shape, F32),
            pltpu.VMEM(u_basis.shape, F32),
            pltpu.VMEM((comps, comps), F32),
            pltpu.VMEM((comps, comps), F32),
            pltpu.SemaphoreType.DMA((6,)),
        ],
    )(v_next, small)


def solution(mesh):
    in_specs = (
        P(("ray", "cell"), None, None),
        P(("ray", "cell"), None),
        P(("ray", "cell"), None),
        P(("ray", "cell"), None),
        P(None, ("ray", "cell")),
        P(None, "cell"),
        P(),
    )
    out_specs = (P(None, "cell"), P(None, ("ray", "cell")), P(), P())
    return jax.shard_map(
        functools.partial(per_device, mesh.shape["ray"], mesh.shape["cell"]),
        mesh=mesh,
        in_specs=in_specs,
        out_specs=out_specs,
        check_vma=False,
    )
```

```python
import functools

import jax
import jax.numpy as jnp
from jax import lax
from jax.experimental import pallas as pl
from jax.experimental.pallas import tpu as pltpu
from jax.sharding import PartitionSpec as P

CAP = 4
GROUPS = 8
CHUNKS = 8
UNROLL = 8
DIRECT = 32
SWAPS = 2
ANNOUNCE = 4
BATCH = 4
MESH = pl.DeviceIdType.MESH
F32 = jnp.float32
BF16 = jnp.bfloat16


def split_rows(value):
    high = value.astype(BF16).astype(F32)
    return jnp.concatenate([high, value - high], axis=0).astype(BF16)


def local_kernel(group_ref, slot_ref, block_ref, tiles_hbm, u_ref, packet_ref, high_hbm, low_hbm, tiles, dense, high_ref, low_ref, sems, out_sems):
    tile_count, tile_rays, width = tiles.shape
    slots = block_ref.shape[1]
    per_chunk = tile_count // CHUNKS

    def chunk(i):
        rows = pl.ds(i * per_chunk, per_chunk)
        return pltpu.make_async_copy(tiles_hbm.at[rows], tiles.at[rows], sems.at[i])

    for i in range(CHUNKS):
        chunk(i).start()

    row = lax.broadcasted_iota(jnp.int32, (8, width), 0)
    for p in range(slots // CAP):
        index = jnp.full((8, width), -1, jnp.int32)
        for s in range(CAP):
            index = jnp.where(row == s, block_ref[0, p * CAP + s], index)
        packet_ref[p, CAP] = index.astype(F32)

    @pl.loop(0, slots)
    def _(s):
        dense[:, pl.ds(pl.multiple_of(s * width, width), width)] = jnp.zeros((dense.shape[0], width), F32)

    for i in range(CHUNKS):
        chunk(i).wait()

        @pl.loop(0, per_chunk // BATCH)
        def _(at):
            first = i * per_chunk + at * BATCH
            where = [(group_ref[0, first + n], slot_ref[0, first + n]) for n in range(BATCH)]
            values = [tiles[first + n] for n in range(BATCH)]
            for (group, slot), value in zip(where, values):
                rows = pl.ds(pl.multiple_of(group * tile_rays, tile_rays), tile_rays)
                columns = pl.ds(pl.multiple_of(slot * width, width), width)
                dense[rows, columns] += value

    u_pair = split_rows(u_ref[...])
    comps = u_ref.shape[0]
    span = 2 * width

    def stores(n):
        return [
            pltpu.make_async_copy(source.at[n], target.at[n], out_sems.at[at, n])
            for at, (source, target) in enumerate(((high_ref, high_hbm), (low_ref, low_hbm)))
        ]

    def product(n):
        columns = pl.ds(pl.multiple_of(n * span, span), span)
        block = dense[:, columns]
        high = block.astype(BF16)
        low = (block - high.astype(F32)).astype(BF16)
        high_ref[n] = high
        low_ref[n] = low
        for store in stores(n):
            store.start()
        both = jnp.dot(u_pair, high, preferred_element_type=F32)
        rest = jnp.dot(u_pair, low, preferred_element_type=F32)
        total = both[:comps] + (both[comps:] + rest[:comps])
        for half in range(2):
            s = 2 * n + half
            packet_ref[s // CAP, s % CAP] = total[:, half * width : (half + 1) * width]

    def finish(n):
        for store in stores(n):
            store.wait()

    each_peer(slots // 2, product, 0)
    each_peer(slots // 2, finish, 0)


def each_peer(n, body, first=1):
    if n <= UNROLL:
        for k in range(first, n):
            body(k)
    else:
        pl.loop(first, n)(body)


def row_of(tile, k):
    return jnp.broadcast_to(tile[k : k + 1, :], tile.shape)


def column_of(tile, k):
    return jnp.broadcast_to(tile[:, k : k + 1], (tile.shape[0], 128))


def gram(blocks):
    lane = lax.broadcasted_iota(jnp.int32, (8, 128), 1)
    tile = jnp.zeros((8, 128), F32)
    for j in range(8):
        products = blocks[0] * row_of(blocks[0], j)
        for block in blocks[1:]:
            products = products + block * row_of(block, j)
        tile = jnp.where(lane == j, jnp.sum(products, axis=1, keepdims=True), tile)
    return tile


def factor(tile):
    row = lax.broadcasted_iota(jnp.int32, (8, 128), 0)
    lane = lax.broadcasted_iota(jnp.int32, (8, 128), 1)
    lower = jnp.zeros((8, 128), F32)
    upper = jnp.zeros((8, 128), F32)
    inverse = jnp.where(row == lane, 1.0, 0.0).astype(F32)
    for j in range(8):
        across = row_of(tile, j)
        down = column_of(tile, j)
        scale = 1.0 / jnp.sqrt(row_of(down, j))
        across = across * scale
        down = jnp.where(row >= j, down * scale, 0.0)
        lower = jnp.where(lane == j, down, lower)
        upper = jnp.where((row == j) & (lane >= j), across, upper)
        tile = tile - down * across
        pivot = row_of(inverse, j) * scale
        inverse = jnp.where(row == j, pivot, inverse - jnp.where(row > j, down, 0.0) * pivot)
    return lower, upper, inverse


def columns_of(tile):
    return [column_of(tile, k) for k in range(8)]


def apply(columns, block):
    total = columns[0] * row_of(block, 0)
    for k in range(1, 8):
        total = total + columns[k] * row_of(block, k)
    return total


def step_kernel(
    n_ray, n_cell, cells_all, rays_all,
    packet_hbm, high_hbm, low_hbm, u_hbm, v_prev_hbm, b_hbm,
    v_hbm, small_ref,
    packet_ref, u_ref, v_prev_ref, b_ref, v_ref, slots_in, part, pieces_in, slab_in, back_out, back_in, ray_gram, cell_gram, all_gram, high, low, w_slots,
    load_sem, send1, recv1, send2, recv2, send3, recv3, send4, recv4, send5, recv5, send6, recv6, send7, recv7,
):
    ray = lax.axis_index("ray")
    cell = lax.axis_index("cell")
    piece = pieces_in.shape[1]
    blocks = n_ray * piece

    early = [
        pltpu.make_async_copy(source, target, load_sem.at[2 + i])
        for i, (source, target) in enumerate(
            ((packet_hbm, packet_ref), (u_hbm, u_ref), (v_prev_hbm, v_prev_ref), (b_hbm, b_ref))
        )
    ]
    for load in early:
        load.start()
    loads = [
        pltpu.make_async_copy(high_hbm, high, load_sem.at[0]),
        pltpu.make_async_copy(low_hbm, low, load_sem.at[1]),
    ]
    for load in loads:
        load.start()

    barrier = pltpu.get_barrier_semaphore()

    each_peer(n_ray, lambda k: pl.semaphore_signal(barrier, inc=1, device_id={"ray": lax.rem(ray + k, n_ray)}, device_id_type=MESH))

    each_peer(n_cell, lambda k: pl.semaphore_signal(barrier, inc=1, device_id={"cell": lax.rem(cell + k, n_cell)}, device_id_type=MESH))

    pl.semaphore_wait(barrier, n_ray + n_cell - 2)

    def over(axis, me, n, source, target, send, recv):
        def copy(k):
            peer = lax.rem(me + k, n)
            return pltpu.make_async_remote_copy(
                src_ref=source(peer),
                dst_ref=target(me),
                send_sem=send.at[k - 1],
                recv_sem=recv.at[k - 1],
                device_id={axis: peer},
                device_id_type=MESH,
            )

        def wait_recv(k):
            origin = lax.rem(me + n - k, n)
            pltpu.make_async_remote_copy(
                src_ref=source(lax.rem(me + k, n)),
                dst_ref=target(origin),
                send_sem=send.at[k - 1],
                recv_sem=recv.at[k - 1],
                device_id={axis: lax.rem(me + k, n)},
                device_id_type=MESH,
            ).wait_recv()

        def receive():
            each_peer(n, wait_recv)

        def finish():
            each_peer(n, lambda k: copy(k).wait_send())

        return copy, receive, finish

    to_slab, from_slots, end1 = over(
        "cell", cell, n_cell, lambda peer: packet_ref.at[peer], lambda me: slots_in.at[me], send1, recv1
    )
    early[0].wait()
    each_peer(n_cell, lambda k: to_slab(k).start())
    for load in early[1:]:
        load.wait()
    slots_in[cell] = packet_ref[cell]
    from_slots()

    def index_tiles(p):
        tile = slots_in[p, CAP]
        return [row_of(tile, s) for s in range(CAP)]

    indices = [index_tiles(p) for p in range(n_cell)]

    def dense_block(b):
        number = jnp.full((8, 128), b, jnp.int32).astype(F32)
        total = jnp.zeros((8, 128), F32)
        for p in range(n_cell):
            for s in range(CAP):
                total = total + jnp.where(indices[p][s] == number, slots_in[p, s], 0.0)
        return total

    to_piece, from_pieces, end2 = over(
        "ray", ray, n_ray, lambda peer: part.at[peer], lambda me: pieces_in.at[me], send2, recv2
    )

    def send_piece(k):
        peer = lax.rem(ray + k, n_ray)
        for i in range(piece):
            part[peer, i] = dense_block(peer * piece + i)
        to_piece(k).start()

    each_peer(n_ray, send_piece)

    for i in range(piece):
        pieces_in[ray, i] = dense_block(ray * piece + i)

    b_columns = columns_of(b_ref[...])
    known = []
    for i in range(piece):
        at = pl.multiple_of((ray * piece + i) * 128, 128)
        known.append(apply(b_columns, v_prev_ref[:, pl.ds(at, 128)]))
    from_pieces()
    own = []
    for i in range(piece):
        total = pieces_in[0, i]
        for r in range(1, n_ray):
            total = total + pieces_in[r, i]
        own.append(total - known[i])
        slab_in[ray, i] = own[i]
    slab_in[ray, piece] = gram(own)

    to_ray, from_ray, end3 = over(
        "ray", ray, n_ray, lambda peer: slab_in.at[ray], lambda me: slab_in.at[me], send3, recv3
    )
    each_peer(n_ray, lambda k: to_ray(k).start())
    from_ray()

    slab_gram = slab_in[0, piece]
    for r in range(1, n_ray):
        slab_gram = slab_gram + slab_in[r, piece]

    def answer(p):
        wanted = index_tiles(p)
        found = [jnp.zeros((8, 128), F32) for s in range(CAP)]
        for b in range(blocks):
            block = slab_in[b // piece, b % piece]
            for s in range(CAP):
                found[s] = jnp.where(wanted[s] == float(b), block, found[s])
        return found

    to_cell, from_cell, end4 = over(
        "cell", cell, n_cell, lambda peer: back_out.at[peer], lambda me: back_in.at[me], send4, recv4
    )

    def send_answer(k):
        peer = lax.rem(cell + k, n_cell)
        found = answer(peer)
        for s in range(CAP):
            back_out[peer, s] = found[s]
        back_out[peer, CAP] = slab_gram
        to_cell(k).start()

    each_peer(n_cell, send_answer)

    found = answer(cell)
    for s in range(CAP):
        back_in[cell, s] = found[s]
    back_in[cell, CAP] = slab_gram
    for load in loads:
        load.wait()
    from_cell()

    whole_gram = back_in[0, CAP]
    for p in range(1, n_cell):
        whole_gram = whole_gram + back_in[p, CAP]
    for p in range(n_cell):
        for s in range(CAP):
            at = p * CAP + s
            w_slots[at // 2, :, (at % 2) * 128 : (at % 2 + 1) * 128] = back_in[p, s]
    across = (((1,), (1,)), ((), ()))

    def image_of(n):
        w_pair = split_rows(w_slots[n])
        both = lax.dot_general(w_pair, high[n], across, preferred_element_type=F32)
        rest = lax.dot_general(w_pair, low[n], across, preferred_element_type=F32)
        return both[:8] + (both[8:] + rest[:8])

    steps = high.shape[0]
    if steps <= UNROLL:
        image = image_of(0)
        for n in range(1, steps):
            image = image + image_of(n)
    else:
        image = lax.fori_loop(1, steps, lambda n, total: total + image_of(n), image_of(0))

    alpha, alpha_t, alpha_inverse = factor(whole_gram * (1.0 / cells_all))
    inverse_columns = columns_of(alpha_inverse)
    alpha_t_columns = columns_of(alpha_t)
    ray_blocks = u_ref.shape[1] // 128
    residual = []
    for i in range(ray_blocks):
        lanes = slice(i * 128, (i + 1) * 128)
        residual.append(apply(inverse_columns, image[:, lanes]) - apply(alpha_t_columns, u_ref[:, lanes]))
    everyone = n_ray * n_cell
    flat = ray * n_cell + cell
    own_gram = gram(residual)

    def gram_copy(k, back):
        peer = lax.rem(flat + k, everyone)
        slot = lax.rem(flat + everyone - k, everyone) if back else flat
        return pltpu.make_async_remote_copy(
            src_ref=all_gram.at[flat],
            dst_ref=all_gram.at[slot],
            send_sem=send7.at[k - 1],
            recv_sem=recv7.at[k - 1],
            device_id={"ray": lax.div(peer, n_cell), "cell": lax.rem(peer, n_cell)},
            device_id_type=MESH,
        )

    if everyone <= DIRECT:
        all_gram[flat] = own_gram
        for k in range(1, everyone):
            gram_copy(k, False).start()
    else:
        ray_gram[ray] = own_gram
        to_gram, from_gram, end5 = over(
            "ray", ray, n_ray, lambda peer: ray_gram.at[ray], lambda me: ray_gram.at[me], send5, recv5
        )
        each_peer(n_ray, lambda k: to_gram(k).start())

    small_ref[0] = alpha
    for i in range(ray_blocks):
        small_ref[2 + i] = residual[i]
    for b in range(blocks):
        v_ref[:, b * 128 : (b + 1) * 128] = apply(inverse_columns, slab_in[b // piece, b % piece])
    store = pltpu.make_async_copy(v_ref, v_hbm, load_sem.at[6])
    store.start()

    if everyone <= DIRECT:
        for k in range(1, everyone):
            gram_copy(k, True).wait_recv()
        total = all_gram[0]
        for d in range(1, everyone):
            total = total + all_gram[d]
    else:
        from_gram()
        total = ray_gram[0]
        for r in range(1, n_ray):
            total = total + ray_gram[r]
        cell_gram[cell] = total
        to_total, from_total, end6 = over(
            "cell", cell, n_cell, lambda peer: cell_gram.at[cell], lambda me: cell_gram.at[me], send6, recv6
        )
        each_peer(n_cell, lambda k: to_total(k).start())
        from_total()
        total = cell_gram[0]
        for p in range(1, n_cell):
            total = total + cell_gram[p]
    small_ref[1] = total * (1.0 / rays_all)
    store.wait()
    for end in (end1, end2, end3, end4):
        end()
    if everyone <= DIRECT:
        for k in range(1, everyone):
            gram_copy(k, False).wait_send()
    else:
        end5()
        end6()


def cholesky(tile, count=8):
    row = lax.broadcasted_iota(jnp.int32, (8, 128), 0)
    rest = [column_of(tile, k) for k in range(count)]
    lower, scales = [], []
    for j in range(count):
        scale = lax.rsqrt(row_of(rest[j], j))
        column = jnp.where(row >= j, rest[j] * scale, 0.0)
        lower.append(column)
        scales.append(scale)
        for k in range(j + 1, count):
            rest[k] = rest[k] - column * row_of(column, k)
    return lower, scales


def across_of(columns):
    lane = lax.broadcasted_iota(jnp.int32, (8, 128), 1)
    tile = jnp.zeros((8, 128), F32)
    for k, column in enumerate(columns):
        tile = jnp.where(lane == k, column, tile)
    return tile


def transposed(columns):
    row = lax.broadcasted_iota(jnp.int32, (8, 128), 0)
    turned = []
    for k in range(len(columns)):
        column = jnp.zeros((8, 128), F32)
        for i in range(k + 1):
            column = jnp.where(row == i, row_of(columns[i], k), column)
        turned.append(column)
    return turned


def solve(lower, scales, block):
    row = lax.broadcasted_iota(jnp.int32, (8, 128), 0)
    found = block
    for j, (column, scale) in enumerate(zip(lower, scales)):
        value = row_of(block, j) * scale
        found = jnp.where(row == j, value, found)
        block = block - column * value
    return found


def last_kernel(v_hbm, small_hbm, v_out, u_out, alpha_out, beta_out, v_ref, small, u_ref, alpha_ref, beta_ref, sems):
    load = pltpu.make_async_copy(small_hbm, small, sems.at[0])
    v_load = pltpu.make_async_copy(v_hbm, v_ref, sems.at[1])
    load.start()
    v_load.start()
    stores = [
        pltpu.make_async_copy(source, target, sems.at[2 + i])
        for i, (source, target) in enumerate(
            ((v_ref, v_out), (alpha_ref, alpha_out), (beta_ref, beta_out), (u_ref, u_out))
        )
    ]
    load.wait()
    alpha_ref[...] = small[0][:, :8]
    stores[1].start()
    v_load.wait()
    stores[0].start()
    lower, scales = cholesky(small[1])
    beta_ref[...] = across_of(lower)[:, :8]
    for i in range(small.shape[0] - 2):
        u_ref[:, i * 128 : (i + 1) * 128] = solve(lower, scales, small[2 + i])
    stores[2].start()
    stores[3].start()
    for store in stores:
        store.wait()


def flips_of(index, count):
    flips, bit = {}, 1
    while bit < count:
        flips[bit] = bit * (1 - 2 * lax.rem(lax.div(index, bit), 2))
        bit *= 2
    return flips


def flipped(index, flips, mask):
    for bit, step in flips.items():
        if mask & bit:
            index = index + step
    return index


def far_first(n_ray, n_cell):
    masks = [(2 * a, c) for a in range(n_ray // 2) for c in range(n_cell) if a or c]
    return sorted(masks, key=lambda m: -(2 * bin(m[0]).count("1") + m[1]))


def halves_of(value):
    high = value.astype(BF16)
    return high, (value - high.astype(F32)).astype(BF16)


def fused_kernel(
    n_ray, n_cell, cells_all, rays_all,
    group_hbm, slot_hbm, block_hbm, tiles_hbm, u_hbm, v_prev_hbm, b_hbm,
    v_hbm, small_ref,
    group_ref, slot_ref, block_ref, asked_ref, index_out, index_in, tiles, u_ref, v_prev_ref, b_ref,
    u_left, u_right, gather, products, split, turned, pick, packet, recv, part, part_in, known, w_ref,
    back_out, back_in, gram_out, gram_in, w_slots, pair_gram, all_gram, v_ref,
    tile_sem, load_sem, send1, recv1, send2, recv2, send3, recv3, send4, recv4, send5, recv5, send6, recv6, send7, recv7,
):
    ray = lax.axis_index("ray")
    cell = lax.axis_index("cell")
    tile_count, tile_rays, width = tiles.shape
    slots = block_ref.shape[1]
    comps = u_ref.shape[0]
    sources = n_ray // 2 * n_cell
    blocks = w_ref.shape[0]
    steps, span = split.shape[0], split.shape[1]
    chunks = tile_sem.shape[0]
    per_chunk = tile_count // chunks
    per_step = steps // chunks
    quad = span // tile_rays

    small_loads = [
        pltpu.make_async_copy(source, target, load_sem.at[i])
        for i, (source, target) in enumerate(
            (
                (block_hbm, block_ref), (u_hbm, u_ref), (slot_hbm, slot_ref), (group_hbm, group_ref),
                (v_prev_hbm, v_prev_ref), (b_hbm, b_ref),
            )
        )
    ]

    def chunk(i):
        rows = pl.ds(i * per_chunk, per_chunk)
        return pltpu.make_async_copy(tiles_hbm.at[rows], tiles.at[rows], tile_sem.at[i])

    for load in small_loads[:4]:
        load.start()
    for i in range(chunks):
        chunk(i).start()
    for load in small_loads[4:]:
        load.start()

    ray_flips = flips_of(ray, n_ray)
    cell_flips = flips_of(cell, n_cell)
    masks = far_first(n_ray, n_cell)
    peers = [(flipped(ray, ray_flips, a), flipped(cell, cell_flips, c)) for a, c in masks]
    twin = ray + ray_flips[1]
    cell_masks = list(range(n_cell - 1, 0, -1))
    cell_peers = [flipped(cell, cell_flips, c) for c in cell_masks]

    def number_of(ray_at, cell_at):
        return lax.div(ray_at, 2) * n_cell + cell_at

    me = number_of(ray, cell)

    barrier = pltpu.get_barrier_semaphore()
    for r, c in peers + [(twin, cell)]:
        pl.semaphore_signal(barrier, inc=1, device_id={"ray": r, "cell": c}, device_id_type=MESH)

    def remote(source, target, send, recv_at, r, c):
        return pltpu.make_async_remote_copy(
            src_ref=source, dst_ref=target, send_sem=send, recv_sem=recv_at,
            device_id={"ray": r, "cell": c}, device_id_type=MESH,
        )

    small_loads[0].wait()
    lane = lax.broadcasted_iota(jnp.int32, (8, width), 1)
    bands = sources * CAP * comps // width
    band = lax.broadcasted_iota(jnp.int32, (bands, width), 0)
    place = band * width + lax.broadcasted_iota(jnp.int32, (bands, width), 1) - me * CAP * comps
    for p in range(n_cell):
        index = jnp.zeros((bands, width), jnp.int32)
        for s in range(CAP):
            b = block_ref[0, p * CAP + s]
            first_row = jnp.where(b < 0, -comps - 1, (b - s) * comps + 1)
            inside = (place >= s * comps) & (place < (s + 1) * comps)
            index = jnp.where(inside, jnp.maximum(place + first_row, 0), index)
        index_out[p] = index
    index_in[me] = index_out[cell]

    def announce():
        pl.semaphore_wait(barrier, len(peers) + 1)
        for copy in indices:
            copy.start()

    indices = [
        remote(index_out.at[c], index_in.at[me], send2.at[i], recv2.at[i], r, c) for i, (r, c) in enumerate(peers)
    ]

    for load in small_loads[1:4]:
        load.wait()
    low = lane < tile_rays
    low_pair = lax.broadcasted_iota(jnp.int32, (2 * comps, width), 1) < tile_rays
    for q in range(u_ref.shape[1] // width):
        block = u_ref[:, q * width : (q + 1) * width]
        turn = pltpu.roll(block, tile_rays, 1)
        for half, (left, right) in enumerate(((block, turn), (turn, block))):
            u_left[2 * q + half] = split_rows(jnp.where(low, left, 0.0))
            u_right[2 * q + half] = split_rows(jnp.where(low, 0.0, right))

    per_band = width // comps
    lane_tile = lax.div(lane, comps)
    slot_row = lax.broadcasted_iota(jnp.int32, (slots * comps, width), 0)
    offset = lax.rem(lane, comps)
    for q in range(tile_count // per_band):
        owner = jnp.zeros((8, width), jnp.int32)
        for t in range(per_band):
            owner = jnp.where(lane_tile == t, slot_ref[0, q * per_band + t], owner)
        owner = jnp.broadcast_to((owner * comps + offset)[:1], slot_row.shape)
        gather[:, q * width : (q + 1) * width] = jnp.where(slot_row == owner, 1.0, 0.0).astype(BF16)

    nothing = jnp.zeros((2 * quad // 2 * comps, width), BF16)
    for i in range(chunks):
        if i == ANNOUNCE:
            announce()
        chunk(i).wait()
        for n in range(i * per_step, (i + 1) * per_step):
            value = tiles[n * quad : (n + 1) * quad].reshape(span, width)
            high, rest = halves_of(value)
            both = jnp.concatenate([high, rest], axis=1)
            split[n] = both
            columns = []
            for h in range(2):
                at = n * quad + 2 * h
                own = jnp.concatenate([u_left[group_ref[0, at]], u_right[group_ref[0, at + 1]]], axis=0)
                columns.append(jnp.concatenate([own, nothing] if h == 0 else [nothing, own], axis=0))
            product = jnp.dot(jnp.concatenate(columns, axis=1), both, preferred_element_type=F32)
            product = (product[:, :width] + product[:, width:]).reshape(quad, 2 * comps, width)
            product = (product[:, :comps] + product[:, comps:]).reshape(quad * comps, width)
            high, rest = halves_of(product)
            products[n * quad * comps : (n + 1) * quad * comps] = jnp.concatenate([high, rest], axis=1)

    slot_sums = jnp.dot(gather[...], products[...], preferred_element_type=F32)
    packet[...] = (slot_sums[:, :width] + slot_sums[:, width:]).reshape(packet.shape)
    recv[me] = packet[cell]

    if ANNOUNCE >= chunks:
        announce()
    first = [
        remote(packet.at[c], recv.at[me], send1.at[i], recv1.at[i], r, c) for i, (r, c) in enumerate(peers)
    ]
    for copy in first:
        copy.start()
    for load in small_loads[4:]:
        load.wait()
    b_columns = columns_of(b_ref[...])
    for b in range(blocks):
        known[b] = apply(b_columns, v_prev_ref[:, b * width : (b + 1) * width])

    @pl.loop(0, steps)
    def _(n):
        turned[n] = split[n].T

    for i, (r, c) in enumerate(peers):
        remote(index_out.at[c], index_in.at[number_of(r, c)], send2.at[i], recv2.at[i], r, c).wait_recv()
    ask_load = pltpu.make_async_copy(index_in, asked_ref, load_sem.at[6])
    ask_load.start()
    asked = index_in[0]
    for d in range(1, sources):
        asked = asked + index_in[d]
    row = lax.broadcasted_iota(jnp.int32, (blocks * comps, width), 0) + 1
    for q in range(bands):
        wanted = jnp.broadcast_to(asked[q : q + 1], (blocks * comps, width))
        pick[:, q * width : (q + 1) * width] = jnp.where(row == wanted, 1.0, 0.0).astype(BF16)
    ask_load.wait()

    for i, (r, c) in enumerate(peers):
        remote(packet.at[c], recv.at[number_of(r, c)], send1.at[i], recv1.at[i], r, c).wait_recv()

    received = recv[...].reshape(sources * CAP * comps, width)
    high, rest = halves_of(received)
    both = jnp.concatenate([high, rest], axis=1)
    swaps = []
    section = blocks // SWAPS
    for i in range(SWAPS):
        rows = pl.ds(i * section, section)
        added = jnp.dot(pick[i * section * comps : (i + 1) * section * comps], both, preferred_element_type=F32)
        part[rows] = (added[:, :width] + added[:, width:]).reshape(section, comps, width)
        swaps.append(remote(part.at[rows], part_in.at[rows], send3.at[i], recv3.at[i], twin, cell))
        swaps[i].start()
    for copy in swaps:
        copy.wait_recv()
    for b in range(blocks):
        w_ref[b] = part[b] + part_in[b] - known[b]

    answers = []
    for i, c in enumerate(cell_peers):
        for s in range(CAP):
            at = (number_of(ray, c) * CAP + s) * comps
            row_at = asked_ref[number_of(ray, c), lax.div(at, width), lax.rem(at, width)]
            back_out[i, s] = w_ref[lax.div(jnp.maximum(row_at - 1, 0), comps)]
        answers.append(remote(back_out.at[i], back_in.at[cell], send4.at[i], recv4.at[i], ray, c))
        answers[i].start()
    for s in range(CAP):
        back_in[cell, s] = w_ref[jnp.maximum(block_ref[0, cell * CAP + s], 0)]

    slab_gram = gram([w_ref[b] for b in range(blocks)])
    gram_out[...] = slab_gram
    gram_in[cell] = slab_gram
    grams = [
        remote(gram_out, gram_in.at[cell], send5.at[i], recv5.at[i], ray, c) for i, c in enumerate(cell_peers)
    ]
    for copy in grams:
        copy.start()

    for i, c in enumerate(cell_peers):
        remote(back_out.at[i], back_in.at[c], send4.at[i], recv4.at[i], ray, c).wait_recv()
    for p in range(n_cell):
        for s in range(CAP):
            w_slots[p * CAP + s] = split_rows(back_in[p, s])

    groups = u_ref.shape[1] // tile_rays
    totals = [jnp.zeros((8, width), F32) for g in range(groups)]
    for n in range(steps):
        at = n * quad
        rows = jnp.concatenate([w_slots[slot_ref[0, at + j]] for j in range(quad)], axis=0)
        found = jnp.dot(jnp.concatenate([rows, rows], axis=1), turned[n], preferred_element_type=F32)
        for j in range(quad // 2):
            lanes = slice(j * width, (j + 1) * width)
            top = 2 * j * 2 * comps
            pair = jnp.where(
                low_pair, found[top : top + 2 * comps, lanes], found[top + 2 * comps : top + 4 * comps, lanes]
            )
            pair = pair[:comps] + pair[comps:]
            owner = jnp.where(low, group_ref[0, at + 2 * j], group_ref[0, at + 2 * j + 1])
            for g in range(groups):
                totals[g] = totals[g] + jnp.where(owner == g, pair, 0.0)

    for i, c in enumerate(cell_peers):
        remote(gram_out, gram_in.at[c], send5.at[i], recv5.at[i], ray, c).wait_recv()
    whole_gram = gram_in[0]
    for p in range(1, n_cell):
        whole_gram = whole_gram + gram_in[p]
    lower, scales = cholesky(whole_gram * (1.0 / cells_all))
    alpha_t_columns = transposed(lower)
    totals = [total + pltpu.roll(total, tile_rays, 1) for total in totals]
    ray_blocks = u_ref.shape[1] // width
    residual = []
    for i in range(ray_blocks):
        image = jnp.where(low, totals[2 * i], totals[2 * i + 1])
        lanes = slice(i * width, (i + 1) * width)
        residual.append(solve(lower, scales, image) - apply(alpha_t_columns, u_ref[:, lanes]))
    pair_gram[0] = gram(residual)
    pairs = remote(pair_gram.at[0], pair_gram.at[1], send6.at[0], recv6.at[0], twin, cell)
    pairs.start()
    small_ref[0] = across_of(lower)
    for i in range(ray_blocks):
        small_ref[2 + i] = residual[i]
    pairs.wait_recv()
    all_gram[me] = pair_gram[0] + pair_gram[1]
    last = [
        remote(all_gram.at[me], all_gram.at[me], send7.at[i], recv7.at[i], r, c) for i, (r, c) in enumerate(peers)
    ]
    for copy in last:
        copy.start()
    for b in range(blocks):
        v_ref[:, b * width : (b + 1) * width] = solve(lower, scales, w_ref[b])
    store = pltpu.make_async_copy(v_ref, v_hbm, load_sem.at[8])
    store.start()
    for i, (r, c) in enumerate(peers):
        remote(all_gram.at[me], all_gram.at[number_of(r, c)], send7.at[i], recv7.at[i], r, c).wait_recv()
    total = all_gram[0]
    for d in range(1, sources):
        total = total + all_gram[d]
    small_ref[1] = total * (1.0 / rays_all)
    store.wait()
    for copy in first + indices + swaps + answers + grams + [pairs] + last:
        copy.wait_send()


def fused(n_ray, n_cell, ray_tiles, tile_group, tile_slot, slot_block, u_basis, v_prev, b_prev):
    tile_count, tile_rays, width = ray_tiles.shape
    comps, rays = u_basis.shape
    slots = slot_block.shape[1]
    blocks = v_prev.shape[1] // width
    sources = n_ray // 2 * n_cell
    bands = sources * CAP * comps // width
    steps = tile_count * tile_rays // (2 * width)
    vmem = pl.BlockSpec(memory_space=pltpu.VMEM)
    anywhere = pl.BlockSpec(memory_space=pl.ANY)
    tile = (comps, width)
    one = pltpu.SemaphoreType.DMA((1,))
    parts = pltpu.SemaphoreType.DMA((SWAPS,))
    far = pltpu.SemaphoreType.DMA((sources - 1,))
    cells = pltpu.SemaphoreType.DMA((n_cell - 1,))
    return pl.pallas_call(
        functools.partial(fused_kernel, n_ray, n_cell, v_prev.shape[1] * n_cell, rays * n_ray * n_cell),
        out_shape=(
            jax.ShapeDtypeStruct(v_prev.shape, F32),
            jax.ShapeDtypeStruct((2 + rays // width,) + tile, F32),
        ),
        in_specs=[anywhere] * 7,
        out_specs=(anywhere, vmem),
        scratch_shapes=[
            pltpu.SMEM(tile_group.shape, jnp.int32),
            pltpu.SMEM(tile_slot.shape, jnp.int32),
            pltpu.SMEM(slot_block.shape, jnp.int32),
            pltpu.SMEM((sources, bands, width), jnp.int32),
            pltpu.VMEM((n_cell, bands, width), jnp.int32),
            pltpu.VMEM((sources, bands, width), jnp.int32),
            pltpu.VMEM(ray_tiles.shape, F32),
            pltpu.VMEM(u_basis.shape, F32),
            pltpu.VMEM(v_prev.shape, F32),
            pltpu.VMEM(b_prev.shape, F32),
            pltpu.VMEM((rays // tile_rays, 2 * comps, width), BF16),
            pltpu.VMEM((rays // tile_rays, 2 * comps, width), BF16),
            pltpu.VMEM((slots * comps, tile_count * comps), BF16),
            pltpu.VMEM((tile_count * comps, 2 * width), BF16),
            pltpu.VMEM((steps, 2 * width, 2 * width), BF16),
            pltpu.VMEM((steps, 2 * width, 2 * width), BF16),
            pltpu.VMEM((blocks * comps, sources * CAP * comps), BF16),
            pltpu.VMEM((n_cell, CAP * comps, width), F32),
            pltpu.VMEM((sources, CAP * comps, width), F32),
            pltpu.VMEM((blocks,) + tile, F32),
            pltpu.VMEM((blocks,) + tile, F32),
            pltpu.VMEM((blocks,) + tile, F32),
            pltpu.VMEM((blocks,) + tile, F32),
            pltpu.VMEM((n_cell - 1, CAP) + tile, F32),
            pltpu.VMEM((n_cell, CAP) + tile, F32),
            pltpu.VMEM(tile, F32),
            pltpu.VMEM((n_cell,) + tile, F32),
            pltpu.VMEM((slots, 2 * comps, width), BF16),
            pltpu.VMEM((2,) + tile, F32),
            pltpu.VMEM((sources,) + tile, F32),
            pltpu.VMEM(v_prev.shape, F32),
            pltpu.SemaphoreType.DMA((CHUNKS,)),
            pltpu.SemaphoreType.DMA((9,)),
            far, far, far, far, parts, parts, cells, cells, cells, cells, one, one, far, far,
        ],
        compiler_params=pltpu.CompilerParams(
            collective_id=0, has_side_effects=True, vmem_limit_bytes=56 << 20
        ),
    )(tile_group, tile_slot, slot_block, ray_tiles, u_basis, v_prev, b_prev)


def per_device(n_ray, n_cell, ray_tiles, tile_group, tile_slot, slot_block, u_basis, v_prev, b_prev):
    tile_count, tile_rays, width = ray_tiles.shape
    comps, rays = u_basis.shape
    slots = slot_block.shape[1]
    blocks = v_prev.shape[1] // width
    piece = blocks // n_ray
    vmem = pl.BlockSpec(memory_space=pltpu.VMEM)
    smem = pl.BlockSpec(memory_space=pltpu.SMEM)
    anywhere = pl.BlockSpec(memory_space=pl.ANY)
    tile = (comps, width)
    packets = (n_cell, CAP + 1) + tile
    limit = 56 << 20
    small_shape = (2 + rays // width,) + tile
    if n_ray * n_cell <= DIRECT:
        v_next, small = fused(n_ray, n_cell, ray_tiles, tile_group, tile_slot, slot_block, u_basis, v_prev, b_prev)
    else:
        packet, high, low = pl.pallas_call(
            local_kernel,
            out_shape=(
                jax.ShapeDtypeStruct(packets, F32),
                jax.ShapeDtypeStruct((slots // 2, rays, 2 * width), BF16),
                jax.ShapeDtypeStruct((slots // 2, rays, 2 * width), BF16),
            ),
            in_specs=[smem, smem, smem, anywhere, vmem],
            out_specs=(vmem, anywhere, anywhere),
            scratch_shapes=[
                pltpu.VMEM(ray_tiles.shape, F32),
                pltpu.VMEM((rays, slots * width), F32),
                pltpu.VMEM((slots // 2, rays, 2 * width), BF16),
                pltpu.VMEM((slots // 2, rays, 2 * width), BF16),
                pltpu.SemaphoreType.DMA((CHUNKS,)),
                pltpu.SemaphoreType.DMA((2, slots // 2)),
            ],
            compiler_params=pltpu.CompilerParams(vmem_limit_bytes=limit),
        )(tile_group, tile_slot, slot_block, ray_tiles, u_basis)

        ray_sem = pltpu.SemaphoreType.DMA((n_ray - 1,))
        direct = min(n_ray * n_cell, DIRECT)
        all_sem = pltpu.SemaphoreType.DMA((direct - 1,))
        cell_sem = pltpu.SemaphoreType.DMA((n_cell - 1,))
        v_next, small = pl.pallas_call(
            functools.partial(step_kernel, n_ray, n_cell, v_prev.shape[1] * n_cell, rays * n_ray * n_cell),
            out_shape=(jax.ShapeDtypeStruct(v_prev.shape, F32), jax.ShapeDtypeStruct(small_shape, F32)),
            in_specs=[anywhere] * 6,
            out_specs=(anywhere, vmem),
            scratch_shapes=[
                pltpu.VMEM(packets, F32),
                pltpu.VMEM(u_basis.shape, F32),
                pltpu.VMEM(v_prev.shape, F32),
                pltpu.VMEM(b_prev.shape, F32),
                pltpu.VMEM(v_prev.shape, F32),
                pltpu.VMEM(packets, F32),
                pltpu.VMEM((n_ray, piece) + tile, F32),
                pltpu.VMEM((n_ray, piece) + tile, F32),
                pltpu.VMEM((n_ray, piece + 1) + tile, F32),
                pltpu.VMEM(packets, F32),
                pltpu.VMEM(packets, F32),
                pltpu.VMEM((n_ray,) + tile, F32),
                pltpu.VMEM((n_cell,) + tile, F32),
                pltpu.VMEM((direct,) + tile, F32),
                pltpu.VMEM((slots // 2, rays, 2 * width), BF16),
                pltpu.VMEM((slots // 2, rays, 2 * width), BF16),
                pltpu.VMEM((slots // 2, comps, 2 * width), F32),
                pltpu.SemaphoreType.DMA((7,)),
                cell_sem, cell_sem, ray_sem, ray_sem, ray_sem, ray_sem,
                cell_sem, cell_sem, ray_sem, ray_sem, cell_sem, cell_sem, all_sem, all_sem,
            ],
            compiler_params=pltpu.CompilerParams(
                collective_id=0, has_side_effects=True, vmem_limit_bytes=limit
            ),
        )(packet, high, low, u_basis, v_prev, b_prev)
    return pl.pallas_call(
        last_kernel,
        out_shape=(
            jax.ShapeDtypeStruct(v_prev.shape, F32),
            jax.ShapeDtypeStruct(u_basis.shape, F32),
            jax.ShapeDtypeStruct((comps, comps), F32),
            jax.ShapeDtypeStruct((comps, comps), F32),
        ),
        in_specs=[anywhere, anywhere],
        out_specs=(anywhere, anywhere, anywhere, anywhere),
        scratch_shapes=[
            pltpu.VMEM(v_prev.shape, F32),
            pltpu.VMEM(small_shape, F32),
            pltpu.VMEM(u_basis.shape, F32),
            pltpu.VMEM((comps, comps), F32),
            pltpu.VMEM((comps, comps), F32),
            pltpu.SemaphoreType.DMA((6,)),
        ],
    )(v_next, small)


def solution(mesh):
    in_specs = (
        P(("ray", "cell"), None, None),
        P(("ray", "cell"), None),
        P(("ray", "cell"), None),
        P(("ray", "cell"), None),
        P(None, ("ray", "cell")),
        P(None, "cell"),
        P(),
    )
    out_specs = (P(None, "cell"), P(None, ("ray", "cell")), P(), P())
    return jax.shard_map(
        functools.partial(per_device, mesh.shape["ray"], mesh.shape["cell"]),
        mesh=mesh,
        in_specs=in_specs,
        out_specs=out_specs,
        check_vma=False,
    )
```

```python
import functools

import jax
import jax.numpy as jnp
from jax import lax
from jax.experimental import pallas as pl
from jax.experimental.pallas import tpu as pltpu
from jax.sharding import PartitionSpec as P

CAP = 4
GROUPS = 8
CHUNKS = 3
UNROLL = 8
DIRECT = 32
SWAPS = 1
ORDER = 1
ANNOUNCE = 2
BATCH = 4
MESH = pl.DeviceIdType.MESH
F32 = jnp.float32
BF16 = jnp.bfloat16


def split_rows(value):
    high = value.astype(BF16).astype(F32)
    return jnp.concatenate([high, value - high], axis=0).astype(BF16)


def local_kernel(group_ref, slot_ref, block_ref, tiles_hbm, u_ref, packet_ref, high_hbm, low_hbm, tiles, dense, high_ref, low_ref, sems, out_sems):
    tile_count, tile_rays, width = tiles.shape
    slots = block_ref.shape[1]
    per_chunk = tile_count // CHUNKS

    def chunk(i):
        rows = pl.ds(i * per_chunk, per_chunk)
        return pltpu.make_async_copy(tiles_hbm.at[rows], tiles.at[rows], sems.at[i])

    for i in range(CHUNKS):
        chunk(i).start()

    row = lax.broadcasted_iota(jnp.int32, (8, width), 0)
    for p in range(slots // CAP):
        index = jnp.full((8, width), -1, jnp.int32)
        for s in range(CAP):
            index = jnp.where(row == s, block_ref[0, p * CAP + s], index)
        packet_ref[p, CAP] = index.astype(F32)

    @pl.loop(0, slots)
    def _(s):
        dense[:, pl.ds(pl.multiple_of(s * width, width), width)] = jnp.zeros((dense.shape[0], width), F32)

    for i in range(CHUNKS):
        chunk(i).wait()

        @pl.loop(0, per_chunk // BATCH)
        def _(at):
            first = i * per_chunk + at * BATCH
            where = [(group_ref[0, first + n], slot_ref[0, first + n]) for n in range(BATCH)]
            values = [tiles[first + n] for n in range(BATCH)]
            for (group, slot), value in zip(where, values):
                rows = pl.ds(pl.multiple_of(group * tile_rays, tile_rays), tile_rays)
                columns = pl.ds(pl.multiple_of(slot * width, width), width)
                dense[rows, columns] += value

    u_pair = split_rows(u_ref[...])
    comps = u_ref.shape[0]
    span = 2 * width

    def stores(n):
        return [
            pltpu.make_async_copy(source.at[n], target.at[n], out_sems.at[at, n])
            for at, (source, target) in enumerate(((high_ref, high_hbm), (low_ref, low_hbm)))
        ]

    def product(n):
        columns = pl.ds(pl.multiple_of(n * span, span), span)
        block = dense[:, columns]
        high = block.astype(BF16)
        low = (block - high.astype(F32)).astype(BF16)
        high_ref[n] = high
        low_ref[n] = low
        for store in stores(n):
            store.start()
        both = jnp.dot(u_pair, high, preferred_element_type=F32)
        rest = jnp.dot(u_pair, low, preferred_element_type=F32)
        total = both[:comps] + (both[comps:] + rest[:comps])
        for half in range(2):
            s = 2 * n + half
            packet_ref[s // CAP, s % CAP] = total[:, half * width : (half + 1) * width]

    def finish(n):
        for store in stores(n):
            store.wait()

    each_peer(slots // 2, product, 0)
    each_peer(slots // 2, finish, 0)


def each_peer(n, body, first=1):
    if n <= UNROLL:
        for k in range(first, n):
            body(k)
    else:
        pl.loop(first, n)(body)


def row_of(tile, k):
    return jnp.broadcast_to(tile[k : k + 1, :], tile.shape)


def column_of(tile, k):
    return jnp.broadcast_to(tile[:, k : k + 1], (tile.shape[0], 128))


def gram(blocks):
    lane = lax.broadcasted_iota(jnp.int32, (8, 128), 1)
    tile = jnp.zeros((8, 128), F32)
    for j in range(8):
        products = blocks[0] * row_of(blocks[0], j)
        for block in blocks[1:]:
            products = products + block * row_of(block, j)
        tile = jnp.where(lane == j, jnp.sum(products, axis=1, keepdims=True), tile)
    return tile


def factor(tile):
    row = lax.broadcasted_iota(jnp.int32, (8, 128), 0)
    lane = lax.broadcasted_iota(jnp.int32, (8, 128), 1)
    lower = jnp.zeros((8, 128), F32)
    upper = jnp.zeros((8, 128), F32)
    inverse = jnp.where(row == lane, 1.0, 0.0).astype(F32)
    for j in range(8):
        across = row_of(tile, j)
        down = column_of(tile, j)
        scale = 1.0 / jnp.sqrt(row_of(down, j))
        across = across * scale
        down = jnp.where(row >= j, down * scale, 0.0)
        lower = jnp.where(lane == j, down, lower)
        upper = jnp.where((row == j) & (lane >= j), across, upper)
        tile = tile - down * across
        pivot = row_of(inverse, j) * scale
        inverse = jnp.where(row == j, pivot, inverse - jnp.where(row > j, down, 0.0) * pivot)
    return lower, upper, inverse


def columns_of(tile):
    return [column_of(tile, k) for k in range(8)]


def apply(columns, block):
    total = columns[0] * row_of(block, 0)
    for k in range(1, 8):
        total = total + columns[k] * row_of(block, k)
    return total


def step_kernel(
    n_ray, n_cell, cells_all, rays_all,
    packet_hbm, high_hbm, low_hbm, u_hbm, v_prev_hbm, b_hbm,
    v_hbm, small_ref,
    packet_ref, u_ref, v_prev_ref, b_ref, v_ref, slots_in, part, pieces_in, slab_in, back_out, back_in, ray_gram, cell_gram, all_gram, high, low, w_slots,
    load_sem, send1, recv1, send2, recv2, send3, recv3, send4, recv4, send5, recv5, send6, recv6, send7, recv7,
):
    ray = lax.axis_index("ray")
    cell = lax.axis_index("cell")
    piece = pieces_in.shape[1]
    blocks = n_ray * piece

    early = [
        pltpu.make_async_copy(source, target, load_sem.at[2 + i])
        for i, (source, target) in enumerate(
            ((packet_hbm, packet_ref), (u_hbm, u_ref), (v_prev_hbm, v_prev_ref), (b_hbm, b_ref))
        )
    ]
    for load in early:
        load.start()
    loads = [
        pltpu.make_async_copy(high_hbm, high, load_sem.at[0]),
        pltpu.make_async_copy(low_hbm, low, load_sem.at[1]),
    ]
    for load in loads:
        load.start()

    barrier = pltpu.get_barrier_semaphore()

    each_peer(n_ray, lambda k: pl.semaphore_signal(barrier, inc=1, device_id={"ray": lax.rem(ray + k, n_ray)}, device_id_type=MESH))

    each_peer(n_cell, lambda k: pl.semaphore_signal(barrier, inc=1, device_id={"cell": lax.rem(cell + k, n_cell)}, device_id_type=MESH))

    pl.semaphore_wait(barrier, n_ray + n_cell - 2)

    def over(axis, me, n, source, target, send, recv):
        def copy(k):
            peer = lax.rem(me + k, n)
            return pltpu.make_async_remote_copy(
                src_ref=source(peer),
                dst_ref=target(me),
                send_sem=send.at[k - 1],
                recv_sem=recv.at[k - 1],
                device_id={axis: peer},
                device_id_type=MESH,
            )

        def wait_recv(k):
            origin = lax.rem(me + n - k, n)
            pltpu.make_async_remote_copy(
                src_ref=source(lax.rem(me + k, n)),
                dst_ref=target(origin),
                send_sem=send.at[k - 1],
                recv_sem=recv.at[k - 1],
                device_id={axis: lax.rem(me + k, n)},
                device_id_type=MESH,
            ).wait_recv()

        def receive():
            each_peer(n, wait_recv)

        def finish():
            each_peer(n, lambda k: copy(k).wait_send())

        return copy, receive, finish

    to_slab, from_slots, end1 = over(
        "cell", cell, n_cell, lambda peer: packet_ref.at[peer], lambda me: slots_in.at[me], send1, recv1
    )
    early[0].wait()
    each_peer(n_cell, lambda k: to_slab(k).start())
    for load in early[1:]:
        load.wait()
    slots_in[cell] = packet_ref[cell]
    from_slots()

    def index_tiles(p):
        tile = slots_in[p, CAP]
        return [row_of(tile, s) for s in range(CAP)]

    indices = [index_tiles(p) for p in range(n_cell)]

    def dense_block(b):
        number = jnp.full((8, 128), b, jnp.int32).astype(F32)
        total = jnp.zeros((8, 128), F32)
        for p in range(n_cell):
            for s in range(CAP):
                total = total + jnp.where(indices[p][s] == number, slots_in[p, s], 0.0)
        return total

    to_piece, from_pieces, end2 = over(
        "ray", ray, n_ray, lambda peer: part.at[peer], lambda me: pieces_in.at[me], send2, recv2
    )

    def send_piece(k):
        peer = lax.rem(ray + k, n_ray)
        for i in range(piece):
            part[peer, i] = dense_block(peer * piece + i)
        to_piece(k).start()

    each_peer(n_ray, send_piece)

    for i in range(piece):
        pieces_in[ray, i] = dense_block(ray * piece + i)

    b_columns = columns_of(b_ref[...])
    known = []
    for i in range(piece):
        at = pl.multiple_of((ray * piece + i) * 128, 128)
        known.append(apply(b_columns, v_prev_ref[:, pl.ds(at, 128)]))
    from_pieces()
    own = []
    for i in range(piece):
        total = pieces_in[0, i]
        for r in range(1, n_ray):
            total = total + pieces_in[r, i]
        own.append(total - known[i])
        slab_in[ray, i] = own[i]
    slab_in[ray, piece] = gram(own)

    to_ray, from_ray, end3 = over(
        "ray", ray, n_ray, lambda peer: slab_in.at[ray], lambda me: slab_in.at[me], send3, recv3
    )
    each_peer(n_ray, lambda k: to_ray(k).start())
    from_ray()

    slab_gram = slab_in[0, piece]
    for r in range(1, n_ray):
        slab_gram = slab_gram + slab_in[r, piece]

    def answer(p):
        wanted = index_tiles(p)
        found = [jnp.zeros((8, 128), F32) for s in range(CAP)]
        for b in range(blocks):
            block = slab_in[b // piece, b % piece]
            for s in range(CAP):
                found[s] = jnp.where(wanted[s] == float(b), block, found[s])
        return found

    to_cell, from_cell, end4 = over(
        "cell", cell, n_cell, lambda peer: back_out.at[peer], lambda me: back_in.at[me], send4, recv4
    )

    def send_answer(k):
        peer = lax.rem(cell + k, n_cell)
        found = answer(peer)
        for s in range(CAP):
            back_out[peer, s] = found[s]
        back_out[peer, CAP] = slab_gram
        to_cell(k).start()

    each_peer(n_cell, send_answer)

    found = answer(cell)
    for s in range(CAP):
        back_in[cell, s] = found[s]
    back_in[cell, CAP] = slab_gram
    for load in loads:
        load.wait()
    from_cell()

    whole_gram = back_in[0, CAP]
    for p in range(1, n_cell):
        whole_gram = whole_gram + back_in[p, CAP]
    for p in range(n_cell):
        for s in range(CAP):
            at = p * CAP + s
            w_slots[at // 2, :, (at % 2) * 128 : (at % 2 + 1) * 128] = back_in[p, s]
    across = (((1,), (1,)), ((), ()))

    def image_of(n):
        w_pair = split_rows(w_slots[n])
        both = lax.dot_general(w_pair, high[n], across, preferred_element_type=F32)
        rest = lax.dot_general(w_pair, low[n], across, preferred_element_type=F32)
        return both[:8] + (both[8:] + rest[:8])

    steps = high.shape[0]
    if steps <= UNROLL:
        image = image_of(0)
        for n in range(1, steps):
            image = image + image_of(n)
    else:
        image = lax.fori_loop(1, steps, lambda n, total: total + image_of(n), image_of(0))

    alpha, alpha_t, alpha_inverse = factor(whole_gram * (1.0 / cells_all))
    inverse_columns = columns_of(alpha_inverse)
    alpha_t_columns = columns_of(alpha_t)
    ray_blocks = u_ref.shape[1] // 128
    residual = []
    for i in range(ray_blocks):
        lanes = slice(i * 128, (i + 1) * 128)
        residual.append(apply(inverse_columns, image[:, lanes]) - apply(alpha_t_columns, u_ref[:, lanes]))
    everyone = n_ray * n_cell
    flat = ray * n_cell + cell
    own_gram = gram(residual)

    def gram_copy(k, back):
        peer = lax.rem(flat + k, everyone)
        slot = lax.rem(flat + everyone - k, everyone) if back else flat
        return pltpu.make_async_remote_copy(
            src_ref=all_gram.at[flat],
            dst_ref=all_gram.at[slot],
            send_sem=send7.at[k - 1],
            recv_sem=recv7.at[k - 1],
            device_id={"ray": lax.div(peer, n_cell), "cell": lax.rem(peer, n_cell)},
            device_id_type=MESH,
        )

    if everyone <= DIRECT:
        all_gram[flat] = own_gram
        for k in range(1, everyone):
            gram_copy(k, False).start()
    else:
        ray_gram[ray] = own_gram
        to_gram, from_gram, end5 = over(
            "ray", ray, n_ray, lambda peer: ray_gram.at[ray], lambda me: ray_gram.at[me], send5, recv5
        )
        each_peer(n_ray, lambda k: to_gram(k).start())

    small_ref[0] = alpha
    for i in range(ray_blocks):
        small_ref[2 + i] = residual[i]
    for b in range(blocks):
        v_ref[:, b * 128 : (b + 1) * 128] = apply(inverse_columns, slab_in[b // piece, b % piece])
    store = pltpu.make_async_copy(v_ref, v_hbm, load_sem.at[6])
    store.start()

    if everyone <= DIRECT:
        for k in range(1, everyone):
            gram_copy(k, True).wait_recv()
        total = all_gram[0]
        for d in range(1, everyone):
            total = total + all_gram[d]
    else:
        from_gram()
        total = ray_gram[0]
        for r in range(1, n_ray):
            total = total + ray_gram[r]
        cell_gram[cell] = total
        to_total, from_total, end6 = over(
            "cell", cell, n_cell, lambda peer: cell_gram.at[cell], lambda me: cell_gram.at[me], send6, recv6
        )
        each_peer(n_cell, lambda k: to_total(k).start())
        from_total()
        total = cell_gram[0]
        for p in range(1, n_cell):
            total = total + cell_gram[p]
    small_ref[1] = total * (1.0 / rays_all)
    store.wait()
    for end in (end1, end2, end3, end4):
        end()
    if everyone <= DIRECT:
        for k in range(1, everyone):
            gram_copy(k, False).wait_send()
    else:
        end5()
        end6()


def cholesky(tile, count=8):
    row = lax.broadcasted_iota(jnp.int32, (8, 128), 0)
    rest = [column_of(tile, k) for k in range(count)]
    lower, scales = [], []
    for j in range(count):
        scale = lax.rsqrt(row_of(rest[j], j))
        column = jnp.where(row >= j, rest[j] * scale, 0.0)
        lower.append(column)
        scales.append(scale)
        for k in range(j + 1, count):
            rest[k] = rest[k] - column * row_of(column, k)
    return lower, scales


def across_of(columns):
    lane = lax.broadcasted_iota(jnp.int32, (8, 128), 1)
    tile = jnp.zeros((8, 128), F32)
    for k, column in enumerate(columns):
        tile = jnp.where(lane == k, column, tile)
    return tile


def transposed(columns):
    row = lax.broadcasted_iota(jnp.int32, (8, 128), 0)
    turned = []
    for k in range(len(columns)):
        column = jnp.zeros((8, 128), F32)
        for i in range(k + 1):
            column = jnp.where(row == i, row_of(columns[i], k), column)
        turned.append(column)
    return turned


def solve(lower, scales, block):
    row = lax.broadcasted_iota(jnp.int32, (8, 128), 0)
    found = block
    for j, (column, scale) in enumerate(zip(lower, scales)):
        value = row_of(block, j) * scale
        found = jnp.where(row == j, value, found)
        block = block - column * value
    return found


def last_kernel(v_hbm, small_hbm, v_out, u_out, alpha_out, beta_out, v_ref, small, u_ref, alpha_ref, beta_ref, sems):
    load = pltpu.make_async_copy(small_hbm, small, sems.at[0])
    v_load = pltpu.make_async_copy(v_hbm, v_ref, sems.at[1])
    load.start()
    v_load.start()
    stores = [
        pltpu.make_async_copy(source, target, sems.at[2 + i])
        for i, (source, target) in enumerate(
            ((v_ref, v_out), (alpha_ref, alpha_out), (beta_ref, beta_out), (u_ref, u_out))
        )
    ]
    load.wait()
    alpha_ref[...] = small[0][:, :8]
    stores[1].start()
    v_load.wait()
    stores[0].start()
    lower, scales = cholesky(small[1])
    beta_ref[...] = across_of(lower)[:, :8]
    for i in range(small.shape[0] - 2):
        u_ref[:, i * 128 : (i + 1) * 128] = solve(lower, scales, small[2 + i])
    stores[2].start()
    stores[3].start()
    for store in stores:
        store.wait()


def flips_of(index, count):
    flips, bit = {}, 1
    while bit < count:
        flips[bit] = bit * (1 - 2 * lax.rem(lax.div(index, bit), 2))
        bit *= 2
    return flips


def flipped(index, flips, mask):
    for bit, step in flips.items():
        if mask & bit:
            index = index + step
    return index


def far_first(n_ray, n_cell):
    masks = [(2 * a, c) for a in range(n_ray // 2) for c in range(n_cell) if a or c]
    return sorted(masks, key=lambda m: -(8 * (m[1] >= 2) + 2 * bin(m[0]).count("1") + m[1]))


def halves_of(value):
    high = value.astype(BF16)
    return high, (value - high.astype(F32)).astype(BF16)


def fused_kernel(
    n_ray, n_cell, cells_all, rays_all,
    group_hbm, slot_hbm, block_hbm, tiles_hbm, u_hbm, v_prev_hbm, b_hbm,
    v_hbm, small_ref,
    group_ref, slot_ref, block_ref, asked_ref, index_out, index_in, tiles, u_ref, v_prev_ref, b_ref,
    u_left, u_right, gather, products, split, turned, pick, packet, recv, part, part_in, known, w_ref,
    back_out, back_in, gram_out, gram_in, w_slots, pair_gram, all_gram, v_ref,
    tile_sem, load_sem, send1, recv1, send2, recv2, send3, recv3, send4, recv4, send5, recv5, send6, recv6, send7, recv7,
):
    ray = lax.axis_index("ray")
    cell = lax.axis_index("cell")
    tile_count, tile_rays, width = tiles.shape
    slots = block_ref.shape[1]
    comps = u_ref.shape[0]
    sources = n_ray // 2 * n_cell
    blocks = w_ref.shape[0]
    steps, span = split.shape[0], split.shape[1]
    chunks = tile_sem.shape[0]
    per_chunk = tile_count // chunks
    per_step = steps // chunks
    quad = span // tile_rays

    small_loads = [
        pltpu.make_async_copy(source, target, load_sem.at[i])
        for i, (source, target) in enumerate(
            (
                (block_hbm, block_ref), (u_hbm, u_ref), (slot_hbm, slot_ref), (group_hbm, group_ref),
                (v_prev_hbm, v_prev_ref), (b_hbm, b_ref),
            )
        )
    ]

    def chunk(i):
        rows = pl.ds(i * per_chunk, per_chunk)
        return pltpu.make_async_copy(tiles_hbm.at[rows], tiles.at[rows], tile_sem.at[i])

    for load in small_loads[:4]:
        load.start()
    for i in range(chunks):
        chunk(i).start()
    for load in small_loads[4:]:
        load.start()

    ray_flips = flips_of(ray, n_ray)
    cell_flips = flips_of(cell, n_cell)
    masks = far_first(n_ray, n_cell)
    peers = [(flipped(ray, ray_flips, a), flipped(cell, cell_flips, c)) for a, c in masks]
    twin = ray + ray_flips[1]
    cell_masks = list(range(n_cell - 1, 0, -1))
    cell_peers = [flipped(cell, cell_flips, c) for c in cell_masks]

    def number_of(ray_at, cell_at):
        return lax.div(ray_at, 2) * n_cell + cell_at

    me = number_of(ray, cell)

    barrier = pltpu.get_barrier_semaphore()
    for r, c in peers + [(twin, cell)]:
        pl.semaphore_signal(barrier, inc=1, device_id={"ray": r, "cell": c}, device_id_type=MESH)

    def remote(source, target, send, recv_at, r, c):
        return pltpu.make_async_remote_copy(
            src_ref=source, dst_ref=target, send_sem=send, recv_sem=recv_at,
            device_id={"ray": r, "cell": c}, device_id_type=MESH,
        )

    small_loads[0].wait()
    lane = lax.broadcasted_iota(jnp.int32, (8, width), 1)
    bands = sources * CAP * comps // width
    band = lax.broadcasted_iota(jnp.int32, (bands, width), 0)
    place = band * width + lax.broadcasted_iota(jnp.int32, (bands, width), 1) - me * CAP * comps
    for p in range(n_cell):
        index = jnp.zeros((bands, width), jnp.int32)
        for s in range(CAP):
            b = block_ref[0, p * CAP + s]
            first_row = jnp.where(b < 0, -comps - 1, (b - s) * comps + 1)
            inside = (place >= s * comps) & (place < (s + 1) * comps)
            index = jnp.where(inside, jnp.maximum(place + first_row, 0), index)
        index_out[p] = index
    index_in[me] = index_out[cell]

    def announce():
        pl.semaphore_wait(barrier, len(peers) + 1)
        for copy in indices:
            copy.start()

    indices = [
        remote(index_out.at[c], index_in.at[me], send2.at[i], recv2.at[i], r, c) for i, (r, c) in enumerate(peers)
    ]

    for load in small_loads[1:4]:
        load.wait()
    low = lane < tile_rays
    low_pair = lax.broadcasted_iota(jnp.int32, (2 * comps, width), 1) < tile_rays
    for q in range(u_ref.shape[1] // width):
        block = u_ref[:, q * width : (q + 1) * width]
        turn = pltpu.roll(block, tile_rays, 1)
        for half, (left, right) in enumerate(((block, turn), (turn, block))):
            u_left[2 * q + half] = split_rows(jnp.where(low, left, 0.0))
            u_right[2 * q + half] = split_rows(jnp.where(low, 0.0, right))

    per_band = width // comps
    lane_tile = lax.div(lane, comps)
    slot_row = lax.broadcasted_iota(jnp.int32, (slots * comps, width), 0)
    offset = lax.rem(lane, comps)
    for q in range(tile_count // per_band):
        owner = jnp.zeros((8, width), jnp.int32)
        for t in range(per_band):
            owner = jnp.where(lane_tile == t, slot_ref[0, q * per_band + t], owner)
        owner = jnp.broadcast_to((owner * comps + offset)[:1], slot_row.shape)
        gather[:, q * width : (q + 1) * width] = jnp.where(slot_row == owner, 1.0, 0.0).astype(BF16)

    nothing = jnp.zeros((2 * quad // 2 * comps, width), BF16)
    for i in range(chunks):
        if i == ANNOUNCE:
            announce()
        chunk(i).wait()
        for n in range(i * per_step, (i + 1) * per_step):
            value = tiles[n * quad : (n + 1) * quad].reshape(span, width)
            high, rest = halves_of(value)
            both = jnp.concatenate([high, rest], axis=1)
            split[n] = both
            columns = []
            for h in range(2):
                at = n * quad + 2 * h
                own = jnp.concatenate([u_left[group_ref[0, at]], u_right[group_ref[0, at + 1]]], axis=0)
                columns.append(jnp.concatenate([own, nothing] if h == 0 else [nothing, own], axis=0))
            product = jnp.dot(jnp.concatenate(columns, axis=1), both, preferred_element_type=F32)
            product = (product[:, :width] + product[:, width:]).reshape(quad, 2 * comps, width)
            product = (product[:, :comps] + product[:, comps:]).reshape(quad * comps, width)
            high, rest = halves_of(product)
            products[n * quad * comps : (n + 1) * quad * comps] = jnp.concatenate([high, rest], axis=1)

    slot_sums = jnp.dot(gather[...], products[...], preferred_element_type=F32)
    packet[...] = (slot_sums[:, :width] + slot_sums[:, width:]).reshape(packet.shape)
    recv[me] = packet[cell]

    if ANNOUNCE >= chunks:
        announce()
    half = n_cell // 2
    passed = [(a, c) for a, c in masks if c >= half and bin(a).count("1") == 1]
    sent = [i for i, mask in enumerate(masks) if mask not in passed]
    sent.sort(key=lambda i: (masks[i][1] < half, ORDER * bin(masks[i][0]).count("1") - masks[i][1]))
    first = [remote(packet.at[peers[i][1]], recv.at[me], send1.at[i], recv1.at[i], *peers[i]) for i in sent]
    for copy in first:
        copy.start()

    def pass_on(mask, c):
        i = masks.index(mask)
        source = recv.at[number_of(ray, c)]
        return remote(source, source, send1.at[i], recv1.at[i], flipped(ray, ray_flips, mask[0]), cell)

    arrived = [i for i in sent if masks[i][0] == 0 and masks[i][1] >= half]
    for i in arrived[::-1]:
        r, c = peers[i]
        remote(packet.at[c], recv.at[number_of(r, c)], send1.at[i], recv1.at[i], r, c).wait_recv()
        for mask in passed:
            if mask[1] == masks[i][1]:
                copy = pass_on(mask, c)
                copy.start()
                first.append(copy)

    for load in small_loads[4:]:
        load.wait()
    b_columns = columns_of(b_ref[...])
    for b in range(blocks):
        known[b] = apply(b_columns, v_prev_ref[:, b * width : (b + 1) * width])

    @pl.loop(0, steps)
    def _(n):
        turned[n] = split[n].T

    for i, (r, c) in enumerate(peers):
        remote(index_out.at[c], index_in.at[number_of(r, c)], send2.at[i], recv2.at[i], r, c).wait_recv()
    ask_load = pltpu.make_async_copy(index_in, asked_ref, load_sem.at[6])
    ask_load.start()
    asked = index_in[0]
    for d in range(1, sources):
        asked = asked + index_in[d]
    row = lax.broadcasted_iota(jnp.int32, (blocks * comps, width), 0) + 1
    for q in range(bands):
        wanted = jnp.broadcast_to(asked[q : q + 1], (blocks * comps, width))
        pick[:, q * width : (q + 1) * width] = jnp.where(row == wanted, 1.0, 0.0).astype(BF16)
    ask_load.wait()

    for i, (r, c) in enumerate(peers):
        if i not in arrived:
            remote(packet.at[c], recv.at[number_of(r, c)], send1.at[i], recv1.at[i], r, c).wait_recv()

    received = recv[...].reshape(sources * CAP * comps, width)
    high, rest = halves_of(received)
    both = jnp.concatenate([high, rest], axis=1)
    swaps = []
    section = blocks // SWAPS
    for i in range(SWAPS):
        rows = pl.ds(i * section, section)
        added = jnp.dot(pick[i * section * comps : (i + 1) * section * comps], both, preferred_element_type=F32)
        part[rows] = (added[:, :width] + added[:, width:]).reshape(section, comps, width)
        swaps.append(remote(part.at[rows], part_in.at[rows], send3.at[i], recv3.at[i], twin, cell))
        swaps[i].start()
    for copy in swaps:
        copy.wait_recv()
    def block_of(b):
        return part[b] + part_in[b] - known[b]

    answers = []
    for i, c in enumerate(cell_peers):
        for s in range(CAP):
            at = (number_of(ray, c) * CAP + s) * comps
            row_at = asked_ref[number_of(ray, c), lax.div(at, width), lax.rem(at, width)]
            back_out[i, s] = block_of(lax.div(jnp.maximum(row_at - 1, 0), comps))
        answers.append(remote(back_out.at[i], back_in.at[cell], send4.at[i], recv4.at[i], ray, c))
        answers[i].start()
    for s in range(CAP):
        back_in[cell, s] = block_of(jnp.maximum(block_ref[0, cell * CAP + s], 0))
    for b in range(blocks):
        w_ref[b] = block_of(b)

    slab_gram = gram([w_ref[b] for b in range(blocks)])
    gram_out[...] = slab_gram
    gram_in[cell] = slab_gram
    grams = [
        remote(gram_out, gram_in.at[cell], send5.at[i], recv5.at[i], ray, c) for i, c in enumerate(cell_peers)
    ]
    for copy in grams:
        copy.start()

    for i, c in enumerate(cell_peers):
        remote(back_out.at[i], back_in.at[c], send4.at[i], recv4.at[i], ray, c).wait_recv()
    for p in range(n_cell):
        for s in range(CAP):
            w_slots[p * CAP + s] = split_rows(back_in[p, s])

    groups = u_ref.shape[1] // tile_rays
    totals = [jnp.zeros((8, width), F32) for g in range(groups)]
    for n in range(steps):
        at = n * quad
        rows = jnp.concatenate([w_slots[slot_ref[0, at + j]] for j in range(quad)], axis=0)
        found = jnp.dot(jnp.concatenate([rows, rows], axis=1), turned[n], preferred_element_type=F32)
        for j in range(quad // 2):
            lanes = slice(j * width, (j + 1) * width)
            top = 2 * j * 2 * comps
            pair = jnp.where(
                low_pair, found[top : top + 2 * comps, lanes], found[top + 2 * comps : top + 4 * comps, lanes]
            )
            pair = pair[:comps] + pair[comps:]
            owner = jnp.where(low, group_ref[0, at + 2 * j], group_ref[0, at + 2 * j + 1])
            for g in range(groups):
                totals[g] = totals[g] + jnp.where(owner == g, pair, 0.0)

    for i, c in enumerate(cell_peers):
        remote(gram_out, gram_in.at[c], send5.at[i], recv5.at[i], ray, c).wait_recv()
    whole_gram = gram_in[0]
    for p in range(1, n_cell):
        whole_gram = whole_gram + gram_in[p]
    lower, scales = cholesky(whole_gram * (1.0 / cells_all))
    alpha_t_columns = transposed(lower)
    totals = [total + pltpu.roll(total, tile_rays, 1) for total in totals]
    ray_blocks = u_ref.shape[1] // width
    residual = []
    for i in range(ray_blocks):
        image = jnp.where(low, totals[2 * i], totals[2 * i + 1])
        lanes = slice(i * width, (i + 1) * width)
        residual.append(solve(lower, scales, image) - apply(alpha_t_columns, u_ref[:, lanes]))
    pair_gram[0] = gram(residual)
    pairs = remote(pair_gram.at[0], pair_gram.at[1], send6.at[0], recv6.at[0], twin, cell)
    pairs.start()
    small_ref[0] = across_of(lower)
    for i in range(ray_blocks):
        small_ref[2 + i] = residual[i]
    pairs.wait_recv()
    all_gram[me] = pair_gram[0] + pair_gram[1]
    last = [
        remote(all_gram.at[me], all_gram.at[me], send7.at[i], recv7.at[i], r, c) for i, (r, c) in enumerate(peers)
    ]
    for copy in last:
        copy.start()
    for b in range(blocks):
        v_ref[:, b * width : (b + 1) * width] = solve(lower, scales, w_ref[b])
    store = pltpu.make_async_copy(v_ref, v_hbm, load_sem.at[8])
    store.start()
    for i, (r, c) in enumerate(peers):
        remote(all_gram.at[me], all_gram.at[number_of(r, c)], send7.at[i], recv7.at[i], r, c).wait_recv()
    total = all_gram[0]
    for d in range(1, sources):
        total = total + all_gram[d]
    small_ref[1] = total * (1.0 / rays_all)
    store.wait()
    for copy in first + indices + swaps + answers + grams + [pairs] + last:
        copy.wait_send()


def fused(n_ray, n_cell, ray_tiles, tile_group, tile_slot, slot_block, u_basis, v_prev, b_prev):
    tile_count, tile_rays, width = ray_tiles.shape
    comps, rays = u_basis.shape
    slots = slot_block.shape[1]
    blocks = v_prev.shape[1] // width
    sources = n_ray // 2 * n_cell
    bands = sources * CAP * comps // width
    steps = tile_count * tile_rays // (2 * width)
    vmem = pl.BlockSpec(memory_space=pltpu.VMEM)
    anywhere = pl.BlockSpec(memory_space=pl.ANY)
    tile = (comps, width)
    one = pltpu.SemaphoreType.DMA((1,))
    parts = pltpu.SemaphoreType.DMA((SWAPS,))
    far = pltpu.SemaphoreType.DMA((sources - 1,))
    cells = pltpu.SemaphoreType.DMA((n_cell - 1,))
    return pl.pallas_call(
        functools.partial(fused_kernel, n_ray, n_cell, v_prev.shape[1] * n_cell, rays * n_ray * n_cell),
        out_shape=(
            jax.ShapeDtypeStruct(v_prev.shape, F32),
            jax.ShapeDtypeStruct((2 + rays // width,) + tile, F32),
        ),
        in_specs=[anywhere] * 7,
        out_specs=(anywhere, vmem),
        scratch_shapes=[
            pltpu.SMEM(tile_group.shape, jnp.int32),
            pltpu.SMEM(tile_slot.shape, jnp.int32),
            pltpu.SMEM(slot_block.shape, jnp.int32),
            pltpu.SMEM((sources, bands, width), jnp.int32),
            pltpu.VMEM((n_cell, bands, width), jnp.int32),
            pltpu.VMEM((sources, bands, width), jnp.int32),
            pltpu.VMEM(ray_tiles.shape, F32),
            pltpu.VMEM(u_basis.shape, F32),
            pltpu.VMEM(v_prev.shape, F32),
            pltpu.VMEM(b_prev.shape, F32),
            pltpu.VMEM((rays // tile_rays, 2 * comps, width), BF16),
            pltpu.VMEM((rays // tile_rays, 2 * comps, width), BF16),
            pltpu.VMEM((slots * comps, tile_count * comps), BF16),
            pltpu.VMEM((tile_count * comps, 2 * width), BF16),
            pltpu.VMEM((steps, 2 * width, 2 * width), BF16),
            pltpu.VMEM((steps, 2 * width, 2 * width), BF16),
            pltpu.VMEM((blocks * comps, sources * CAP * comps), BF16),
            pltpu.VMEM((n_cell, CAP * comps, width), F32),
            pltpu.VMEM((sources, CAP * comps, width), F32),
            pltpu.VMEM((blocks,) + tile, F32),
            pltpu.VMEM((blocks,) + tile, F32),
            pltpu.VMEM((blocks,) + tile, F32),
            pltpu.VMEM((blocks,) + tile, F32),
            pltpu.VMEM((n_cell - 1, CAP) + tile, F32),
            pltpu.VMEM((n_cell, CAP) + tile, F32),
            pltpu.VMEM(tile, F32),
            pltpu.VMEM((n_cell,) + tile, F32),
            pltpu.VMEM((slots, 2 * comps, width), BF16),
            pltpu.VMEM((2,) + tile, F32),
            pltpu.VMEM((sources,) + tile, F32),
            pltpu.VMEM(v_prev.shape, F32),
            pltpu.SemaphoreType.DMA((CHUNKS,)),
            pltpu.SemaphoreType.DMA((9,)),
            far, far, far, far, parts, parts, cells, cells, cells, cells, one, one, far, far,
        ],
        compiler_params=pltpu.CompilerParams(
            collective_id=0, has_side_effects=True, vmem_limit_bytes=56 << 20
        ),
    )(tile_group, tile_slot, slot_block, ray_tiles, u_basis, v_prev, b_prev)


def per_device(n_ray, n_cell, ray_tiles, tile_group, tile_slot, slot_block, u_basis, v_prev, b_prev):
    tile_count, tile_rays, width = ray_tiles.shape
    comps, rays = u_basis.shape
    slots = slot_block.shape[1]
    blocks = v_prev.shape[1] // width
    piece = blocks // n_ray
    vmem = pl.BlockSpec(memory_space=pltpu.VMEM)
    smem = pl.BlockSpec(memory_space=pltpu.SMEM)
    anywhere = pl.BlockSpec(memory_space=pl.ANY)
    tile = (comps, width)
    packets = (n_cell, CAP + 1) + tile
    limit = 56 << 20
    small_shape = (2 + rays // width,) + tile
    if n_ray * n_cell <= DIRECT:
        v_next, small = fused(n_ray, n_cell, ray_tiles, tile_group, tile_slot, slot_block, u_basis, v_prev, b_prev)
    else:
        packet, high, low = pl.pallas_call(
            local_kernel,
            out_shape=(
                jax.ShapeDtypeStruct(packets, F32),
                jax.ShapeDtypeStruct((slots // 2, rays, 2 * width), BF16),
                jax.ShapeDtypeStruct((slots // 2, rays, 2 * width), BF16),
            ),
            in_specs=[smem, smem, smem, anywhere, vmem],
            out_specs=(vmem, anywhere, anywhere),
            scratch_shapes=[
                pltpu.VMEM(ray_tiles.shape, F32),
                pltpu.VMEM((rays, slots * width), F32),
                pltpu.VMEM((slots // 2, rays, 2 * width), BF16),
                pltpu.VMEM((slots // 2, rays, 2 * width), BF16),
                pltpu.SemaphoreType.DMA((CHUNKS,)),
                pltpu.SemaphoreType.DMA((2, slots // 2)),
            ],
            compiler_params=pltpu.CompilerParams(vmem_limit_bytes=limit),
        )(tile_group, tile_slot, slot_block, ray_tiles, u_basis)

        ray_sem = pltpu.SemaphoreType.DMA((n_ray - 1,))
        direct = min(n_ray * n_cell, DIRECT)
        all_sem = pltpu.SemaphoreType.DMA((direct - 1,))
        cell_sem = pltpu.SemaphoreType.DMA((n_cell - 1,))
        v_next, small = pl.pallas_call(
            functools.partial(step_kernel, n_ray, n_cell, v_prev.shape[1] * n_cell, rays * n_ray * n_cell),
            out_shape=(jax.ShapeDtypeStruct(v_prev.shape, F32), jax.ShapeDtypeStruct(small_shape, F32)),
            in_specs=[anywhere] * 6,
            out_specs=(anywhere, vmem),
            scratch_shapes=[
                pltpu.VMEM(packets, F32),
                pltpu.VMEM(u_basis.shape, F32),
                pltpu.VMEM(v_prev.shape, F32),
                pltpu.VMEM(b_prev.shape, F32),
                pltpu.VMEM(v_prev.shape, F32),
                pltpu.VMEM(packets, F32),
                pltpu.VMEM((n_ray, piece) + tile, F32),
                pltpu.VMEM((n_ray, piece) + tile, F32),
                pltpu.VMEM((n_ray, piece + 1) + tile, F32),
                pltpu.VMEM(packets, F32),
                pltpu.VMEM(packets, F32),
                pltpu.VMEM((n_ray,) + tile, F32),
                pltpu.VMEM((n_cell,) + tile, F32),
                pltpu.VMEM((direct,) + tile, F32),
                pltpu.VMEM((slots // 2, rays, 2 * width), BF16),
                pltpu.VMEM((slots // 2, rays, 2 * width), BF16),
                pltpu.VMEM((slots // 2, comps, 2 * width), F32),
                pltpu.SemaphoreType.DMA((7,)),
                cell_sem, cell_sem, ray_sem, ray_sem, ray_sem, ray_sem,
                cell_sem, cell_sem, ray_sem, ray_sem, cell_sem, cell_sem, all_sem, all_sem,
            ],
            compiler_params=pltpu.CompilerParams(
                collective_id=0, has_side_effects=True, vmem_limit_bytes=limit
            ),
        )(packet, high, low, u_basis, v_prev, b_prev)
    return pl.pallas_call(
        last_kernel,
        out_shape=(
            jax.ShapeDtypeStruct(v_prev.shape, F32),
            jax.ShapeDtypeStruct(u_basis.shape, F32),
            jax.ShapeDtypeStruct((comps, comps), F32),
            jax.ShapeDtypeStruct((comps, comps), F32),
        ),
        in_specs=[anywhere, anywhere],
        out_specs=(anywhere, anywhere, anywhere, anywhere),
        scratch_shapes=[
            pltpu.VMEM(v_prev.shape, F32),
            pltpu.VMEM(small_shape, F32),
            pltpu.VMEM(u_basis.shape, F32),
            pltpu.VMEM((comps, comps), F32),
            pltpu.VMEM((comps, comps), F32),
            pltpu.SemaphoreType.DMA((6,)),
        ],
    )(v_next, small)


def solution(mesh):
    in_specs = (
        P(("ray", "cell"), None, None),
        P(("ray", "cell"), None),
        P(("ray", "cell"), None),
        P(("ray", "cell"), None),
        P(None, ("ray", "cell")),
        P(None, "cell"),
        P(),
    )
    out_specs = (P(None, "cell"), P(None, ("ray", "cell")), P(), P())
    return jax.shard_map(
        functools.partial(per_device, mesh.shape["ray"], mesh.shape["cell"]),
        mesh=mesh,
        in_specs=in_specs,
        out_specs=out_specs,
        check_vma=False,
    )
```

```python
import functools

import jax
import jax.numpy as jnp
from jax import lax
from jax.experimental import pallas as pl
from jax.experimental.pallas import tpu as pltpu
from jax.sharding import PartitionSpec as P

CAP = 4
GROUPS = 8
CHUNKS = 3
UNROLL = 8
DIRECT = 32
SWAPS = 1
ORDER = 1
ANNOUNCE = 2
BATCH = 4
MESH = pl.DeviceIdType.MESH
F32 = jnp.float32
BF16 = jnp.bfloat16


def split_rows(value):
    high = value.astype(BF16).astype(F32)
    return jnp.concatenate([high, value - high], axis=0).astype(BF16)


def local_kernel(group_ref, slot_ref, block_ref, tiles_hbm, u_ref, packet_ref, high_hbm, low_hbm, tiles, dense, high_ref, low_ref, sems, out_sems):
    tile_count, tile_rays, width = tiles.shape
    slots = block_ref.shape[1]
    per_chunk = tile_count // CHUNKS

    def chunk(i):
        rows = pl.ds(i * per_chunk, per_chunk)
        return pltpu.make_async_copy(tiles_hbm.at[rows], tiles.at[rows], sems.at[i])

    for i in range(CHUNKS):
        chunk(i).start()

    row = lax.broadcasted_iota(jnp.int32, (8, width), 0)
    for p in range(slots // CAP):
        index = jnp.full((8, width), -1, jnp.int32)
        for s in range(CAP):
            index = jnp.where(row == s, block_ref[0, p * CAP + s], index)
        packet_ref[p, CAP] = index.astype(F32)

    @pl.loop(0, slots)
    def _(s):
        dense[:, pl.ds(pl.multiple_of(s * width, width), width)] = jnp.zeros((dense.shape[0], width), F32)

    for i in range(CHUNKS):
        chunk(i).wait()

        @pl.loop(0, per_chunk // BATCH)
        def _(at):
            first = i * per_chunk + at * BATCH
            where = [(group_ref[0, first + n], slot_ref[0, first + n]) for n in range(BATCH)]
            values = [tiles[first + n] for n in range(BATCH)]
            for (group, slot), value in zip(where, values):
                rows = pl.ds(pl.multiple_of(group * tile_rays, tile_rays), tile_rays)
                columns = pl.ds(pl.multiple_of(slot * width, width), width)
                dense[rows, columns] += value

    u_pair = split_rows(u_ref[...])
    comps = u_ref.shape[0]
    span = 2 * width

    def stores(n):
        return [
            pltpu.make_async_copy(source.at[n], target.at[n], out_sems.at[at, n])
            for at, (source, target) in enumerate(((high_ref, high_hbm), (low_ref, low_hbm)))
        ]

    def product(n):
        columns = pl.ds(pl.multiple_of(n * span, span), span)
        block = dense[:, columns]
        high = block.astype(BF16)
        low = (block - high.astype(F32)).astype(BF16)
        high_ref[n] = high
        low_ref[n] = low
        for store in stores(n):
            store.start()
        both = jnp.dot(u_pair, high, preferred_element_type=F32)
        rest = jnp.dot(u_pair, low, preferred_element_type=F32)
        total = both[:comps] + (both[comps:] + rest[:comps])
        for half in range(2):
            s = 2 * n + half
            packet_ref[s // CAP, s % CAP] = total[:, half * width : (half + 1) * width]

    def finish(n):
        for store in stores(n):
            store.wait()

    each_peer(slots // 2, product, 0)
    each_peer(slots // 2, finish, 0)


def each_peer(n, body, first=1):
    if n <= UNROLL:
        for k in range(first, n):
            body(k)
    else:
        pl.loop(first, n)(body)


def row_of(tile, k):
    return jnp.broadcast_to(tile[k : k + 1, :], tile.shape)


def column_of(tile, k):
    return jnp.broadcast_to(tile[:, k : k + 1], (tile.shape[0], 128))


def gram(blocks):
    lane = lax.broadcasted_iota(jnp.int32, (8, 128), 1)
    tile = jnp.zeros((8, 128), F32)
    for j in range(8):
        products = blocks[0] * row_of(blocks[0], j)
        for block in blocks[1:]:
            products = products + block * row_of(block, j)
        tile = jnp.where(lane == j, jnp.sum(products, axis=1, keepdims=True), tile)
    return tile


def factor(tile):
    row = lax.broadcasted_iota(jnp.int32, (8, 128), 0)
    lane = lax.broadcasted_iota(jnp.int32, (8, 128), 1)
    lower = jnp.zeros((8, 128), F32)
    upper = jnp.zeros((8, 128), F32)
    inverse = jnp.where(row == lane, 1.0, 0.0).astype(F32)
    for j in range(8):
        across = row_of(tile, j)
        down = column_of(tile, j)
        scale = 1.0 / jnp.sqrt(row_of(down, j))
        across = across * scale
        down = jnp.where(row >= j, down * scale, 0.0)
        lower = jnp.where(lane == j, down, lower)
        upper = jnp.where((row == j) & (lane >= j), across, upper)
        tile = tile - down * across
        pivot = row_of(inverse, j) * scale
        inverse = jnp.where(row == j, pivot, inverse - jnp.where(row > j, down, 0.0) * pivot)
    return lower, upper, inverse


def columns_of(tile):
    return [column_of(tile, k) for k in range(8)]


def apply(columns, block):
    total = columns[0] * row_of(block, 0)
    for k in range(1, 8):
        total = total + columns[k] * row_of(block, k)
    return total


def step_kernel(
    n_ray, n_cell, cells_all, rays_all,
    packet_hbm, high_hbm, low_hbm, u_hbm, v_prev_hbm, b_hbm,
    v_hbm, small_ref,
    packet_ref, u_ref, v_prev_ref, b_ref, v_ref, slots_in, part, pieces_in, slab_in, back_out, back_in, ray_gram, cell_gram, all_gram, high, low, w_slots,
    load_sem, send1, recv1, send2, recv2, send3, recv3, send4, recv4, send5, recv5, send6, recv6, send7, recv7,
):
    ray = lax.axis_index("ray")
    cell = lax.axis_index("cell")
    piece = pieces_in.shape[1]
    blocks = n_ray * piece

    early = [
        pltpu.make_async_copy(source, target, load_sem.at[2 + i])
        for i, (source, target) in enumerate(
            ((packet_hbm, packet_ref), (u_hbm, u_ref), (v_prev_hbm, v_prev_ref), (b_hbm, b_ref))
        )
    ]
    for load in early:
        load.start()
    loads = [
        pltpu.make_async_copy(high_hbm, high, load_sem.at[0]),
        pltpu.make_async_copy(low_hbm, low, load_sem.at[1]),
    ]
    for load in loads:
        load.start()

    barrier = pltpu.get_barrier_semaphore()

    each_peer(n_ray, lambda k: pl.semaphore_signal(barrier, inc=1, device_id={"ray": lax.rem(ray + k, n_ray)}, device_id_type=MESH))

    each_peer(n_cell, lambda k: pl.semaphore_signal(barrier, inc=1, device_id={"cell": lax.rem(cell + k, n_cell)}, device_id_type=MESH))

    pl.semaphore_wait(barrier, n_ray + n_cell - 2)

    def over(axis, me, n, source, target, send, recv):
        def copy(k):
            peer = lax.rem(me + k, n)
            return pltpu.make_async_remote_copy(
                src_ref=source(peer),
                dst_ref=target(me),
                send_sem=send.at[k - 1],
                recv_sem=recv.at[k - 1],
                device_id={axis: peer},
                device_id_type=MESH,
            )

        def wait_recv(k):
            origin = lax.rem(me + n - k, n)
            pltpu.make_async_remote_copy(
                src_ref=source(lax.rem(me + k, n)),
                dst_ref=target(origin),
                send_sem=send.at[k - 1],
                recv_sem=recv.at[k - 1],
                device_id={axis: lax.rem(me + k, n)},
                device_id_type=MESH,
            ).wait_recv()

        def receive():
            each_peer(n, wait_recv)

        def finish():
            each_peer(n, lambda k: copy(k).wait_send())

        return copy, receive, finish

    to_slab, from_slots, end1 = over(
        "cell", cell, n_cell, lambda peer: packet_ref.at[peer], lambda me: slots_in.at[me], send1, recv1
    )
    early[0].wait()
    each_peer(n_cell, lambda k: to_slab(k).start())
    for load in early[1:]:
        load.wait()
    slots_in[cell] = packet_ref[cell]
    from_slots()

    def index_tiles(p):
        tile = slots_in[p, CAP]
        return [row_of(tile, s) for s in range(CAP)]

    indices = [index_tiles(p) for p in range(n_cell)]

    def dense_block(b):
        number = jnp.full((8, 128), b, jnp.int32).astype(F32)
        total = jnp.zeros((8, 128), F32)
        for p in range(n_cell):
            for s in range(CAP):
                total = total + jnp.where(indices[p][s] == number, slots_in[p, s], 0.0)
        return total

    to_piece, from_pieces, end2 = over(
        "ray", ray, n_ray, lambda peer: part.at[peer], lambda me: pieces_in.at[me], send2, recv2
    )

    def send_piece(k):
        peer = lax.rem(ray + k, n_ray)
        for i in range(piece):
            part[peer, i] = dense_block(peer * piece + i)
        to_piece(k).start()

    each_peer(n_ray, send_piece)

    for i in range(piece):
        pieces_in[ray, i] = dense_block(ray * piece + i)

    b_columns = columns_of(b_ref[...])
    known = []
    for i in range(piece):
        at = pl.multiple_of((ray * piece + i) * 128, 128)
        known.append(apply(b_columns, v_prev_ref[:, pl.ds(at, 128)]))
    from_pieces()
    own = []
    for i in range(piece):
        total = pieces_in[0, i]
        for r in range(1, n_ray):
            total = total + pieces_in[r, i]
        own.append(total - known[i])
        slab_in[ray, i] = own[i]
    slab_in[ray, piece] = gram(own)

    to_ray, from_ray, end3 = over(
        "ray", ray, n_ray, lambda peer: slab_in.at[ray], lambda me: slab_in.at[me], send3, recv3
    )
    each_peer(n_ray, lambda k: to_ray(k).start())
    from_ray()

    slab_gram = slab_in[0, piece]
    for r in range(1, n_ray):
        slab_gram = slab_gram + slab_in[r, piece]

    def answer(p):
        wanted = index_tiles(p)
        found = [jnp.zeros((8, 128), F32) for s in range(CAP)]
        for b in range(blocks):
            block = slab_in[b // piece, b % piece]
            for s in range(CAP):
                found[s] = jnp.where(wanted[s] == float(b), block, found[s])
        return found

    to_cell, from_cell, end4 = over(
        "cell", cell, n_cell, lambda peer: back_out.at[peer], lambda me: back_in.at[me], send4, recv4
    )

    def send_answer(k):
        peer = lax.rem(cell + k, n_cell)
        found = answer(peer)
        for s in range(CAP):
            back_out[peer, s] = found[s]
        back_out[peer, CAP] = slab_gram
        to_cell(k).start()

    each_peer(n_cell, send_answer)

    found = answer(cell)
    for s in range(CAP):
        back_in[cell, s] = found[s]
    back_in[cell, CAP] = slab_gram
    for load in loads:
        load.wait()
    from_cell()

    whole_gram = back_in[0, CAP]
    for p in range(1, n_cell):
        whole_gram = whole_gram + back_in[p, CAP]
    for p in range(n_cell):
        for s in range(CAP):
            at = p * CAP + s
            w_slots[at // 2, :, (at % 2) * 128 : (at % 2 + 1) * 128] = back_in[p, s]
    across = (((1,), (1,)), ((), ()))

    def image_of(n):
        w_pair = split_rows(w_slots[n])
        both = lax.dot_general(w_pair, high[n], across, preferred_element_type=F32)
        rest = lax.dot_general(w_pair, low[n], across, preferred_element_type=F32)
        return both[:8] + (both[8:] + rest[:8])

    steps = high.shape[0]
    if steps <= UNROLL:
        image = image_of(0)
        for n in range(1, steps):
            image = image + image_of(n)
    else:
        image = lax.fori_loop(1, steps, lambda n, total: total + image_of(n), image_of(0))

    alpha, alpha_t, alpha_inverse = factor(whole_gram * (1.0 / cells_all))
    inverse_columns = columns_of(alpha_inverse)
    alpha_t_columns = columns_of(alpha_t)
    ray_blocks = u_ref.shape[1] // 128
    residual = []
    for i in range(ray_blocks):
        lanes = slice(i * 128, (i + 1) * 128)
        residual.append(apply(inverse_columns, image[:, lanes]) - apply(alpha_t_columns, u_ref[:, lanes]))
    everyone = n_ray * n_cell
    flat = ray * n_cell + cell
    own_gram = gram(residual)

    def gram_copy(k, back):
        peer = lax.rem(flat + k, everyone)
        slot = lax.rem(flat + everyone - k, everyone) if back else flat
        return pltpu.make_async_remote_copy(
            src_ref=all_gram.at[flat],
            dst_ref=all_gram.at[slot],
            send_sem=send7.at[k - 1],
            recv_sem=recv7.at[k - 1],
            device_id={"ray": lax.div(peer, n_cell), "cell": lax.rem(peer, n_cell)},
            device_id_type=MESH,
        )

    if everyone <= DIRECT:
        all_gram[flat] = own_gram
        for k in range(1, everyone):
            gram_copy(k, False).start()
    else:
        ray_gram[ray] = own_gram
        to_gram, from_gram, end5 = over(
            "ray", ray, n_ray, lambda peer: ray_gram.at[ray], lambda me: ray_gram.at[me], send5, recv5
        )
        each_peer(n_ray, lambda k: to_gram(k).start())

    small_ref[0] = alpha
    for i in range(ray_blocks):
        small_ref[2 + i] = residual[i]
    for b in range(blocks):
        v_ref[:, b * 128 : (b + 1) * 128] = apply(inverse_columns, slab_in[b // piece, b % piece])
    store = pltpu.make_async_copy(v_ref, v_hbm, load_sem.at[6])
    store.start()

    if everyone <= DIRECT:
        for k in range(1, everyone):
            gram_copy(k, True).wait_recv()
        total = all_gram[0]
        for d in range(1, everyone):
            total = total + all_gram[d]
    else:
        from_gram()
        total = ray_gram[0]
        for r in range(1, n_ray):
            total = total + ray_gram[r]
        cell_gram[cell] = total
        to_total, from_total, end6 = over(
            "cell", cell, n_cell, lambda peer: cell_gram.at[cell], lambda me: cell_gram.at[me], send6, recv6
        )
        each_peer(n_cell, lambda k: to_total(k).start())
        from_total()
        total = cell_gram[0]
        for p in range(1, n_cell):
            total = total + cell_gram[p]
    small_ref[1] = total * (1.0 / rays_all)
    store.wait()
    for end in (end1, end2, end3, end4):
        end()
    if everyone <= DIRECT:
        for k in range(1, everyone):
            gram_copy(k, False).wait_send()
    else:
        end5()
        end6()


def cholesky(tile, count=8):
    row = lax.broadcasted_iota(jnp.int32, (8, 128), 0)
    rest = [column_of(tile, k) for k in range(count)]
    lower, scales = [], []
    for j in range(count):
        scale = lax.rsqrt(row_of(rest[j], j))
        column = jnp.where(row >= j, rest[j] * scale, 0.0)
        lower.append(column)
        scales.append(scale)
        for k in range(j + 1, count):
            rest[k] = rest[k] - column * row_of(column, k)
    return lower, scales


def across_of(columns):
    lane = lax.broadcasted_iota(jnp.int32, (8, 128), 1)
    tile = jnp.zeros((8, 128), F32)
    for k, column in enumerate(columns):
        tile = jnp.where(lane == k, column, tile)
    return tile


def transposed(columns):
    row = lax.broadcasted_iota(jnp.int32, (8, 128), 0)
    turned = []
    for k in range(len(columns)):
        column = jnp.zeros((8, 128), F32)
        for i in range(k + 1):
            column = jnp.where(row == i, row_of(columns[i], k), column)
        turned.append(column)
    return turned


def solve(lower, scales, block):
    row = lax.broadcasted_iota(jnp.int32, (8, 128), 0)
    found = block
    for j, (column, scale) in enumerate(zip(lower, scales)):
        value = row_of(block, j) * scale
        found = jnp.where(row == j, value, found)
        block = block - column * value
    return found


def last_kernel(v_hbm, small_hbm, v_out, u_out, alpha_out, beta_out, v_ref, small, u_ref, alpha_ref, beta_ref, sems):
    load = pltpu.make_async_copy(small_hbm, small, sems.at[0])
    v_load = pltpu.make_async_copy(v_hbm, v_ref, sems.at[1])
    load.start()
    v_load.start()
    stores = [
        pltpu.make_async_copy(source, target, sems.at[2 + i])
        for i, (source, target) in enumerate(
            ((v_ref, v_out), (alpha_ref, alpha_out), (beta_ref, beta_out), (u_ref, u_out))
        )
    ]
    load.wait()
    alpha_ref[...] = small[0][:, :8]
    stores[1].start()
    v_load.wait()
    stores[0].start()
    lower, scales = cholesky(small[1])
    beta_ref[...] = across_of(lower)[:, :8]
    for i in range(small.shape[0] - 2):
        u_ref[:, i * 128 : (i + 1) * 128] = solve(lower, scales, small[2 + i])
    stores[2].start()
    stores[3].start()
    for store in stores:
        store.wait()


def flips_of(index, count):
    flips, bit = {}, 1
    while bit < count:
        flips[bit] = bit * (1 - 2 * lax.rem(lax.div(index, bit), 2))
        bit *= 2
    return flips


def flipped(index, flips, mask):
    for bit, step in flips.items():
        if mask & bit:
            index = index + step
    return index


def far_first(n_ray, n_cell):
    masks = [(2 * a, c) for a in range(n_ray // 2) for c in range(n_cell) if a or c]
    return sorted(masks, key=lambda m: -(8 * (m[1] >= 2) + 2 * bin(m[0]).count("1") + m[1]))


def halves_of(value):
    high = value.astype(BF16)
    return high, (value - high.astype(F32)).astype(BF16)


def fused_kernel(
    n_ray, n_cell, cells_all, rays_all,
    group_hbm, slot_hbm, block_hbm, tiles_hbm, u_hbm, v_prev_hbm, b_hbm,
    v_hbm, small_ref,
    group_ref, slot_ref, block_ref, asked_ref, index_out, index_in, tiles, u_ref, v_prev_ref, b_ref,
    u_left, u_right, gather, products, split, turned, pick, packet, recv, part, part_in, known, w_ref,
    back_out, back_in, gram_out, gram_in, w_slots, pair_gram, all_gram, v_ref,
    tile_sem, load_sem, send1, recv1, send2, recv2, send3, recv3, send4, recv4, send5, recv5, send6, recv6, send7, recv7,
):
    ray = lax.axis_index("ray")
    cell = lax.axis_index("cell")
    tile_count, tile_rays, width = tiles.shape
    slots = block_ref.shape[1]
    comps = u_ref.shape[0]
    sources = n_ray // 2 * n_cell
    blocks = w_ref.shape[0]
    steps, span = split.shape[0], split.shape[1]
    chunks = tile_sem.shape[0]
    per_chunk = tile_count // chunks
    per_step = steps // chunks
    quad = span // tile_rays

    small_loads = [
        pltpu.make_async_copy(source, target, load_sem.at[i])
        for i, (source, target) in enumerate(
            (
                (block_hbm, block_ref), (u_hbm, u_ref), (slot_hbm, slot_ref), (group_hbm, group_ref),
                (v_prev_hbm, v_prev_ref), (b_hbm, b_ref),
            )
        )
    ]

    def chunk(i):
        rows = pl.ds(i * per_chunk, per_chunk)
        return pltpu.make_async_copy(tiles_hbm.at[rows], tiles.at[rows], tile_sem.at[i])

    for load in small_loads[:4]:
        load.start()
    for i in range(chunks):
        chunk(i).start()
    for load in small_loads[4:]:
        load.start()

    ray_flips = flips_of(ray, n_ray)
    cell_flips = flips_of(cell, n_cell)
    masks = far_first(n_ray, n_cell)
    peers = [(flipped(ray, ray_flips, a), flipped(cell, cell_flips, c)) for a, c in masks]
    twin = ray + ray_flips[1]
    cell_masks = list(range(n_cell - 1, 0, -1))
    cell_peers = [flipped(cell, cell_flips, c) for c in cell_masks]

    def number_of(ray_at, cell_at):
        return lax.div(ray_at, 2) * n_cell + cell_at

    me = number_of(ray, cell)

    barrier = pltpu.get_barrier_semaphore()
    for r, c in peers + [(twin, cell)]:
        pl.semaphore_signal(barrier, inc=1, device_id={"ray": r, "cell": c}, device_id_type=MESH)

    def remote(source, target, send, recv_at, r, c):
        return pltpu.make_async_remote_copy(
            src_ref=source, dst_ref=target, send_sem=send, recv_sem=recv_at,
            device_id={"ray": r, "cell": c}, device_id_type=MESH,
        )

    small_loads[0].wait()
    lane = lax.broadcasted_iota(jnp.int32, (8, width), 1)
    bands = sources * CAP * comps // width
    band = lax.broadcasted_iota(jnp.int32, (bands, width), 0)
    place = band * width + lax.broadcasted_iota(jnp.int32, (bands, width), 1) - me * CAP * comps
    for p in range(n_cell):
        index = jnp.zeros((bands, width), jnp.int32)
        for s in range(CAP):
            b = block_ref[0, p * CAP + s]
            first_row = jnp.where(b < 0, -comps - 1, (b - s) * comps + 1)
            inside = (place >= s * comps) & (place < (s + 1) * comps)
            index = jnp.where(inside, jnp.maximum(place + first_row, 0), index)
        index_out[p] = index
    index_in[me] = index_out[cell]

    def announce():
        pl.semaphore_wait(barrier, len(peers) + 1)
        for copy in indices:
            copy.start()

    indices = [
        remote(index_out.at[c], index_in.at[me], send2.at[i], recv2.at[i], r, c) for i, (r, c) in enumerate(peers)
    ]

    for load in small_loads[1:4]:
        load.wait()
    low = lane < tile_rays
    low_pair = lax.broadcasted_iota(jnp.int32, (2 * comps, width), 1) < tile_rays
    for q in range(u_ref.shape[1] // width):
        block = u_ref[:, q * width : (q + 1) * width]
        turn = pltpu.roll(block, tile_rays, 1)
        for half, (left, right) in enumerate(((block, turn), (turn, block))):
            u_left[2 * q + half] = split_rows(jnp.where(low, left, 0.0))
            u_right[2 * q + half] = split_rows(jnp.where(low, 0.0, right))

    per_band = width // comps
    lane_tile = lax.div(lane, comps)
    slot_row = lax.broadcasted_iota(jnp.int32, (slots * comps, width), 0)
    offset = lax.rem(lane, comps)
    for q in range(tile_count // per_band):
        owner = jnp.zeros((8, width), jnp.int32)
        for t in range(per_band):
            owner = jnp.where(lane_tile == t, slot_ref[0, q * per_band + t], owner)
        owner = jnp.broadcast_to((owner * comps + offset)[:1], slot_row.shape)
        gather[:, q * width : (q + 1) * width] = jnp.where(slot_row == owner, 1.0, 0.0).astype(BF16)

    nothing = jnp.zeros((2 * quad // 2 * comps, width), BF16)
    for i in range(chunks):
        if i == ANNOUNCE:
            announce()
        chunk(i).wait()
        for n in range(i * per_step, (i + 1) * per_step):
            value = tiles[n * quad : (n + 1) * quad].reshape(span, width)
            high, rest = halves_of(value)
            both = jnp.concatenate([high, rest], axis=1)
            split[n] = both
            columns = []
            for h in range(2):
                at = n * quad + 2 * h
                own = jnp.concatenate([u_left[group_ref[0, at]], u_right[group_ref[0, at + 1]]], axis=0)
                columns.append(jnp.concatenate([own, nothing] if h == 0 else [nothing, own], axis=0))
            product = jnp.dot(jnp.concatenate(columns, axis=1), both, preferred_element_type=F32)
            product = (product[:, :width] + product[:, width:]).reshape(quad, 2 * comps, width)
            product = (product[:, :comps] + product[:, comps:]).reshape(quad * comps, width)
            high, rest = halves_of(product)
            products[n * quad * comps : (n + 1) * quad * comps] = jnp.concatenate([high, rest], axis=1)

    slot_sums = jnp.dot(gather[...], products[...], preferred_element_type=F32)
    packet[...] = (slot_sums[:, :width] + slot_sums[:, width:]).reshape(packet.shape)
    recv[me] = packet[cell]

    if ANNOUNCE >= chunks:
        announce()
    half = n_cell // 2
    passed = [(a, c) for a, c in masks if c >= half and a]
    sent = [i for i, mask in enumerate(masks) if mask not in passed]
    sent.sort(key=lambda i: (masks[i][1] < half, ORDER * bin(masks[i][0]).count("1") - masks[i][1]))
    first = [remote(packet.at[peers[i][1]], recv.at[me], send1.at[i], recv1.at[i], *peers[i]) for i in sent]
    for copy in first:
        copy.start()

    def pass_on(mask, c):
        i = masks.index(mask)
        source = recv.at[number_of(ray, c)]
        return remote(source, source, send1.at[i], recv1.at[i], flipped(ray, ray_flips, mask[0]), cell)

    arrived = [i for i in sent if masks[i][0] == 0 and masks[i][1] >= half]
    for i in arrived[::-1]:
        r, c = peers[i]
        remote(packet.at[c], recv.at[number_of(r, c)], send1.at[i], recv1.at[i], r, c).wait_recv()
        for mask in passed:
            if mask[1] == masks[i][1]:
                copy = pass_on(mask, c)
                copy.start()
                first.append(copy)

    for load in small_loads[4:]:
        load.wait()
    b_columns = columns_of(b_ref[...])
    for b in range(blocks):
        known[b] = apply(b_columns, v_prev_ref[:, b * width : (b + 1) * width])

    @pl.loop(0, steps)
    def _(n):
        turned[n] = split[n].T

    for i, (r, c) in enumerate(peers):
        remote(index_out.at[c], index_in.at[number_of(r, c)], send2.at[i], recv2.at[i], r, c).wait_recv()
    ask_load = pltpu.make_async_copy(index_in, asked_ref, load_sem.at[6])
    ask_load.start()
    asked = index_in[0]
    for d in range(1, sources):
        asked = asked + index_in[d]
    row = lax.broadcasted_iota(jnp.int32, (blocks * comps, width), 0) + 1
    for q in range(bands):
        wanted = jnp.broadcast_to(asked[q : q + 1], (blocks * comps, width))
        pick[:, q * width : (q + 1) * width] = jnp.where(row == wanted, 1.0, 0.0).astype(BF16)
    ask_load.wait()

    for i, (r, c) in enumerate(peers):
        if i not in arrived:
            remote(packet.at[c], recv.at[number_of(r, c)], send1.at[i], recv1.at[i], r, c).wait_recv()

    received = recv[...].reshape(sources * CAP * comps, width)
    high, rest = halves_of(received)
    both = jnp.concatenate([high, rest], axis=1)
    swaps = []
    section = blocks // SWAPS
    for i in range(SWAPS):
        rows = pl.ds(i * section, section)
        added = jnp.dot(pick[i * section * comps : (i + 1) * section * comps], both, preferred_element_type=F32)
        part[rows] = (added[:, :width] + added[:, width:]).reshape(section, comps, width)
        swaps.append(remote(part.at[rows], part_in.at[rows], send3.at[i], recv3.at[i], twin, cell))
        swaps[i].start()
    for copy in swaps:
        copy.wait_recv()
    def block_of(b):
        return part[b] + part_in[b] - known[b]

    answers = []
    for i, c in enumerate(cell_peers):
        for s in range(CAP):
            at = (number_of(ray, c) * CAP + s) * comps
            row_at = asked_ref[number_of(ray, c), lax.div(at, width), lax.rem(at, width)]
            back_out[i, s] = block_of(lax.div(jnp.maximum(row_at - 1, 0), comps))
        answers.append(remote(back_out.at[i], back_in.at[cell], send4.at[i], recv4.at[i], ray, c))
        answers[i].start()
    for s in range(CAP):
        back_in[cell, s] = block_of(jnp.maximum(block_ref[0, cell * CAP + s], 0))
    for b in range(blocks):
        w_ref[b] = block_of(b)

    slab_gram = gram([w_ref[b] for b in range(blocks)])
    gram_out[...] = slab_gram
    gram_in[cell] = slab_gram
    grams = [
        remote(gram_out, gram_in.at[cell], send5.at[i], recv5.at[i], ray, c) for i, c in enumerate(cell_peers)
    ]
    for copy in grams:
        copy.start()

    for i, c in enumerate(cell_peers):
        remote(back_out.at[i], back_in.at[c], send4.at[i], recv4.at[i], ray, c).wait_recv()
    for p in range(n_cell):
        for s in range(CAP):
            w_slots[p * CAP + s] = split_rows(back_in[p, s])

    groups = u_ref.shape[1] // tile_rays
    totals = [jnp.zeros((8, width), F32) for g in range(groups)]
    for n in range(steps):
        at = n * quad
        rows = jnp.concatenate([w_slots[slot_ref[0, at + j]] for j in range(quad)], axis=0)
        found = jnp.dot(jnp.concatenate([rows, rows], axis=1), turned[n], preferred_element_type=F32)
        for j in range(quad // 2):
            lanes = slice(j * width, (j + 1) * width)
            top = 2 * j * 2 * comps
            pair = jnp.where(
                low_pair, found[top : top + 2 * comps, lanes], found[top + 2 * comps : top + 4 * comps, lanes]
            )
            pair = pair[:comps] + pair[comps:]
            owner = jnp.where(low, group_ref[0, at + 2 * j], group_ref[0, at + 2 * j + 1])
            for g in range(groups):
                totals[g] = totals[g] + jnp.where(owner == g, pair, 0.0)

    for i, c in enumerate(cell_peers):
        remote(gram_out, gram_in.at[c], send5.at[i], recv5.at[i], ray, c).wait_recv()
    whole_gram = gram_in[0]
    for p in range(1, n_cell):
        whole_gram = whole_gram + gram_in[p]
    lower, scales = cholesky(whole_gram * (1.0 / cells_all))
    alpha_t_columns = transposed(lower)
    totals = [total + pltpu.roll(total, tile_rays, 1) for total in totals]
    ray_blocks = u_ref.shape[1] // width
    residual = []
    for i in range(ray_blocks):
        image = jnp.where(low, totals[2 * i], totals[2 * i + 1])
        lanes = slice(i * width, (i + 1) * width)
        residual.append(solve(lower, scales, image) - apply(alpha_t_columns, u_ref[:, lanes]))
    pair_gram[0] = gram(residual)
    pairs = remote(pair_gram.at[0], pair_gram.at[1], send6.at[0], recv6.at[0], twin, cell)
    pairs.start()
    small_ref[0] = across_of(lower)
    for i in range(ray_blocks):
        small_ref[2 + i] = residual[i]
    pairs.wait_recv()
    all_gram[me] = pair_gram[0] + pair_gram[1]
    last = [
        remote(all_gram.at[me], all_gram.at[me], send7.at[i], recv7.at[i], r, c) for i, (r, c) in enumerate(peers)
    ]
    for copy in last:
        copy.start()
    for b in range(blocks):
        v_ref[:, b * width : (b + 1) * width] = solve(lower, scales, w_ref[b])
    store = pltpu.make_async_copy(v_ref, v_hbm, load_sem.at[8])
    store.start()
    for copy in first + indices + swaps + answers + grams + [pairs] + last:
        copy.wait_send()
    store.wait()
    for i, (r, c) in enumerate(peers):
        remote(all_gram.at[me], all_gram.at[number_of(r, c)], send7.at[i], recv7.at[i], r, c).wait_recv()
    total = all_gram[0]
    for d in range(1, sources):
        total = total + all_gram[d]
    small_ref[1] = total * (1.0 / rays_all)


def fused(n_ray, n_cell, ray_tiles, tile_group, tile_slot, slot_block, u_basis, v_prev, b_prev):
    tile_count, tile_rays, width = ray_tiles.shape
    comps, rays = u_basis.shape
    slots = slot_block.shape[1]
    blocks = v_prev.shape[1] // width
    sources = n_ray // 2 * n_cell
    bands = sources * CAP * comps // width
    steps = tile_count * tile_rays // (2 * width)
    vmem = pl.BlockSpec(memory_space=pltpu.VMEM)
    anywhere = pl.BlockSpec(memory_space=pl.ANY)
    tile = (comps, width)
    one = pltpu.SemaphoreType.DMA((1,))
    parts = pltpu.SemaphoreType.DMA((SWAPS,))
    far = pltpu.SemaphoreType.DMA((sources - 1,))
    cells = pltpu.SemaphoreType.DMA((n_cell - 1,))
    return pl.pallas_call(
        functools.partial(fused_kernel, n_ray, n_cell, v_prev.shape[1] * n_cell, rays * n_ray * n_cell),
        out_shape=(
            jax.ShapeDtypeStruct(v_prev.shape, F32),
            jax.ShapeDtypeStruct((2 + rays // width,) + tile, F32),
        ),
        in_specs=[anywhere] * 7,
        out_specs=(anywhere, vmem),
        scratch_shapes=[
            pltpu.SMEM(tile_group.shape, jnp.int32),
            pltpu.SMEM(tile_slot.shape, jnp.int32),
            pltpu.SMEM(slot_block.shape, jnp.int32),
            pltpu.SMEM((sources, bands, width), jnp.int32),
            pltpu.VMEM((n_cell, bands, width), jnp.int32),
            pltpu.VMEM((sources, bands, width), jnp.int32),
            pltpu.VMEM(ray_tiles.shape, F32),
            pltpu.VMEM(u_basis.shape, F32),
            pltpu.VMEM(v_prev.shape, F32),
            pltpu.VMEM(b_prev.shape, F32),
            pltpu.VMEM((rays // tile_rays, 2 * comps, width), BF16),
            pltpu.VMEM((rays // tile_rays, 2 * comps, width), BF16),
            pltpu.VMEM((slots * comps, tile_count * comps), BF16),
            pltpu.VMEM((tile_count * comps, 2 * width), BF16),
            pltpu.VMEM((steps, 2 * width, 2 * width), BF16),
            pltpu.VMEM((steps, 2 * width, 2 * width), BF16),
            pltpu.VMEM((blocks * comps, sources * CAP * comps), BF16),
            pltpu.VMEM((n_cell, CAP * comps, width), F32),
            pltpu.VMEM((sources, CAP * comps, width), F32),
            pltpu.VMEM((blocks,) + tile, F32),
            pltpu.VMEM((blocks,) + tile, F32),
            pltpu.VMEM((blocks,) + tile, F32),
            pltpu.VMEM((blocks,) + tile, F32),
            pltpu.VMEM((n_cell - 1, CAP) + tile, F32),
            pltpu.VMEM((n_cell, CAP) + tile, F32),
            pltpu.VMEM(tile, F32),
            pltpu.VMEM((n_cell,) + tile, F32),
            pltpu.VMEM((slots, 2 * comps, width), BF16),
            pltpu.VMEM((2,) + tile, F32),
            pltpu.VMEM((sources,) + tile, F32),
            pltpu.VMEM(v_prev.shape, F32),
            pltpu.SemaphoreType.DMA((CHUNKS,)),
            pltpu.SemaphoreType.DMA((9,)),
            far, far, far, far, parts, parts, cells, cells, cells, cells, one, one, far, far,
        ],
        compiler_params=pltpu.CompilerParams(
            collective_id=0, has_side_effects=True, vmem_limit_bytes=56 << 20
        ),
    )(tile_group, tile_slot, slot_block, ray_tiles, u_basis, v_prev, b_prev)


def per_device(n_ray, n_cell, ray_tiles, tile_group, tile_slot, slot_block, u_basis, v_prev, b_prev):
    tile_count, tile_rays, width = ray_tiles.shape
    comps, rays = u_basis.shape
    slots = slot_block.shape[1]
    blocks = v_prev.shape[1] // width
    piece = blocks // n_ray
    vmem = pl.BlockSpec(memory_space=pltpu.VMEM)
    smem = pl.BlockSpec(memory_space=pltpu.SMEM)
    anywhere = pl.BlockSpec(memory_space=pl.ANY)
    tile = (comps, width)
    packets = (n_cell, CAP + 1) + tile
    limit = 56 << 20
    small_shape = (2 + rays // width,) + tile
    if n_ray * n_cell <= DIRECT:
        v_next, small = fused(n_ray, n_cell, ray_tiles, tile_group, tile_slot, slot_block, u_basis, v_prev, b_prev)
    else:
        packet, high, low = pl.pallas_call(
            local_kernel,
            out_shape=(
                jax.ShapeDtypeStruct(packets, F32),
                jax.ShapeDtypeStruct((slots // 2, rays, 2 * width), BF16),
                jax.ShapeDtypeStruct((slots // 2, rays, 2 * width), BF16),
            ),
            in_specs=[smem, smem, smem, anywhere, vmem],
            out_specs=(vmem, anywhere, anywhere),
            scratch_shapes=[
                pltpu.VMEM(ray_tiles.shape, F32),
                pltpu.VMEM((rays, slots * width), F32),
                pltpu.VMEM((slots // 2, rays, 2 * width), BF16),
                pltpu.VMEM((slots // 2, rays, 2 * width), BF16),
                pltpu.SemaphoreType.DMA((CHUNKS,)),
                pltpu.SemaphoreType.DMA((2, slots // 2)),
            ],
            compiler_params=pltpu.CompilerParams(vmem_limit_bytes=limit),
        )(tile_group, tile_slot, slot_block, ray_tiles, u_basis)

        ray_sem = pltpu.SemaphoreType.DMA((n_ray - 1,))
        direct = min(n_ray * n_cell, DIRECT)
        all_sem = pltpu.SemaphoreType.DMA((direct - 1,))
        cell_sem = pltpu.SemaphoreType.DMA((n_cell - 1,))
        v_next, small = pl.pallas_call(
            functools.partial(step_kernel, n_ray, n_cell, v_prev.shape[1] * n_cell, rays * n_ray * n_cell),
            out_shape=(jax.ShapeDtypeStruct(v_prev.shape, F32), jax.ShapeDtypeStruct(small_shape, F32)),
            in_specs=[anywhere] * 6,
            out_specs=(anywhere, vmem),
            scratch_shapes=[
                pltpu.VMEM(packets, F32),
                pltpu.VMEM(u_basis.shape, F32),
                pltpu.VMEM(v_prev.shape, F32),
                pltpu.VMEM(b_prev.shape, F32),
                pltpu.VMEM(v_prev.shape, F32),
                pltpu.VMEM(packets, F32),
                pltpu.VMEM((n_ray, piece) + tile, F32),
                pltpu.VMEM((n_ray, piece) + tile, F32),
                pltpu.VMEM((n_ray, piece + 1) + tile, F32),
                pltpu.VMEM(packets, F32),
                pltpu.VMEM(packets, F32),
                pltpu.VMEM((n_ray,) + tile, F32),
                pltpu.VMEM((n_cell,) + tile, F32),
                pltpu.VMEM((direct,) + tile, F32),
                pltpu.VMEM((slots // 2, rays, 2 * width), BF16),
                pltpu.VMEM((slots // 2, rays, 2 * width), BF16),
                pltpu.VMEM((slots // 2, comps, 2 * width), F32),
                pltpu.SemaphoreType.DMA((7,)),
                cell_sem, cell_sem, ray_sem, ray_sem, ray_sem, ray_sem,
                cell_sem, cell_sem, ray_sem, ray_sem, cell_sem, cell_sem, all_sem, all_sem,
            ],
            compiler_params=pltpu.CompilerParams(
                collective_id=0, has_side_effects=True, vmem_limit_bytes=limit
            ),
        )(packet, high, low, u_basis, v_prev, b_prev)
    return pl.pallas_call(
        last_kernel,
        out_shape=(
            jax.ShapeDtypeStruct(v_prev.shape, F32),
            jax.ShapeDtypeStruct(u_basis.shape, F32),
            jax.ShapeDtypeStruct((comps, comps), F32),
            jax.ShapeDtypeStruct((comps, comps), F32),
        ),
        in_specs=[anywhere, anywhere],
        out_specs=(anywhere, anywhere, anywhere, anywhere),
        scratch_shapes=[
            pltpu.VMEM(v_prev.shape, F32),
            pltpu.VMEM(small_shape, F32),
            pltpu.VMEM(u_basis.shape, F32),
            pltpu.VMEM((comps, comps), F32),
            pltpu.VMEM((comps, comps), F32),
            pltpu.SemaphoreType.DMA((6,)),
        ],
    )(v_next, small)


def solution(mesh):
    in_specs = (
        P(("ray", "cell"), None, None),
        P(("ray", "cell"), None),
        P(("ray", "cell"), None),
        P(("ray", "cell"), None),
        P(None, ("ray", "cell")),
        P(None, "cell"),
        P(),
    )
    out_specs = (P(None, "cell"), P(None, ("ray", "cell")), P(), P())
    return jax.shard_map(
        functools.partial(per_device, mesh.shape["ray"], mesh.shape["cell"]),
        mesh=mesh,
        in_specs=in_specs,
        out_specs=out_specs,
        check_vma=False,
    )
```

```python
import functools

import jax
import jax.numpy as jnp
from jax import lax
from jax.experimental import pallas as pl
from jax.experimental.pallas import tpu as pltpu
from jax.sharding import PartitionSpec as P

CAP = 4
GROUPS = 8
CHUNKS = 3
UNROLL = 8
DIRECT = 32
SWAPS = 1
ORDER = 1
ANNOUNCE = 3
BATCH = 4
MESH = pl.DeviceIdType.MESH
F32 = jnp.float32
BF16 = jnp.bfloat16


def split_rows(value):
    high = value.astype(BF16).astype(F32)
    return jnp.concatenate([high, value - high], axis=0).astype(BF16)


def local_kernel(group_ref, slot_ref, block_ref, tiles_hbm, u_ref, packet_ref, high_hbm, low_hbm, tiles, dense, high_ref, low_ref, sems, out_sems):
    tile_count, tile_rays, width = tiles.shape
    slots = block_ref.shape[1]
    per_chunk = tile_count // CHUNKS

    def chunk(i):
        rows = pl.ds(i * per_chunk, per_chunk)
        return pltpu.make_async_copy(tiles_hbm.at[rows], tiles.at[rows], sems.at[i])

    for i in range(CHUNKS):
        chunk(i).start()

    row = lax.broadcasted_iota(jnp.int32, (8, width), 0)
    for p in range(slots // CAP):
        index = jnp.full((8, width), -1, jnp.int32)
        for s in range(CAP):
            index = jnp.where(row == s, block_ref[0, p * CAP + s], index)
        packet_ref[p, CAP] = index.astype(F32)

    @pl.loop(0, slots)
    def _(s):
        dense[:, pl.ds(pl.multiple_of(s * width, width), width)] = jnp.zeros((dense.shape[0], width), F32)

    for i in range(CHUNKS):
        chunk(i).wait()

        @pl.loop(0, per_chunk // BATCH)
        def _(at):
            first = i * per_chunk + at * BATCH
            where = [(group_ref[0, first + n], slot_ref[0, first + n]) for n in range(BATCH)]
            values = [tiles[first + n] for n in range(BATCH)]
            for (group, slot), value in zip(where, values):
                rows = pl.ds(pl.multiple_of(group * tile_rays, tile_rays), tile_rays)
                columns = pl.ds(pl.multiple_of(slot * width, width), width)
                dense[rows, columns] += value

    u_pair = split_rows(u_ref[...])
    comps = u_ref.shape[0]
    span = 2 * width

    def stores(n):
        return [
            pltpu.make_async_copy(source.at[n], target.at[n], out_sems.at[at, n])
            for at, (source, target) in enumerate(((high_ref, high_hbm), (low_ref, low_hbm)))
        ]

    def product(n):
        columns = pl.ds(pl.multiple_of(n * span, span), span)
        block = dense[:, columns]
        high = block.astype(BF16)
        low = (block - high.astype(F32)).astype(BF16)
        high_ref[n] = high
        low_ref[n] = low
        for store in stores(n):
            store.start()
        both = jnp.dot(u_pair, high, preferred_element_type=F32)
        rest = jnp.dot(u_pair, low, preferred_element_type=F32)
        total = both[:comps] + (both[comps:] + rest[:comps])
        for half in range(2):
            s = 2 * n + half
            packet_ref[s // CAP, s % CAP] = total[:, half * width : (half + 1) * width]

    def finish(n):
        for store in stores(n):
            store.wait()

    each_peer(slots // 2, product, 0)
    each_peer(slots // 2, finish, 0)


def each_peer(n, body, first=1):
    if n <= UNROLL:
        for k in range(first, n):
            body(k)
    else:
        pl.loop(first, n)(body)


def row_of(tile, k):
    return jnp.broadcast_to(tile[k : k + 1, :], tile.shape)


def column_of(tile, k):
    return jnp.broadcast_to(tile[:, k : k + 1], (tile.shape[0], 128))


def gram(blocks):
    lane = lax.broadcasted_iota(jnp.int32, (8, 128), 1)
    tile = jnp.zeros((8, 128), F32)
    for j in range(8):
        products = blocks[0] * row_of(blocks[0], j)
        for block in blocks[1:]:
            products = products + block * row_of(block, j)
        tile = jnp.where(lane == j, jnp.sum(products, axis=1, keepdims=True), tile)
    return tile


def factor(tile):
    row = lax.broadcasted_iota(jnp.int32, (8, 128), 0)
    lane = lax.broadcasted_iota(jnp.int32, (8, 128), 1)
    lower = jnp.zeros((8, 128), F32)
    upper = jnp.zeros((8, 128), F32)
    inverse = jnp.where(row == lane, 1.0, 0.0).astype(F32)
    for j in range(8):
        across = row_of(tile, j)
        down = column_of(tile, j)
        scale = 1.0 / jnp.sqrt(row_of(down, j))
        across = across * scale
        down = jnp.where(row >= j, down * scale, 0.0)
        lower = jnp.where(lane == j, down, lower)
        upper = jnp.where((row == j) & (lane >= j), across, upper)
        tile = tile - down * across
        pivot = row_of(inverse, j) * scale
        inverse = jnp.where(row == j, pivot, inverse - jnp.where(row > j, down, 0.0) * pivot)
    return lower, upper, inverse


def columns_of(tile):
    return [column_of(tile, k) for k in range(8)]


def apply(columns, block):
    total = columns[0] * row_of(block, 0)
    for k in range(1, 8):
        total = total + columns[k] * row_of(block, k)
    return total


def step_kernel(
    n_ray, n_cell, cells_all, rays_all,
    packet_hbm, high_hbm, low_hbm, u_hbm, v_prev_hbm, b_hbm,
    v_hbm, small_ref,
    packet_ref, u_ref, v_prev_ref, b_ref, v_ref, slots_in, part, pieces_in, slab_in, back_out, back_in, ray_gram, cell_gram, all_gram, high, low, w_slots,
    load_sem, send1, recv1, send2, recv2, send3, recv3, send4, recv4, send5, recv5, send6, recv6, send7, recv7,
):
    ray = lax.axis_index("ray")
    cell = lax.axis_index("cell")
    piece = pieces_in.shape[1]
    blocks = n_ray * piece

    early = [
        pltpu.make_async_copy(source, target, load_sem.at[2 + i])
        for i, (source, target) in enumerate(
            ((packet_hbm, packet_ref), (u_hbm, u_ref), (v_prev_hbm, v_prev_ref), (b_hbm, b_ref))
        )
    ]
    for load in early:
        load.start()
    loads = [
        pltpu.make_async_copy(high_hbm, high, load_sem.at[0]),
        pltpu.make_async_copy(low_hbm, low, load_sem.at[1]),
    ]
    for load in loads:
        load.start()

    barrier = pltpu.get_barrier_semaphore()

    each_peer(n_ray, lambda k: pl.semaphore_signal(barrier, inc=1, device_id={"ray": lax.rem(ray + k, n_ray)}, device_id_type=MESH))

    each_peer(n_cell, lambda k: pl.semaphore_signal(barrier, inc=1, device_id={"cell": lax.rem(cell + k, n_cell)}, device_id_type=MESH))

    pl.semaphore_wait(barrier, n_ray + n_cell - 2)

    def over(axis, me, n, source, target, send, recv):
        def copy(k):
            peer = lax.rem(me + k, n)
            return pltpu.make_async_remote_copy(
                src_ref=source(peer),
                dst_ref=target(me),
                send_sem=send.at[k - 1],
                recv_sem=recv.at[k - 1],
                device_id={axis: peer},
                device_id_type=MESH,
            )

        def wait_recv(k):
            origin = lax.rem(me + n - k, n)
            pltpu.make_async_remote_copy(
                src_ref=source(lax.rem(me + k, n)),
                dst_ref=target(origin),
                send_sem=send.at[k - 1],
                recv_sem=recv.at[k - 1],
                device_id={axis: lax.rem(me + k, n)},
                device_id_type=MESH,
            ).wait_recv()

        def receive():
            each_peer(n, wait_recv)

        def finish():
            each_peer(n, lambda k: copy(k).wait_send())

        return copy, receive, finish

    to_slab, from_slots, end1 = over(
        "cell", cell, n_cell, lambda peer: packet_ref.at[peer], lambda me: slots_in.at[me], send1, recv1
    )
    early[0].wait()
    each_peer(n_cell, lambda k: to_slab(k).start())
    for load in early[1:]:
        load.wait()
    slots_in[cell] = packet_ref[cell]
    from_slots()

    def index_tiles(p):
        tile = slots_in[p, CAP]
        return [row_of(tile, s) for s in range(CAP)]

    indices = [index_tiles(p) for p in range(n_cell)]

    def dense_block(b):
        number = jnp.full((8, 128), b, jnp.int32).astype(F32)
        total = jnp.zeros((8, 128), F32)
        for p in range(n_cell):
            for s in range(CAP):
                total = total + jnp.where(indices[p][s] == number, slots_in[p, s], 0.0)
        return total

    to_piece, from_pieces, end2 = over(
        "ray", ray, n_ray, lambda peer: part.at[peer], lambda me: pieces_in.at[me], send2, recv2
    )

    def send_piece(k):
        peer = lax.rem(ray + k, n_ray)
        for i in range(piece):
            part[peer, i] = dense_block(peer * piece + i)
        to_piece(k).start()

    each_peer(n_ray, send_piece)

    for i in range(piece):
        pieces_in[ray, i] = dense_block(ray * piece + i)

    b_columns = columns_of(b_ref[...])
    known = []
    for i in range(piece):
        at = pl.multiple_of((ray * piece + i) * 128, 128)
        known.append(apply(b_columns, v_prev_ref[:, pl.ds(at, 128)]))
    from_pieces()
    own = []
    for i in range(piece):
        total = pieces_in[0, i]
        for r in range(1, n_ray):
            total = total + pieces_in[r, i]
        own.append(total - known[i])
        slab_in[ray, i] = own[i]
    slab_in[ray, piece] = gram(own)

    to_ray, from_ray, end3 = over(
        "ray", ray, n_ray, lambda peer: slab_in.at[ray], lambda me: slab_in.at[me], send3, recv3
    )
    each_peer(n_ray, lambda k: to_ray(k).start())
    from_ray()

    slab_gram = slab_in[0, piece]
    for r in range(1, n_ray):
        slab_gram = slab_gram + slab_in[r, piece]

    def answer(p):
        wanted = index_tiles(p)
        found = [jnp.zeros((8, 128), F32) for s in range(CAP)]
        for b in range(blocks):
            block = slab_in[b // piece, b % piece]
            for s in range(CAP):
                found[s] = jnp.where(wanted[s] == float(b), block, found[s])
        return found

    to_cell, from_cell, end4 = over(
        "cell", cell, n_cell, lambda peer: back_out.at[peer], lambda me: back_in.at[me], send4, recv4
    )

    def send_answer(k):
        peer = lax.rem(cell + k, n_cell)
        found = answer(peer)
        for s in range(CAP):
            back_out[peer, s] = found[s]
        back_out[peer, CAP] = slab_gram
        to_cell(k).start()

    each_peer(n_cell, send_answer)

    found = answer(cell)
    for s in range(CAP):
        back_in[cell, s] = found[s]
    back_in[cell, CAP] = slab_gram
    for load in loads:
        load.wait()
    from_cell()

    whole_gram = back_in[0, CAP]
    for p in range(1, n_cell):
        whole_gram = whole_gram + back_in[p, CAP]
    for p in range(n_cell):
        for s in range(CAP):
            at = p * CAP + s
            w_slots[at // 2, :, (at % 2) * 128 : (at % 2 + 1) * 128] = back_in[p, s]
    across = (((1,), (1,)), ((), ()))

    def image_of(n):
        w_pair = split_rows(w_slots[n])
        both = lax.dot_general(w_pair, high[n], across, preferred_element_type=F32)
        rest = lax.dot_general(w_pair, low[n], across, preferred_element_type=F32)
        return both[:8] + (both[8:] + rest[:8])

    steps = high.shape[0]
    if steps <= UNROLL:
        image = image_of(0)
        for n in range(1, steps):
            image = image + image_of(n)
    else:
        image = lax.fori_loop(1, steps, lambda n, total: total + image_of(n), image_of(0))

    alpha, alpha_t, alpha_inverse = factor(whole_gram * (1.0 / cells_all))
    inverse_columns = columns_of(alpha_inverse)
    alpha_t_columns = columns_of(alpha_t)
    ray_blocks = u_ref.shape[1] // 128
    residual = []
    for i in range(ray_blocks):
        lanes = slice(i * 128, (i + 1) * 128)
        residual.append(apply(inverse_columns, image[:, lanes]) - apply(alpha_t_columns, u_ref[:, lanes]))
    everyone = n_ray * n_cell
    flat = ray * n_cell + cell
    own_gram = gram(residual)

    def gram_copy(k, back):
        peer = lax.rem(flat + k, everyone)
        slot = lax.rem(flat + everyone - k, everyone) if back else flat
        return pltpu.make_async_remote_copy(
            src_ref=all_gram.at[flat],
            dst_ref=all_gram.at[slot],
            send_sem=send7.at[k - 1],
            recv_sem=recv7.at[k - 1],
            device_id={"ray": lax.div(peer, n_cell), "cell": lax.rem(peer, n_cell)},
            device_id_type=MESH,
        )

    if everyone <= DIRECT:
        all_gram[flat] = own_gram
        for k in range(1, everyone):
            gram_copy(k, False).start()
    else:
        ray_gram[ray] = own_gram
        to_gram, from_gram, end5 = over(
            "ray", ray, n_ray, lambda peer: ray_gram.at[ray], lambda me: ray_gram.at[me], send5, recv5
        )
        each_peer(n_ray, lambda k: to_gram(k).start())

    small_ref[0] = alpha
    for i in range(ray_blocks):
        small_ref[2 + i] = residual[i]
    for b in range(blocks):
        v_ref[:, b * 128 : (b + 1) * 128] = apply(inverse_columns, slab_in[b // piece, b % piece])
    store = pltpu.make_async_copy(v_ref, v_hbm, load_sem.at[6])
    store.start()

    if everyone <= DIRECT:
        for k in range(1, everyone):
            gram_copy(k, True).wait_recv()
        total = all_gram[0]
        for d in range(1, everyone):
            total = total + all_gram[d]
    else:
        from_gram()
        total = ray_gram[0]
        for r in range(1, n_ray):
            total = total + ray_gram[r]
        cell_gram[cell] = total
        to_total, from_total, end6 = over(
            "cell", cell, n_cell, lambda peer: cell_gram.at[cell], lambda me: cell_gram.at[me], send6, recv6
        )
        each_peer(n_cell, lambda k: to_total(k).start())
        from_total()
        total = cell_gram[0]
        for p in range(1, n_cell):
            total = total + cell_gram[p]
    small_ref[1] = total * (1.0 / rays_all)
    store.wait()
    for end in (end1, end2, end3, end4):
        end()
    if everyone <= DIRECT:
        for k in range(1, everyone):
            gram_copy(k, False).wait_send()
    else:
        end5()
        end6()


def cholesky(tile, count=8):
    row = lax.broadcasted_iota(jnp.int32, (8, 128), 0)
    rest = [column_of(tile, k) for k in range(count)]
    lower, scales = [], []
    for j in range(count):
        scale = lax.rsqrt(row_of(rest[j], j))
        column = jnp.where(row >= j, rest[j] * scale, 0.0)
        lower.append(column)
        scales.append(scale)
        for k in range(j + 1, count):
            rest[k] = rest[k] - column * row_of(column, k)
    return lower, scales


def across_of(columns):
    lane = lax.broadcasted_iota(jnp.int32, (8, 128), 1)
    tile = jnp.zeros((8, 128), F32)
    for k, column in enumerate(columns):
        tile = jnp.where(lane == k, column, tile)
    return tile


def transposed(columns):
    row = lax.broadcasted_iota(jnp.int32, (8, 128), 0)
    turned = []
    for k in range(len(columns)):
        column = jnp.zeros((8, 128), F32)
        for i in range(k + 1):
            column = jnp.where(row == i, row_of(columns[i], k), column)
        turned.append(column)
    return turned


def solve(lower, scales, block):
    row = lax.broadcasted_iota(jnp.int32, (8, 128), 0)
    found = block
    for j, (column, scale) in enumerate(zip(lower, scales)):
        value = row_of(block, j) * scale
        found = jnp.where(row == j, value, found)
        block = block - column * value
    return found


def last_kernel(v_hbm, small_hbm, v_out, u_out, alpha_out, beta_out, v_ref, small, u_ref, alpha_ref, beta_ref, sems):
    load = pltpu.make_async_copy(small_hbm, small, sems.at[0])
    v_load = pltpu.make_async_copy(v_hbm, v_ref, sems.at[1])
    load.start()
    v_load.start()
    stores = [
        pltpu.make_async_copy(source, target, sems.at[2 + i])
        for i, (source, target) in enumerate(
            ((v_ref, v_out), (alpha_ref, alpha_out), (beta_ref, beta_out), (u_ref, u_out))
        )
    ]
    load.wait()
    alpha_ref[...] = small[0][:, :8]
    stores[1].start()
    v_load.wait()
    stores[0].start()
    lower, scales = cholesky(small[1])
    beta_ref[...] = across_of(lower)[:, :8]
    for i in range(small.shape[0] - 2):
        u_ref[:, i * 128 : (i + 1) * 128] = solve(lower, scales, small[2 + i])
    stores[2].start()
    stores[3].start()
    for store in stores:
        store.wait()


def flips_of(index, count):
    flips, bit = {}, 1
    while bit < count:
        flips[bit] = bit * (1 - 2 * lax.rem(lax.div(index, bit), 2))
        bit *= 2
    return flips


def flipped(index, flips, mask):
    for bit, step in flips.items():
        if mask & bit:
            index = index + step
    return index


def far_first(n_ray, n_cell):
    masks = [(2 * a, c) for a in range(n_ray // 2) for c in range(n_cell) if a or c]
    return sorted(masks, key=lambda m: -(8 * (m[1] >= 2) + 2 * bin(m[0]).count("1") + m[1]))


def halves_of(value):
    high = value.astype(BF16)
    return high, (value - high.astype(F32)).astype(BF16)


def fused_kernel(
    n_ray, n_cell, cells_all, rays_all,
    group_hbm, slot_hbm, block_hbm, tiles_hbm, u_hbm, v_prev_hbm, b_hbm,
    v_hbm, small_ref,
    group_ref, slot_ref, block_ref, asked_ref, index_out, index_in, tiles, u_ref, v_prev_ref, b_ref,
    u_left, u_right, gather, products, split, turned, pick, packet, recv, part, part_in, known, w_ref,
    back_out, back_in, gram_out, gram_in, w_slots, pair_gram, all_gram, v_ref,
    tile_sem, load_sem, send1, recv1, send2, recv2, send3, recv3, send4, recv4, send5, recv5, send6, recv6, send7, recv7,
):
    ray = lax.axis_index("ray")
    cell = lax.axis_index("cell")
    tile_count, tile_rays, width = tiles.shape
    slots = block_ref.shape[1]
    comps = u_ref.shape[0]
    sources = n_ray // 2 * n_cell
    blocks = w_ref.shape[0]
    steps, span = split.shape[0], split.shape[1]
    chunks = tile_sem.shape[0]
    per_chunk = tile_count // chunks
    per_step = steps // chunks
    quad = span // tile_rays

    small_loads = [
        pltpu.make_async_copy(source, target, load_sem.at[i])
        for i, (source, target) in enumerate(
            (
                (block_hbm, block_ref), (u_hbm, u_ref), (slot_hbm, slot_ref), (group_hbm, group_ref),
                (v_prev_hbm, v_prev_ref), (b_hbm, b_ref),
            )
        )
    ]

    def chunk(i):
        rows = pl.ds(i * per_chunk, per_chunk)
        return pltpu.make_async_copy(tiles_hbm.at[rows], tiles.at[rows], tile_sem.at[i])

    for load in small_loads[:4]:
        load.start()
    for i in range(chunks):
        chunk(i).start()
    for load in small_loads[4:]:
        load.start()

    ray_flips = flips_of(ray, n_ray)
    cell_flips = flips_of(cell, n_cell)
    masks = far_first(n_ray, n_cell)
    peers = [(flipped(ray, ray_flips, a), flipped(cell, cell_flips, c)) for a, c in masks]
    twin = ray + ray_flips[1]
    cell_masks = list(range(n_cell - 1, 0, -1))
    cell_peers = [flipped(cell, cell_flips, c) for c in cell_masks]

    def number_of(ray_at, cell_at):
        return lax.div(ray_at, 2) * n_cell + cell_at

    me = number_of(ray, cell)

    barrier = pltpu.get_barrier_semaphore()
    for r, c in peers + [(twin, cell)]:
        pl.semaphore_signal(barrier, inc=1, device_id={"ray": r, "cell": c}, device_id_type=MESH)

    def remote(source, target, send, recv_at, r, c):
        return pltpu.make_async_remote_copy(
            src_ref=source, dst_ref=target, send_sem=send, recv_sem=recv_at,
            device_id={"ray": r, "cell": c}, device_id_type=MESH,
        )

    small_loads[0].wait()
    lane = lax.broadcasted_iota(jnp.int32, (8, width), 1)
    bands = sources * CAP * comps // width
    band = lax.broadcasted_iota(jnp.int32, (bands, width), 0)
    place = band * width + lax.broadcasted_iota(jnp.int32, (bands, width), 1) - me * CAP * comps
    for p in range(n_cell):
        index = jnp.zeros((bands, width), jnp.int32)
        for s in range(CAP):
            b = block_ref[0, p * CAP + s]
            first_row = jnp.where(b < 0, -comps - 1, (b - s) * comps + 1)
            inside = (place >= s * comps) & (place < (s + 1) * comps)
            index = jnp.where(inside, jnp.maximum(place + first_row, 0), index)
        index_out[p] = index
    index_in[me] = index_out[cell]

    def announce():
        pl.semaphore_wait(barrier, len(peers) + 1)

    indices = [
        remote(index_out.at[c], index_in.at[me], send2.at[i], recv2.at[i], r, c) for i, (r, c) in enumerate(peers)
    ]

    for load in small_loads[1:4]:
        load.wait()
    low = lane < tile_rays
    low_pair = lax.broadcasted_iota(jnp.int32, (2 * comps, width), 1) < tile_rays
    for q in range(u_ref.shape[1] // width):
        block = u_ref[:, q * width : (q + 1) * width]
        turn = pltpu.roll(block, tile_rays, 1)
        for half, (left, right) in enumerate(((block, turn), (turn, block))):
            u_left[2 * q + half] = split_rows(jnp.where(low, left, 0.0))
            u_right[2 * q + half] = split_rows(jnp.where(low, 0.0, right))

    per_band = width // comps
    lane_tile = lax.div(lane, comps)
    slot_row = lax.broadcasted_iota(jnp.int32, (slots * comps, width), 0)
    offset = lax.rem(lane, comps)
    for q in range(tile_count // per_band):
        owner = jnp.zeros((8, width), jnp.int32)
        for t in range(per_band):
            owner = jnp.where(lane_tile == t, slot_ref[0, q * per_band + t], owner)
        owner = jnp.broadcast_to((owner * comps + offset)[:1], slot_row.shape)
        gather[:, q * width : (q + 1) * width] = jnp.where(slot_row == owner, 1.0, 0.0).astype(BF16)

    nothing = jnp.zeros((2 * quad // 2 * comps, width), BF16)
    for i in range(chunks):
        if i == ANNOUNCE:
            announce()
        chunk(i).wait()
        for n in range(i * per_step, (i + 1) * per_step):
            value = tiles[n * quad : (n + 1) * quad].reshape(span, width)
            high, rest = halves_of(value)
            both = jnp.concatenate([high, rest], axis=1)
            split[n] = both
            columns = []
            for h in range(2):
                at = n * quad + 2 * h
                own = jnp.concatenate([u_left[group_ref[0, at]], u_right[group_ref[0, at + 1]]], axis=0)
                columns.append(jnp.concatenate([own, nothing] if h == 0 else [nothing, own], axis=0))
            product = jnp.dot(jnp.concatenate(columns, axis=1), both, preferred_element_type=F32)
            product = (product[:, :width] + product[:, width:]).reshape(quad, 2 * comps, width)
            product = (product[:, :comps] + product[:, comps:]).reshape(quad * comps, width)
            high, rest = halves_of(product)
            products[n * quad * comps : (n + 1) * quad * comps] = jnp.concatenate([high, rest], axis=1)

    slot_sums = jnp.dot(gather[...], products[...], preferred_element_type=F32)
    packet[...] = (slot_sums[:, :width] + slot_sums[:, width:]).reshape(packet.shape)
    recv[me] = packet[cell]

    if ANNOUNCE >= chunks:
        announce()
    half = n_cell // 2
    passed = [(a, c) for a, c in masks if c >= half and a]
    sent = [i for i, mask in enumerate(masks) if mask not in passed]
    sent.sort(key=lambda i: (masks[i][1] < half, ORDER * bin(masks[i][0]).count("1") - masks[i][1]))
    first = [remote(packet.at[peers[i][1]], recv.at[me], send1.at[i], recv1.at[i], *peers[i]) for i in sent]
    for copy in first + indices:
        copy.start()

    def pass_on(mask, c):
        i = masks.index(mask)
        source = recv.at[number_of(ray, c)]
        return remote(source, source, send1.at[i], recv1.at[i], flipped(ray, ray_flips, mask[0]), cell)

    for load in small_loads[4:]:
        load.wait()
    b_columns = columns_of(b_ref[...])
    for b in range(blocks):
        known[b] = apply(b_columns, v_prev_ref[:, b * width : (b + 1) * width])

    @pl.loop(0, steps // 2)
    def _(n):
        turned[n] = split[n].T

    arrived = [i for i in sent if masks[i][0] == 0 and masks[i][1] >= half]
    for i in arrived[::-1]:
        r, c = peers[i]
        remote(packet.at[c], recv.at[number_of(r, c)], send1.at[i], recv1.at[i], r, c).wait_recv()
        for mask in passed:
            if mask[1] == masks[i][1]:
                copy = pass_on(mask, c)
                copy.start()
                first.append(copy)

    @pl.loop(steps // 2, steps)
    def _(n):
        turned[n] = split[n].T

    for i, (r, c) in enumerate(peers):
        remote(index_out.at[c], index_in.at[number_of(r, c)], send2.at[i], recv2.at[i], r, c).wait_recv()
    ask_load = pltpu.make_async_copy(index_in, asked_ref, load_sem.at[6])
    ask_load.start()
    asked = index_in[0]
    for d in range(1, sources):
        asked = asked + index_in[d]
    row = lax.broadcasted_iota(jnp.int32, (blocks * comps, width), 0) + 1
    for q in range(bands):
        wanted = jnp.broadcast_to(asked[q : q + 1], (blocks * comps, width))
        pick[:, q * width : (q + 1) * width] = jnp.where(row == wanted, 1.0, 0.0).astype(BF16)
    ask_load.wait()

    for i, (r, c) in enumerate(peers):
        if i not in arrived:
            remote(packet.at[c], recv.at[number_of(r, c)], send1.at[i], recv1.at[i], r, c).wait_recv()

    received = recv[...].reshape(sources * CAP * comps, width)
    high, rest = halves_of(received)
    both = jnp.concatenate([high, rest], axis=1)
    swaps = []
    section = blocks // SWAPS
    for i in range(SWAPS):
        rows = pl.ds(i * section, section)
        added = jnp.dot(pick[i * section * comps : (i + 1) * section * comps], both, preferred_element_type=F32)
        part[rows] = (added[:, :width] + added[:, width:]).reshape(section, comps, width)
        swaps.append(remote(part.at[rows], part_in.at[rows], send3.at[i], recv3.at[i], twin, cell))
        swaps[i].start()
    for copy in swaps:
        copy.wait_recv()
    def block_of(b):
        return part[b] + part_in[b] - known[b]

    answers = []
    for i, c in enumerate(cell_peers):
        for s in range(CAP):
            at = (number_of(ray, c) * CAP + s) * comps
            row_at = asked_ref[number_of(ray, c), lax.div(at, width), lax.rem(at, width)]
            back_out[i, s] = block_of(lax.div(jnp.maximum(row_at - 1, 0), comps))
        answers.append(remote(back_out.at[i], back_in.at[cell], send4.at[i], recv4.at[i], ray, c))
        answers[i].start()
    for s in range(CAP):
        back_in[cell, s] = block_of(jnp.maximum(block_ref[0, cell * CAP + s], 0))
    for b in range(blocks):
        w_ref[b] = block_of(b)

    slab_gram = gram([w_ref[b] for b in range(blocks)])
    gram_out[...] = slab_gram
    gram_in[cell] = slab_gram
    grams = [
        remote(gram_out, gram_in.at[cell], send5.at[i], recv5.at[i], ray, c) for i, c in enumerate(cell_peers)
    ]
    for copy in grams:
        copy.start()

    for i, c in enumerate(cell_peers):
        remote(back_out.at[i], back_in.at[c], send4.at[i], recv4.at[i], ray, c).wait_recv()
    for p in range(n_cell):
        for s in range(CAP):
            w_slots[p * CAP + s] = split_rows(back_in[p, s])

    groups = u_ref.shape[1] // tile_rays
    totals = [jnp.zeros((8, width), F32) for g in range(groups)]
    for n in range(steps):
        at = n * quad
        rows = jnp.concatenate([w_slots[slot_ref[0, at + j]] for j in range(quad)], axis=0)
        found = jnp.dot(jnp.concatenate([rows, rows], axis=1), turned[n], preferred_element_type=F32)
        for j in range(quad // 2):
            lanes = slice(j * width, (j + 1) * width)
            top = 2 * j * 2 * comps
            pair = jnp.where(
                low_pair, found[top : top + 2 * comps, lanes], found[top + 2 * comps : top + 4 * comps, lanes]
            )
            pair = pair[:comps] + pair[comps:]
            owner = jnp.where(low, group_ref[0, at + 2 * j], group_ref[0, at + 2 * j + 1])
            for g in range(groups):
                totals[g] = totals[g] + jnp.where(owner == g, pair, 0.0)

    for i, c in enumerate(cell_peers):
        remote(gram_out, gram_in.at[c], send5.at[i], recv5.at[i], ray, c).wait_recv()
    whole_gram = gram_in[0]
    for p in range(1, n_cell):
        whole_gram = whole_gram + gram_in[p]
    lower, scales = cholesky(whole_gram * (1.0 / cells_all))
    alpha_t_columns = transposed(lower)
    totals = [total + pltpu.roll(total, tile_rays, 1) for total in totals]
    ray_blocks = u_ref.shape[1] // width
    residual = []
    for i in range(ray_blocks):
        image = jnp.where(low, totals[2 * i], totals[2 * i + 1])
        lanes = slice(i * width, (i + 1) * width)
        residual.append(solve(lower, scales, image) - apply(alpha_t_columns, u_ref[:, lanes]))
    pair_gram[0] = gram(residual)
    pairs = remote(pair_gram.at[0], pair_gram.at[1], send6.at[0], recv6.at[0], twin, cell)
    pairs.start()
    small_ref[0] = across_of(lower)
    for i in range(ray_blocks):
        small_ref[2 + i] = residual[i]
    pairs.wait_recv()
    all_gram[me] = pair_gram[0] + pair_gram[1]
    last = [
        remote(all_gram.at[me], all_gram.at[me], send7.at[i], recv7.at[i], r, c) for i, (r, c) in enumerate(peers)
    ]
    for copy in last:
        copy.start()
    for b in range(blocks):
        v_ref[:, b * width : (b + 1) * width] = solve(lower, scales, w_ref[b])
    store = pltpu.make_async_copy(v_ref, v_hbm, load_sem.at[8])
    store.start()
    for copy in first + indices + swaps + answers + grams + [pairs] + last:
        copy.wait_send()
    store.wait()
    for i, (r, c) in enumerate(peers):
        remote(all_gram.at[me], all_gram.at[number_of(r, c)], send7.at[i], recv7.at[i], r, c).wait_recv()
    total = all_gram[0]
    for d in range(1, sources):
        total = total + all_gram[d]
    small_ref[1] = total * (1.0 / rays_all)


def fused(n_ray, n_cell, ray_tiles, tile_group, tile_slot, slot_block, u_basis, v_prev, b_prev):
    tile_count, tile_rays, width = ray_tiles.shape
    comps, rays = u_basis.shape
    slots = slot_block.shape[1]
    blocks = v_prev.shape[1] // width
    sources = n_ray // 2 * n_cell
    bands = sources * CAP * comps // width
    steps = tile_count * tile_rays // (2 * width)
    vmem = pl.BlockSpec(memory_space=pltpu.VMEM)
    anywhere = pl.BlockSpec(memory_space=pl.ANY)
    tile = (comps, width)
    one = pltpu.SemaphoreType.DMA((1,))
    parts = pltpu.SemaphoreType.DMA((SWAPS,))
    far = pltpu.SemaphoreType.DMA((sources - 1,))
    cells = pltpu.SemaphoreType.DMA((n_cell - 1,))
    return pl.pallas_call(
        functools.partial(fused_kernel, n_ray, n_cell, v_prev.shape[1] * n_cell, rays * n_ray * n_cell),
        out_shape=(
            jax.ShapeDtypeStruct(v_prev.shape, F32),
            jax.ShapeDtypeStruct((2 + rays // width,) + tile, F32),
        ),
        in_specs=[anywhere] * 7,
        out_specs=(anywhere, vmem),
        scratch_shapes=[
            pltpu.SMEM(tile_group.shape, jnp.int32),
            pltpu.SMEM(tile_slot.shape, jnp.int32),
            pltpu.SMEM(slot_block.shape, jnp.int32),
            pltpu.SMEM((sources, bands, width), jnp.int32),
            pltpu.VMEM((n_cell, bands, width), jnp.int32),
            pltpu.VMEM((sources, bands, width), jnp.int32),
            pltpu.VMEM(ray_tiles.shape, F32),
            pltpu.VMEM(u_basis.shape, F32),
            pltpu.VMEM(v_prev.shape, F32),
            pltpu.VMEM(b_prev.shape, F32),
            pltpu.VMEM((rays // tile_rays, 2 * comps, width), BF16),
            pltpu.VMEM((rays // tile_rays, 2 * comps, width), BF16),
            pltpu.VMEM((slots * comps, tile_count * comps), BF16),
            pltpu.VMEM((tile_count * comps, 2 * width), BF16),
            pltpu.VMEM((steps, 2 * width, 2 * width), BF16),
            pltpu.VMEM((steps, 2 * width, 2 * width), BF16),
            pltpu.VMEM((blocks * comps, sources * CAP * comps), BF16),
            pltpu.VMEM((n_cell, CAP * comps, width), F32),
            pltpu.VMEM((sources, CAP * comps, width), F32),
            pltpu.VMEM((blocks,) + tile, F32),
            pltpu.VMEM((blocks,) + tile, F32),
            pltpu.VMEM((blocks,) + tile, F32),
            pltpu.VMEM((blocks,) + tile, F32),
            pltpu.VMEM((n_cell - 1, CAP) + tile, F32),
            pltpu.VMEM((n_cell, CAP) + tile, F32),
            pltpu.VMEM(tile, F32),
            pltpu.VMEM((n_cell,) + tile, F32),
            pltpu.VMEM((slots, 2 * comps, width), BF16),
            pltpu.VMEM((2,) + tile, F32),
            pltpu.VMEM((sources,) + tile, F32),
            pltpu.VMEM(v_prev.shape, F32),
            pltpu.SemaphoreType.DMA((CHUNKS,)),
            pltpu.SemaphoreType.DMA((9,)),
            far, far, far, far, parts, parts, cells, cells, cells, cells, one, one, far, far,
        ],
        compiler_params=pltpu.CompilerParams(
            collective_id=0, has_side_effects=True, vmem_limit_bytes=56 << 20
        ),
    )(tile_group, tile_slot, slot_block, ray_tiles, u_basis, v_prev, b_prev)


def per_device(n_ray, n_cell, ray_tiles, tile_group, tile_slot, slot_block, u_basis, v_prev, b_prev):
    tile_count, tile_rays, width = ray_tiles.shape
    comps, rays = u_basis.shape
    slots = slot_block.shape[1]
    blocks = v_prev.shape[1] // width
    piece = blocks // n_ray
    vmem = pl.BlockSpec(memory_space=pltpu.VMEM)
    smem = pl.BlockSpec(memory_space=pltpu.SMEM)
    anywhere = pl.BlockSpec(memory_space=pl.ANY)
    tile = (comps, width)
    packets = (n_cell, CAP + 1) + tile
    limit = 56 << 20
    small_shape = (2 + rays // width,) + tile
    if n_ray * n_cell <= DIRECT:
        v_next, small = fused(n_ray, n_cell, ray_tiles, tile_group, tile_slot, slot_block, u_basis, v_prev, b_prev)
    else:
        packet, high, low = pl.pallas_call(
            local_kernel,
            out_shape=(
                jax.ShapeDtypeStruct(packets, F32),
                jax.ShapeDtypeStruct((slots // 2, rays, 2 * width), BF16),
                jax.ShapeDtypeStruct((slots // 2, rays, 2 * width), BF16),
            ),
            in_specs=[smem, smem, smem, anywhere, vmem],
            out_specs=(vmem, anywhere, anywhere),
            scratch_shapes=[
                pltpu.VMEM(ray_tiles.shape, F32),
                pltpu.VMEM((rays, slots * width), F32),
                pltpu.VMEM((slots // 2, rays, 2 * width), BF16),
                pltpu.VMEM((slots // 2, rays, 2 * width), BF16),
                pltpu.SemaphoreType.DMA((CHUNKS,)),
                pltpu.SemaphoreType.DMA((2, slots // 2)),
            ],
            compiler_params=pltpu.CompilerParams(vmem_limit_bytes=limit),
        )(tile_group, tile_slot, slot_block, ray_tiles, u_basis)

        ray_sem = pltpu.SemaphoreType.DMA((n_ray - 1,))
        direct = min(n_ray * n_cell, DIRECT)
        all_sem = pltpu.SemaphoreType.DMA((direct - 1,))
        cell_sem = pltpu.SemaphoreType.DMA((n_cell - 1,))
        v_next, small = pl.pallas_call(
            functools.partial(step_kernel, n_ray, n_cell, v_prev.shape[1] * n_cell, rays * n_ray * n_cell),
            out_shape=(jax.ShapeDtypeStruct(v_prev.shape, F32), jax.ShapeDtypeStruct(small_shape, F32)),
            in_specs=[anywhere] * 6,
            out_specs=(anywhere, vmem),
            scratch_shapes=[
                pltpu.VMEM(packets, F32),
                pltpu.VMEM(u_basis.shape, F32),
                pltpu.VMEM(v_prev.shape, F32),
                pltpu.VMEM(b_prev.shape, F32),
                pltpu.VMEM(v_prev.shape, F32),
                pltpu.VMEM(packets, F32),
                pltpu.VMEM((n_ray, piece) + tile, F32),
                pltpu.VMEM((n_ray, piece) + tile, F32),
                pltpu.VMEM((n_ray, piece + 1) + tile, F32),
                pltpu.VMEM(packets, F32),
                pltpu.VMEM(packets, F32),
                pltpu.VMEM((n_ray,) + tile, F32),
                pltpu.VMEM((n_cell,) + tile, F32),
                pltpu.VMEM((direct,) + tile, F32),
                pltpu.VMEM((slots // 2, rays, 2 * width), BF16),
                pltpu.VMEM((slots // 2, rays, 2 * width), BF16),
                pltpu.VMEM((slots // 2, comps, 2 * width), F32),
                pltpu.SemaphoreType.DMA((7,)),
                cell_sem, cell_sem, ray_sem, ray_sem, ray_sem, ray_sem,
                cell_sem, cell_sem, ray_sem, ray_sem, cell_sem, cell_sem, all_sem, all_sem,
            ],
            compiler_params=pltpu.CompilerParams(
                collective_id=0, has_side_effects=True, vmem_limit_bytes=limit
            ),
        )(packet, high, low, u_basis, v_prev, b_prev)
    return pl.pallas_call(
        last_kernel,
        out_shape=(
            jax.ShapeDtypeStruct(v_prev.shape, F32),
            jax.ShapeDtypeStruct(u_basis.shape, F32),
            jax.ShapeDtypeStruct((comps, comps), F32),
            jax.ShapeDtypeStruct((comps, comps), F32),
        ),
        in_specs=[anywhere, anywhere],
        out_specs=(anywhere, anywhere, anywhere, anywhere),
        scratch_shapes=[
            pltpu.VMEM(v_prev.shape, F32),
            pltpu.VMEM(small_shape, F32),
            pltpu.VMEM(u_basis.shape, F32),
            pltpu.VMEM((comps, comps), F32),
            pltpu.VMEM((comps, comps), F32),
            pltpu.SemaphoreType.DMA((6,)),
        ],
    )(v_next, small)


def solution(mesh):
    in_specs = (
        P(("ray", "cell"), None, None),
        P(("ray", "cell"), None),
        P(("ray", "cell"), None),
        P(("ray", "cell"), None),
        P(None, ("ray", "cell")),
        P(None, "cell"),
        P(),
    )
    out_specs = (P(None, "cell"), P(None, ("ray", "cell")), P(), P())
    return jax.shard_map(
        functools.partial(per_device, mesh.shape["ray"], mesh.shape["cell"]),
        mesh=mesh,
        in_specs=in_specs,
        out_specs=out_specs,
        check_vma=False,
    )
```

```python
import functools

import jax
import jax.numpy as jnp
from jax import lax
from jax.experimental import pallas as pl
from jax.experimental.pallas import tpu as pltpu
from jax.sharding import PartitionSpec as P

CAP = 4
GROUPS = 8
CHUNKS = 3
UNROLL = 8
DIRECT = 32
SWAPS = 1
ORDER = -1
ANNOUNCE = 3
BATCH = 4
MESH = pl.DeviceIdType.MESH
F32 = jnp.float32
BF16 = jnp.bfloat16


def split_rows(value):
    high = value.astype(BF16).astype(F32)
    return jnp.concatenate([high, value - high], axis=0).astype(BF16)


def local_kernel(group_ref, slot_ref, block_ref, tiles_hbm, u_ref, packet_ref, high_hbm, low_hbm, tiles, dense, high_ref, low_ref, sems, out_sems):
    tile_count, tile_rays, width = tiles.shape
    slots = block_ref.shape[1]
    per_chunk = tile_count // CHUNKS

    def chunk(i):
        rows = pl.ds(i * per_chunk, per_chunk)
        return pltpu.make_async_copy(tiles_hbm.at[rows], tiles.at[rows], sems.at[i])

    for i in range(CHUNKS):
        chunk(i).start()

    row = lax.broadcasted_iota(jnp.int32, (8, width), 0)
    for p in range(slots // CAP):
        index = jnp.full((8, width), -1, jnp.int32)
        for s in range(CAP):
            index = jnp.where(row == s, block_ref[0, p * CAP + s], index)
        packet_ref[p, CAP] = index.astype(F32)

    @pl.loop(0, slots)
    def _(s):
        dense[:, pl.ds(pl.multiple_of(s * width, width), width)] = jnp.zeros((dense.shape[0], width), F32)

    for i in range(CHUNKS):
        chunk(i).wait()

        @pl.loop(0, per_chunk // BATCH)
        def _(at):
            first = i * per_chunk + at * BATCH
            where = [(group_ref[0, first + n], slot_ref[0, first + n]) for n in range(BATCH)]
            values = [tiles[first + n] for n in range(BATCH)]
            for (group, slot), value in zip(where, values):
                rows = pl.ds(pl.multiple_of(group * tile_rays, tile_rays), tile_rays)
                columns = pl.ds(pl.multiple_of(slot * width, width), width)
                dense[rows, columns] += value

    u_pair = split_rows(u_ref[...])
    comps = u_ref.shape[0]
    span = 2 * width

    def stores(n):
        return [
            pltpu.make_async_copy(source.at[n], target.at[n], out_sems.at[at, n])
            for at, (source, target) in enumerate(((high_ref, high_hbm), (low_ref, low_hbm)))
        ]

    def product(n):
        columns = pl.ds(pl.multiple_of(n * span, span), span)
        block = dense[:, columns]
        high = block.astype(BF16)
        low = (block - high.astype(F32)).astype(BF16)
        high_ref[n] = high
        low_ref[n] = low
        for store in stores(n):
            store.start()
        both = jnp.dot(u_pair, high, preferred_element_type=F32)
        rest = jnp.dot(u_pair, low, preferred_element_type=F32)
        total = both[:comps] + (both[comps:] + rest[:comps])
        for half in range(2):
            s = 2 * n + half
            packet_ref[s // CAP, s % CAP] = total[:, half * width : (half + 1) * width]

    def finish(n):
        for store in stores(n):
            store.wait()

    each_peer(slots // 2, product, 0)
    each_peer(slots // 2, finish, 0)


def each_peer(n, body, first=1):
    if n <= UNROLL:
        for k in range(first, n):
            body(k)
    else:
        pl.loop(first, n)(body)


def row_of(tile, k):
    return jnp.broadcast_to(tile[k : k + 1, :], tile.shape)


def column_of(tile, k):
    return jnp.broadcast_to(tile[:, k : k + 1], (tile.shape[0], 128))


def gram(blocks):
    lane = lax.broadcasted_iota(jnp.int32, (8, 128), 1)
    tile = jnp.zeros((8, 128), F32)
    for j in range(8):
        products = blocks[0] * row_of(blocks[0], j)
        for block in blocks[1:]:
            products = products + block * row_of(block, j)
        tile = jnp.where(lane == j, jnp.sum(products, axis=1, keepdims=True), tile)
    return tile


def factor(tile):
    row = lax.broadcasted_iota(jnp.int32, (8, 128), 0)
    lane = lax.broadcasted_iota(jnp.int32, (8, 128), 1)
    lower = jnp.zeros((8, 128), F32)
    upper = jnp.zeros((8, 128), F32)
    inverse = jnp.where(row == lane, 1.0, 0.0).astype(F32)
    for j in range(8):
        across = row_of(tile, j)
        down = column_of(tile, j)
        scale = 1.0 / jnp.sqrt(row_of(down, j))
        across = across * scale
        down = jnp.where(row >= j, down * scale, 0.0)
        lower = jnp.where(lane == j, down, lower)
        upper = jnp.where((row == j) & (lane >= j), across, upper)
        tile = tile - down * across
        pivot = row_of(inverse, j) * scale
        inverse = jnp.where(row == j, pivot, inverse - jnp.where(row > j, down, 0.0) * pivot)
    return lower, upper, inverse


def columns_of(tile):
    return [column_of(tile, k) for k in range(8)]


def apply(columns, block):
    total = columns[0] * row_of(block, 0)
    for k in range(1, 8):
        total = total + columns[k] * row_of(block, k)
    return total


def step_kernel(
    n_ray, n_cell, cells_all, rays_all,
    packet_hbm, high_hbm, low_hbm, u_hbm, v_prev_hbm, b_hbm,
    v_hbm, small_ref,
    packet_ref, u_ref, v_prev_ref, b_ref, v_ref, slots_in, part, pieces_in, slab_in, back_out, back_in, ray_gram, cell_gram, all_gram, high, low, w_slots,
    load_sem, send1, recv1, send2, recv2, send3, recv3, send4, recv4, send5, recv5, send6, recv6, send7, recv7,
):
    ray = lax.axis_index("ray")
    cell = lax.axis_index("cell")
    piece = pieces_in.shape[1]
    blocks = n_ray * piece

    early = [
        pltpu.make_async_copy(source, target, load_sem.at[2 + i])
        for i, (source, target) in enumerate(
            ((packet_hbm, packet_ref), (u_hbm, u_ref), (v_prev_hbm, v_prev_ref), (b_hbm, b_ref))
        )
    ]
    for load in early:
        load.start()
    loads = [
        pltpu.make_async_copy(high_hbm, high, load_sem.at[0]),
        pltpu.make_async_copy(low_hbm, low, load_sem.at[1]),
    ]
    for load in loads:
        load.start()

    barrier = pltpu.get_barrier_semaphore()

    each_peer(n_ray, lambda k: pl.semaphore_signal(barrier, inc=1, device_id={"ray": lax.rem(ray + k, n_ray)}, device_id_type=MESH))

    each_peer(n_cell, lambda k: pl.semaphore_signal(barrier, inc=1, device_id={"cell": lax.rem(cell + k, n_cell)}, device_id_type=MESH))

    pl.semaphore_wait(barrier, n_ray + n_cell - 2)

    def over(axis, me, n, source, target, send, recv):
        def copy(k):
            peer = lax.rem(me + k, n)
            return pltpu.make_async_remote_copy(
                src_ref=source(peer),
                dst_ref=target(me),
                send_sem=send.at[k - 1],
                recv_sem=recv.at[k - 1],
                device_id={axis: peer},
                device_id_type=MESH,
            )

        def wait_recv(k):
            origin = lax.rem(me + n - k, n)
            pltpu.make_async_remote_copy(
                src_ref=source(lax.rem(me + k, n)),
                dst_ref=target(origin),
                send_sem=send.at[k - 1],
                recv_sem=recv.at[k - 1],
                device_id={axis: lax.rem(me + k, n)},
                device_id_type=MESH,
            ).wait_recv()

        def receive():
            each_peer(n, wait_recv)

        def finish():
            each_peer(n, lambda k: copy(k).wait_send())

        return copy, receive, finish

    to_slab, from_slots, end1 = over(
        "cell", cell, n_cell, lambda peer: packet_ref.at[peer], lambda me: slots_in.at[me], send1, recv1
    )
    early[0].wait()
    each_peer(n_cell, lambda k: to_slab(k).start())
    for load in early[1:]:
        load.wait()
    slots_in[cell] = packet_ref[cell]
    from_slots()

    def index_tiles(p):
        tile = slots_in[p, CAP]
        return [row_of(tile, s) for s in range(CAP)]

    indices = [index_tiles(p) for p in range(n_cell)]

    def dense_block(b):
        number = jnp.full((8, 128), b, jnp.int32).astype(F32)
        total = jnp.zeros((8, 128), F32)
        for p in range(n_cell):
            for s in range(CAP):
                total = total + jnp.where(indices[p][s] == number, slots_in[p, s], 0.0)
        return total

    to_piece, from_pieces, end2 = over(
        "ray", ray, n_ray, lambda peer: part.at[peer], lambda me: pieces_in.at[me], send2, recv2
    )

    def send_piece(k):
        peer = lax.rem(ray + k, n_ray)
        for i in range(piece):
            part[peer, i] = dense_block(peer * piece + i)
        to_piece(k).start()

    each_peer(n_ray, send_piece)

    for i in range(piece):
        pieces_in[ray, i] = dense_block(ray * piece + i)

    b_columns = columns_of(b_ref[...])
    known = []
    for i in range(piece):
        at = pl.multiple_of((ray * piece + i) * 128, 128)
        known.append(apply(b_columns, v_prev_ref[:, pl.ds(at, 128)]))
    from_pieces()
    own = []
    for i in range(piece):
        total = pieces_in[0, i]
        for r in range(1, n_ray):
            total = total + pieces_in[r, i]
        own.append(total - known[i])
        slab_in[ray, i] = own[i]
    slab_in[ray, piece] = gram(own)

    to_ray, from_ray, end3 = over(
        "ray", ray, n_ray, lambda peer: slab_in.at[ray], lambda me: slab_in.at[me], send3, recv3
    )
    each_peer(n_ray, lambda k: to_ray(k).start())
    from_ray()

    slab_gram = slab_in[0, piece]
    for r in range(1, n_ray):
        slab_gram = slab_gram + slab_in[r, piece]

    def answer(p):
        wanted = index_tiles(p)
        found = [jnp.zeros((8, 128), F32) for s in range(CAP)]
        for b in range(blocks):
            block = slab_in[b // piece, b % piece]
            for s in range(CAP):
                found[s] = jnp.where(wanted[s] == float(b), block, found[s])
        return found

    to_cell, from_cell, end4 = over(
        "cell", cell, n_cell, lambda peer: back_out.at[peer], lambda me: back_in.at[me], send4, recv4
    )

    def send_answer(k):
        peer = lax.rem(cell + k, n_cell)
        found = answer(peer)
        for s in range(CAP):
            back_out[peer, s] = found[s]
        back_out[peer, CAP] = slab_gram
        to_cell(k).start()

    each_peer(n_cell, send_answer)

    found = answer(cell)
    for s in range(CAP):
        back_in[cell, s] = found[s]
    back_in[cell, CAP] = slab_gram
    for load in loads:
        load.wait()
    from_cell()

    whole_gram = back_in[0, CAP]
    for p in range(1, n_cell):
        whole_gram = whole_gram + back_in[p, CAP]
    for p in range(n_cell):
        for s in range(CAP):
            at = p * CAP + s
            w_slots[at // 2, :, (at % 2) * 128 : (at % 2 + 1) * 128] = back_in[p, s]
    across = (((1,), (1,)), ((), ()))

    def image_of(n):
        w_pair = split_rows(w_slots[n])
        both = lax.dot_general(w_pair, high[n], across, preferred_element_type=F32)
        rest = lax.dot_general(w_pair, low[n], across, preferred_element_type=F32)
        return both[:8] + (both[8:] + rest[:8])

    steps = high.shape[0]
    if steps <= UNROLL:
        image = image_of(0)
        for n in range(1, steps):
            image = image + image_of(n)
    else:
        image = lax.fori_loop(1, steps, lambda n, total: total + image_of(n), image_of(0))

    alpha, alpha_t, alpha_inverse = factor(whole_gram * (1.0 / cells_all))
    inverse_columns = columns_of(alpha_inverse)
    alpha_t_columns = columns_of(alpha_t)
    ray_blocks = u_ref.shape[1] // 128
    residual = []
    for i in range(ray_blocks):
        lanes = slice(i * 128, (i + 1) * 128)
        residual.append(apply(inverse_columns, image[:, lanes]) - apply(alpha_t_columns, u_ref[:, lanes]))
    everyone = n_ray * n_cell
    flat = ray * n_cell + cell
    own_gram = gram(residual)

    def gram_copy(k, back):
        peer = lax.rem(flat + k, everyone)
        slot = lax.rem(flat + everyone - k, everyone) if back else flat
        return pltpu.make_async_remote_copy(
            src_ref=all_gram.at[flat],
            dst_ref=all_gram.at[slot],
            send_sem=send7.at[k - 1],
            recv_sem=recv7.at[k - 1],
            device_id={"ray": lax.div(peer, n_cell), "cell": lax.rem(peer, n_cell)},
            device_id_type=MESH,
        )

    if everyone <= DIRECT:
        all_gram[flat] = own_gram
        for k in range(1, everyone):
            gram_copy(k, False).start()
    else:
        ray_gram[ray] = own_gram
        to_gram, from_gram, end5 = over(
            "ray", ray, n_ray, lambda peer: ray_gram.at[ray], lambda me: ray_gram.at[me], send5, recv5
        )
        each_peer(n_ray, lambda k: to_gram(k).start())

    small_ref[0] = alpha
    for i in range(ray_blocks):
        small_ref[2 + i] = residual[i]
    for b in range(blocks):
        v_ref[:, b * 128 : (b + 1) * 128] = apply(inverse_columns, slab_in[b // piece, b % piece])
    store = pltpu.make_async_copy(v_ref, v_hbm, load_sem.at[6])
    store.start()

    if everyone <= DIRECT:
        for k in range(1, everyone):
            gram_copy(k, True).wait_recv()
        total = all_gram[0]
        for d in range(1, everyone):
            total = total + all_gram[d]
    else:
        from_gram()
        total = ray_gram[0]
        for r in range(1, n_ray):
            total = total + ray_gram[r]
        cell_gram[cell] = total
        to_total, from_total, end6 = over(
            "cell", cell, n_cell, lambda peer: cell_gram.at[cell], lambda me: cell_gram.at[me], send6, recv6
        )
        each_peer(n_cell, lambda k: to_total(k).start())
        from_total()
        total = cell_gram[0]
        for p in range(1, n_cell):
            total = total + cell_gram[p]
    small_ref[1] = total * (1.0 / rays_all)
    store.wait()
    for end in (end1, end2, end3, end4):
        end()
    if everyone <= DIRECT:
        for k in range(1, everyone):
            gram_copy(k, False).wait_send()
    else:
        end5()
        end6()


def cholesky(tile, count=8):
    row = lax.broadcasted_iota(jnp.int32, (8, 128), 0)
    rest = [column_of(tile, k) for k in range(count)]
    lower, scales = [], []
    for j in range(count):
        scale = lax.rsqrt(row_of(rest[j], j))
        column = jnp.where(row >= j, rest[j] * scale, 0.0)
        lower.append(column)
        scales.append(scale)
        for k in range(j + 1, count):
            rest[k] = rest[k] - column * row_of(column, k)
    return lower, scales


def across_of(columns):
    lane = lax.broadcasted_iota(jnp.int32, (8, 128), 1)
    tile = jnp.zeros((8, 128), F32)
    for k, column in enumerate(columns):
        tile = jnp.where(lane == k, column, tile)
    return tile


def transposed(columns):
    row = lax.broadcasted_iota(jnp.int32, (8, 128), 0)
    turned = []
    for k in range(len(columns)):
        column = jnp.zeros((8, 128), F32)
        for i in range(k + 1):
            column = jnp.where(row == i, row_of(columns[i], k), column)
        turned.append(column)
    return turned


def solve(lower, scales, block):
    row = lax.broadcasted_iota(jnp.int32, (8, 128), 0)
    found = block
    for j, (column, scale) in enumerate(zip(lower, scales)):
        value = row_of(block, j) * scale
        found = jnp.where(row == j, value, found)
        block = block - column * value
    return found


def last_kernel(v_hbm, small_hbm, v_out, u_out, alpha_out, beta_out, v_ref, small, u_ref, alpha_ref, beta_ref, sems):
    load = pltpu.make_async_copy(small_hbm, small, sems.at[0])
    v_load = pltpu.make_async_copy(v_hbm, v_ref, sems.at[1])
    load.start()
    v_load.start()
    stores = [
        pltpu.make_async_copy(source, target, sems.at[2 + i])
        for i, (source, target) in enumerate(
            ((v_ref, v_out), (alpha_ref, alpha_out), (beta_ref, beta_out), (u_ref, u_out))
        )
    ]
    load.wait()
    alpha_ref[...] = small[0][:, :8]
    stores[1].start()
    v_load.wait()
    stores[0].start()
    lower, scales = cholesky(small[1])
    beta_ref[...] = across_of(lower)[:, :8]
    for i in range(small.shape[0] - 2):
        u_ref[:, i * 128 : (i + 1) * 128] = solve(lower, scales, small[2 + i])
    stores[2].start()
    stores[3].start()
    for store in stores:
        store.wait()


def flips_of(index, count):
    flips, bit = {}, 1
    while bit < count:
        flips[bit] = bit * (1 - 2 * lax.rem(lax.div(index, bit), 2))
        bit *= 2
    return flips


def flipped(index, flips, mask):
    for bit, step in flips.items():
        if mask & bit:
            index = index + step
    return index


def far_first(n_ray, n_cell):
    masks = [(2 * a, c) for a in range(n_ray // 2) for c in range(n_cell) if a or c]
    return sorted(masks, key=lambda m: -(8 * (m[1] >= 2) + 2 * bin(m[0]).count("1") + m[1]))


def halves_of(value):
    high = value.astype(BF16)
    return high, (value - high.astype(F32)).astype(BF16)


def fused_kernel(
    n_ray, n_cell, cells_all, rays_all,
    group_hbm, slot_hbm, block_hbm, tiles_hbm, u_hbm, v_prev_hbm, b_hbm,
    v_hbm, small_ref,
    group_ref, slot_ref, block_ref, asked_ref, index_out, index_in, tiles, u_ref, v_prev_ref, b_ref,
    u_left, u_right, gather, products, split, turned, pick, packet, recv, part, part_in, known, w_ref,
    back_out, back_in, gram_out, gram_in, w_slots, pair_gram, all_gram, v_ref,
    tile_sem, load_sem, send1, recv1, send2, recv2, send3, recv3, send4, recv4, send5, recv5, send6, recv6, send7, recv7,
):
    ray = lax.axis_index("ray")
    cell = lax.axis_index("cell")
    tile_count, tile_rays, width = tiles.shape
    slots = block_ref.shape[1]
    comps = u_ref.shape[0]
    sources = n_ray // 2 * n_cell
    blocks = w_ref.shape[0]
    steps, span = split.shape[0], split.shape[1]
    chunks = tile_sem.shape[0]
    per_chunk = tile_count // chunks
    per_step = steps // chunks
    quad = span // tile_rays

    small_loads = [
        pltpu.make_async_copy(source, target, load_sem.at[i])
        for i, (source, target) in enumerate(
            (
                (block_hbm, block_ref), (u_hbm, u_ref), (slot_hbm, slot_ref), (group_hbm, group_ref),
                (v_prev_hbm, v_prev_ref), (b_hbm, b_ref),
            )
        )
    ]

    def chunk(i):
        rows = pl.ds(i * per_chunk, per_chunk)
        return pltpu.make_async_copy(tiles_hbm.at[rows], tiles.at[rows], tile_sem.at[i])

    for load in small_loads[:4]:
        load.start()
    for i in range(chunks):
        chunk(i).start()
    for load in small_loads[4:]:
        load.start()

    ray_flips = flips_of(ray, n_ray)
    cell_flips = flips_of(cell, n_cell)
    masks = far_first(n_ray, n_cell)
    peers = [(flipped(ray, ray_flips, a), flipped(cell, cell_flips, c)) for a, c in masks]
    twin = ray + ray_flips[1]
    cell_masks = list(range(n_cell - 1, 0, -1))
    cell_peers = [flipped(cell, cell_flips, c) for c in cell_masks]

    def number_of(ray_at, cell_at):
        return lax.div(ray_at, 2) * n_cell + cell_at

    me = number_of(ray, cell)

    barrier = pltpu.get_barrier_semaphore()
    for r, c in peers + [(twin, cell)]:
        pl.semaphore_signal(barrier, inc=1, device_id={"ray": r, "cell": c}, device_id_type=MESH)

    def remote(source, target, send, recv_at, r, c):
        return pltpu.make_async_remote_copy(
            src_ref=source, dst_ref=target, send_sem=send, recv_sem=recv_at,
            device_id={"ray": r, "cell": c}, device_id_type=MESH,
        )

    small_loads[0].wait()
    lane = lax.broadcasted_iota(jnp.int32, (8, width), 1)
    bands = sources * CAP * comps // width
    band = lax.broadcasted_iota(jnp.int32, (bands, width), 0)
    place = band * width + lax.broadcasted_iota(jnp.int32, (bands, width), 1) - me * CAP * comps
    for p in range(n_cell):
        index = jnp.zeros((bands, width), jnp.int32)
        for s in range(CAP):
            b = block_ref[0, p * CAP + s]
            first_row = jnp.where(b < 0, -comps - 1, (b - s) * comps + 1)
            inside = (place >= s * comps) & (place < (s + 1) * comps)
            index = jnp.where(inside, jnp.maximum(place + first_row, 0), index)
        index_out[p] = index
    index_in[me] = index_out[cell]

    def announce():
        pl.semaphore_wait(barrier, len(peers) + 1)

    indices = [
        remote(index_out.at[c], index_in.at[me], send2.at[i], recv2.at[i], r, c) for i, (r, c) in enumerate(peers)
    ]

    for load in small_loads[1:4]:
        load.wait()
    low = lane < tile_rays
    low_pair = lax.broadcasted_iota(jnp.int32, (2 * comps, width), 1) < tile_rays
    for q in range(u_ref.shape[1] // width):
        block = u_ref[:, q * width : (q + 1) * width]
        turn = pltpu.roll(block, tile_rays, 1)
        for half, (left, right) in enumerate(((block, turn), (turn, block))):
            u_left[2 * q + half] = split_rows(jnp.where(low, left, 0.0))
            u_right[2 * q + half] = split_rows(jnp.where(low, 0.0, right))

    per_band = width // comps
    lane_tile = lax.div(lane, comps)
    slot_row = lax.broadcasted_iota(jnp.int32, (slots * comps, width), 0)
    offset = lax.rem(lane, comps)
    for q in range(tile_count // per_band):
        owner = jnp.zeros((8, width), jnp.int32)
        for t in range(per_band):
            owner = jnp.where(lane_tile == t, slot_ref[0, q * per_band + t], owner)
        owner = jnp.broadcast_to((owner * comps + offset)[:1], slot_row.shape)
        gather[:, q * width : (q + 1) * width] = jnp.where(slot_row == owner, 1.0, 0.0).astype(BF16)

    nothing = jnp.zeros((2 * quad // 2 * comps, width), BF16)
    for i in range(chunks):
        if i == ANNOUNCE:
            announce()
        chunk(i).wait()
        for n in range(i * per_step, (i + 1) * per_step):
            value = tiles[n * quad : (n + 1) * quad].reshape(span, width)
            high, rest = halves_of(value)
            both = jnp.concatenate([high, rest], axis=1)
            split[n] = both
            columns = []
            for h in range(2):
                at = n * quad + 2 * h
                own = jnp.concatenate([u_left[group_ref[0, at]], u_right[group_ref[0, at + 1]]], axis=0)
                columns.append(jnp.concatenate([own, nothing] if h == 0 else [nothing, own], axis=0))
            product = jnp.dot(jnp.concatenate(columns, axis=1), both, preferred_element_type=F32)
            product = (product[:, :width] + product[:, width:]).reshape(quad, 2 * comps, width)
            product = (product[:, :comps] + product[:, comps:]).reshape(quad * comps, width)
            high, rest = halves_of(product)
            products[n * quad * comps : (n + 1) * quad * comps] = jnp.concatenate([high, rest], axis=1)

    slot_sums = jnp.dot(gather[...], products[...], preferred_element_type=F32)
    packet[...] = (slot_sums[:, :width] + slot_sums[:, width:]).reshape(packet.shape)
    recv[me] = packet[cell]

    if ANNOUNCE >= chunks:
        announce()
    half = n_cell // 2
    passed = [(a, c) for a, c in masks if c >= half and a]
    sent = [i for i, mask in enumerate(masks) if mask not in passed]
    sent.sort(key=lambda i: (masks[i][1] < half, ORDER * bin(masks[i][0]).count("1") - masks[i][1]))
    first = [remote(packet.at[peers[i][1]], recv.at[me], send1.at[i], recv1.at[i], *peers[i]) for i in sent]
    for copy in first + indices:
        copy.start()

    def pass_on(mask, c):
        i = masks.index(mask)
        source = recv.at[number_of(ray, c)]
        return remote(source, source, send1.at[i], recv1.at[i], flipped(ray, ray_flips, mask[0]), cell)

    for load in small_loads[4:]:
        load.wait()
    b_columns = columns_of(b_ref[...])
    for b in range(blocks):
        known[b] = apply(b_columns, v_prev_ref[:, b * width : (b + 1) * width])

    @pl.loop(0, steps // 2)
    def _(n):
        turned[n] = split[n].T

    arrived = [i for i in sent if masks[i][0] == 0 and masks[i][1] >= half]
    for i in arrived[::-1]:
        r, c = peers[i]
        remote(packet.at[c], recv.at[number_of(r, c)], send1.at[i], recv1.at[i], r, c).wait_recv()
        for mask in passed:
            if mask[1] == masks[i][1]:
                copy = pass_on(mask, c)
                copy.start()
                first.append(copy)

    @pl.loop(steps // 2, steps)
    def _(n):
        turned[n] = split[n].T

    for i, (r, c) in enumerate(peers):
        remote(index_out.at[c], index_in.at[number_of(r, c)], send2.at[i], recv2.at[i], r, c).wait_recv()
    ask_load = pltpu.make_async_copy(index_in, asked_ref, load_sem.at[6])
    ask_load.start()
    asked = index_in[0]
    for d in range(1, sources):
        asked = asked + index_in[d]
    row = lax.broadcasted_iota(jnp.int32, (blocks * comps, width), 0) + 1
    for q in range(bands):
        wanted = jnp.broadcast_to(asked[q : q + 1], (blocks * comps, width))
        pick[:, q * width : (q + 1) * width] = jnp.where(row == wanted, 1.0, 0.0).astype(BF16)

    for i, (r, c) in enumerate(peers):
        if i not in arrived:
            remote(packet.at[c], recv.at[number_of(r, c)], send1.at[i], recv1.at[i], r, c).wait_recv()

    received = recv[...].reshape(sources * CAP * comps, width)
    high, rest = halves_of(received)
    both = jnp.concatenate([high, rest], axis=1)
    swaps = []
    section = blocks // SWAPS
    for i in range(SWAPS):
        rows = pl.ds(i * section, section)
        added = jnp.dot(pick[i * section * comps : (i + 1) * section * comps], both, preferred_element_type=F32)
        part[rows] = (added[:, :width] + added[:, width:]).reshape(section, comps, width)
        swaps.append(remote(part.at[rows], part_in.at[rows], send3.at[i], recv3.at[i], twin, cell))
        swaps[i].start()
    ask_load.wait()
    for copy in swaps:
        copy.wait_recv()
    def block_of(b):
        return part[b] + part_in[b] - known[b]

    answers = []
    for i, c in enumerate(cell_peers):
        for s in range(CAP):
            at = (number_of(ray, c) * CAP + s) * comps
            row_at = asked_ref[number_of(ray, c), lax.div(at, width), lax.rem(at, width)]
            back_out[i, s] = block_of(lax.div(jnp.maximum(row_at - 1, 0), comps))
        answers.append(remote(back_out.at[i], back_in.at[cell], send4.at[i], recv4.at[i], ray, c))
        answers[i].start()
    for s in range(CAP):
        back_in[cell, s] = block_of(jnp.maximum(block_ref[0, cell * CAP + s], 0))
    for b in range(blocks):
        w_ref[b] = block_of(b)

    slab_gram = gram([w_ref[b] for b in range(blocks)])
    gram_out[...] = slab_gram
    gram_in[cell] = slab_gram
    grams = [
        remote(gram_out, gram_in.at[cell], send5.at[i], recv5.at[i], ray, c) for i, c in enumerate(cell_peers)
    ]
    for copy in grams:
        copy.start()

    for i, c in enumerate(cell_peers):
        remote(back_out.at[i], back_in.at[c], send4.at[i], recv4.at[i], ray, c).wait_recv()
    for p in range(n_cell):
        for s in range(CAP):
            w_slots[p * CAP + s] = split_rows(back_in[p, s])

    groups = u_ref.shape[1] // tile_rays
    totals = [jnp.zeros((8, width), F32) for g in range(groups)]
    for n in range(steps):
        at = n * quad
        rows = jnp.concatenate([w_slots[slot_ref[0, at + j]] for j in range(quad)], axis=0)
        found = jnp.dot(jnp.concatenate([rows, rows], axis=1), turned[n], preferred_element_type=F32)
        for j in range(quad // 2):
            lanes = slice(j * width, (j + 1) * width)
            top = 2 * j * 2 * comps
            pair = jnp.where(
                low_pair, found[top : top + 2 * comps, lanes], found[top + 2 * comps : top + 4 * comps, lanes]
            )
            pair = pair[:comps] + pair[comps:]
            owner = jnp.where(low, group_ref[0, at + 2 * j], group_ref[0, at + 2 * j + 1])
            for g in range(groups):
                totals[g] = totals[g] + jnp.where(owner == g, pair, 0.0)

    for i, c in enumerate(cell_peers):
        remote(gram_out, gram_in.at[c], send5.at[i], recv5.at[i], ray, c).wait_recv()
    whole_gram = gram_in[0]
    for p in range(1, n_cell):
        whole_gram = whole_gram + gram_in[p]
    lower, scales = cholesky(whole_gram * (1.0 / cells_all))
    alpha_t_columns = transposed(lower)
    totals = [total + pltpu.roll(total, tile_rays, 1) for total in totals]
    ray_blocks = u_ref.shape[1] // width
    residual = []
    for i in range(ray_blocks):
        image = jnp.where(low, totals[2 * i], totals[2 * i + 1])
        lanes = slice(i * width, (i + 1) * width)
        residual.append(solve(lower, scales, image) - apply(alpha_t_columns, u_ref[:, lanes]))
    pair_gram[0] = gram(residual)
    pairs = remote(pair_gram.at[0], pair_gram.at[1], send6.at[0], recv6.at[0], twin, cell)
    pairs.start()
    small_ref[0] = across_of(lower)
    for i in range(ray_blocks):
        small_ref[2 + i] = residual[i]
    pairs.wait_recv()
    all_gram[me] = pair_gram[0] + pair_gram[1]
    last = [
        remote(all_gram.at[me], all_gram.at[me], send7.at[i], recv7.at[i], r, c) for i, (r, c) in enumerate(peers)
    ]
    for copy in last:
        copy.start()
    for b in range(blocks):
        v_ref[:, b * width : (b + 1) * width] = solve(lower, scales, w_ref[b])
    store = pltpu.make_async_copy(v_ref, v_hbm, load_sem.at[8])
    store.start()
    for copy in first + indices + swaps + answers + grams + [pairs] + last:
        copy.wait_send()
    store.wait()
    for i, (r, c) in enumerate(peers):
        remote(all_gram.at[me], all_gram.at[number_of(r, c)], send7.at[i], recv7.at[i], r, c).wait_recv()
    total = all_gram[0]
    for d in range(1, sources):
        total = total + all_gram[d]
    small_ref[1] = total * (1.0 / rays_all)


def fused(n_ray, n_cell, ray_tiles, tile_group, tile_slot, slot_block, u_basis, v_prev, b_prev):
    tile_count, tile_rays, width = ray_tiles.shape
    comps, rays = u_basis.shape
    slots = slot_block.shape[1]
    blocks = v_prev.shape[1] // width
    sources = n_ray // 2 * n_cell
    bands = sources * CAP * comps // width
    steps = tile_count * tile_rays // (2 * width)
    vmem = pl.BlockSpec(memory_space=pltpu.VMEM)
    anywhere = pl.BlockSpec(memory_space=pl.ANY)
    tile = (comps, width)
    one = pltpu.SemaphoreType.DMA((1,))
    parts = pltpu.SemaphoreType.DMA((SWAPS,))
    far = pltpu.SemaphoreType.DMA((sources - 1,))
    cells = pltpu.SemaphoreType.DMA((n_cell - 1,))
    return pl.pallas_call(
        functools.partial(fused_kernel, n_ray, n_cell, v_prev.shape[1] * n_cell, rays * n_ray * n_cell),
        out_shape=(
            jax.ShapeDtypeStruct(v_prev.shape, F32),
            jax.ShapeDtypeStruct((2 + rays // width,) + tile, F32),
        ),
        in_specs=[anywhere] * 7,
        out_specs=(anywhere, vmem),
        scratch_shapes=[
            pltpu.SMEM(tile_group.shape, jnp.int32),
            pltpu.SMEM(tile_slot.shape, jnp.int32),
            pltpu.SMEM(slot_block.shape, jnp.int32),
            pltpu.SMEM((sources, bands, width), jnp.int32),
            pltpu.VMEM((n_cell, bands, width), jnp.int32),
            pltpu.VMEM((sources, bands, width), jnp.int32),
            pltpu.VMEM(ray_tiles.shape, F32),
            pltpu.VMEM(u_basis.shape, F32),
            pltpu.VMEM(v_prev.shape, F32),
            pltpu.VMEM(b_prev.shape, F32),
            pltpu.VMEM((rays // tile_rays, 2 * comps, width), BF16),
            pltpu.VMEM((rays // tile_rays, 2 * comps, width), BF16),
            pltpu.VMEM((slots * comps, tile_count * comps), BF16),
            pltpu.VMEM((tile_count * comps, 2 * width), BF16),
            pltpu.VMEM((steps, 2 * width, 2 * width), BF16),
            pltpu.VMEM((steps, 2 * width, 2 * width), BF16),
            pltpu.VMEM((blocks * comps, sources * CAP * comps), BF16),
            pltpu.VMEM((n_cell, CAP * comps, width), F32),
            pltpu.VMEM((sources, CAP * comps, width), F32),
            pltpu.VMEM((blocks,) + tile, F32),
            pltpu.VMEM((blocks,) + tile, F32),
            pltpu.VMEM((blocks,) + tile, F32),
            pltpu.VMEM((blocks,) + tile, F32),
            pltpu.VMEM((n_cell - 1, CAP) + tile, F32),
            pltpu.VMEM((n_cell, CAP) + tile, F32),
            pltpu.VMEM(tile, F32),
            pltpu.VMEM((n_cell,) + tile, F32),
            pltpu.VMEM((slots, 2 * comps, width), BF16),
            pltpu.VMEM((2,) + tile, F32),
            pltpu.VMEM((sources,) + tile, F32),
            pltpu.VMEM(v_prev.shape, F32),
            pltpu.SemaphoreType.DMA((CHUNKS,)),
            pltpu.SemaphoreType.DMA((9,)),
            far, far, far, far, parts, parts, cells, cells, cells, cells, one, one, far, far,
        ],
        compiler_params=pltpu.CompilerParams(
            collective_id=0, has_side_effects=True, vmem_limit_bytes=56 << 20
        ),
    )(tile_group, tile_slot, slot_block, ray_tiles, u_basis, v_prev, b_prev)


def per_device(n_ray, n_cell, ray_tiles, tile_group, tile_slot, slot_block, u_basis, v_prev, b_prev):
    tile_count, tile_rays, width = ray_tiles.shape
    comps, rays = u_basis.shape
    slots = slot_block.shape[1]
    blocks = v_prev.shape[1] // width
    piece = blocks // n_ray
    vmem = pl.BlockSpec(memory_space=pltpu.VMEM)
    smem = pl.BlockSpec(memory_space=pltpu.SMEM)
    anywhere = pl.BlockSpec(memory_space=pl.ANY)
    tile = (comps, width)
    packets = (n_cell, CAP + 1) + tile
    limit = 56 << 20
    small_shape = (2 + rays // width,) + tile
    if n_ray * n_cell <= DIRECT:
        v_next, small = fused(n_ray, n_cell, ray_tiles, tile_group, tile_slot, slot_block, u_basis, v_prev, b_prev)
    else:
        packet, high, low = pl.pallas_call(
            local_kernel,
            out_shape=(
                jax.ShapeDtypeStruct(packets, F32),
                jax.ShapeDtypeStruct((slots // 2, rays, 2 * width), BF16),
                jax.ShapeDtypeStruct((slots // 2, rays, 2 * width), BF16),
            ),
            in_specs=[smem, smem, smem, anywhere, vmem],
            out_specs=(vmem, anywhere, anywhere),
            scratch_shapes=[
                pltpu.VMEM(ray_tiles.shape, F32),
                pltpu.VMEM((rays, slots * width), F32),
                pltpu.VMEM((slots // 2, rays, 2 * width), BF16),
                pltpu.VMEM((slots // 2, rays, 2 * width), BF16),
                pltpu.SemaphoreType.DMA((CHUNKS,)),
                pltpu.SemaphoreType.DMA((2, slots // 2)),
            ],
            compiler_params=pltpu.CompilerParams(vmem_limit_bytes=limit),
        )(tile_group, tile_slot, slot_block, ray_tiles, u_basis)

        ray_sem = pltpu.SemaphoreType.DMA((n_ray - 1,))
        direct = min(n_ray * n_cell, DIRECT)
        all_sem = pltpu.SemaphoreType.DMA((direct - 1,))
        cell_sem = pltpu.SemaphoreType.DMA((n_cell - 1,))
        v_next, small = pl.pallas_call(
            functools.partial(step_kernel, n_ray, n_cell, v_prev.shape[1] * n_cell, rays * n_ray * n_cell),
            out_shape=(jax.ShapeDtypeStruct(v_prev.shape, F32), jax.ShapeDtypeStruct(small_shape, F32)),
            in_specs=[anywhere] * 6,
            out_specs=(anywhere, vmem),
            scratch_shapes=[
                pltpu.VMEM(packets, F32),
                pltpu.VMEM(u_basis.shape, F32),
                pltpu.VMEM(v_prev.shape, F32),
                pltpu.VMEM(b_prev.shape, F32),
                pltpu.VMEM(v_prev.shape, F32),
                pltpu.VMEM(packets, F32),
                pltpu.VMEM((n_ray, piece) + tile, F32),
                pltpu.VMEM((n_ray, piece) + tile, F32),
                pltpu.VMEM((n_ray, piece + 1) + tile, F32),
                pltpu.VMEM(packets, F32),
                pltpu.VMEM(packets, F32),
                pltpu.VMEM((n_ray,) + tile, F32),
                pltpu.VMEM((n_cell,) + tile, F32),
                pltpu.VMEM((direct,) + tile, F32),
                pltpu.VMEM((slots // 2, rays, 2 * width), BF16),
                pltpu.VMEM((slots // 2, rays, 2 * width), BF16),
                pltpu.VMEM((slots // 2, comps, 2 * width), F32),
                pltpu.SemaphoreType.DMA((7,)),
                cell_sem, cell_sem, ray_sem, ray_sem, ray_sem, ray_sem,
                cell_sem, cell_sem, ray_sem, ray_sem, cell_sem, cell_sem, all_sem, all_sem,
            ],
            compiler_params=pltpu.CompilerParams(
                collective_id=0, has_side_effects=True, vmem_limit_bytes=limit
            ),
        )(packet, high, low, u_basis, v_prev, b_prev)
    return pl.pallas_call(
        last_kernel,
        out_shape=(
            jax.ShapeDtypeStruct(v_prev.shape, F32),
            jax.ShapeDtypeStruct(u_basis.shape, F32),
            jax.ShapeDtypeStruct((comps, comps), F32),
            jax.ShapeDtypeStruct((comps, comps), F32),
        ),
        in_specs=[anywhere, anywhere],
        out_specs=(anywhere, anywhere, anywhere, anywhere),
        scratch_shapes=[
            pltpu.VMEM(v_prev.shape, F32),
            pltpu.VMEM(small_shape, F32),
            pltpu.VMEM(u_basis.shape, F32),
            pltpu.VMEM((comps, comps), F32),
            pltpu.VMEM((comps, comps), F32),
            pltpu.SemaphoreType.DMA((6,)),
        ],
    )(v_next, small)


def solution(mesh):
    in_specs = (
        P(("ray", "cell"), None, None),
        P(("ray", "cell"), None),
        P(("ray", "cell"), None),
        P(("ray", "cell"), None),
        P(None, ("ray", "cell")),
        P(None, "cell"),
        P(),
    )
    out_specs = (P(None, "cell"), P(None, ("ray", "cell")), P(), P())
    return jax.shard_map(
        functools.partial(per_device, mesh.shape["ray"], mesh.shape["cell"]),
        mesh=mesh,
        in_specs=in_specs,
        out_specs=out_specs,
        check_vma=False,
    )
```
